32 devices in a mesh: dp: 8 (over z, x), mp: 4 (over y, core).
Axes of the slice: x: 2, y: 2, z: 4, core: 2. Of those that a mesh axis runs over, the one named last changes fastest.
Arguments:
- inputs: bfloat16 [4096, 768], P('dp'), may hold values from -6 to 6
- lengths: int32 [8], replicated, may hold values from 16 to 500, as said below
- teacher_inputs: bfloat16 [4096, 1600], P('dp'), may hold values from -6 to 6
- teacher_qkv: bfloat16 [1600, 3, 1600], P('dp'), may hold values from -0.15625 to 0.15625
- teacher_proj: bfloat16 [1600, 1600], P(None, 'dp'), may hold values from -3 to 3
- teacher_up: bfloat16 [1600, 6400], P('dp', 'mp'), may hold values from -0.15625 to 0.15625
- teacher_up_bias: float32 [6400], P('mp'), may hold values from -1.8 to 1.8
- teacher_down: bfloat16 [6400, 1600], P('mp', 'dp'), may hold values from -0.078125 to 0.078125
- teacher_vectors: float32 [10, 1600], replicated, may hold values from -1.8 to 1.875
- teacher_head: bfloat16 [1600, 25600], P('dp', 'mp'), may hold values from -0.3125 to 0.3125
- head: bfloat16 [768, 25600], P('dp', 'mp'), may hold values from -0.3125 to 0.3125
- column_weights: float32 [2, 768, 7, 768], P(None, 'dp', None, 'mp'), may hold values from -0.21875 to 0.21875
- column_first: float32 [2, 768, 7, 768], P(None, 'dp', None, 'mp'), may hold values from -3.5762787e-07 to 3.5762787e-07
- column_second: float32 [2, 768, 7, 768], P(None, 'dp', None, 'mp'), may hold values from 2.8257016e-16 to 1.1302807e-15
- column_average: float32 [2, 768, 7, 768], P(None, 'dp', None, 'mp'), may hold values from -0.21875 to 0.21875
- row_weights: float32 [2, 5, 768, 768], P(None, None, 'mp', 'dp'), may hold values from -3 to 3
- row_first: float32 [2, 5, 768, 768], P(None, None, 'mp', 'dp'), may hold values from -3.5762787e-07 to 3.5762787e-07
- row_second: float32 [2, 5, 768, 768], P(None, None, 'mp', 'dp'), may hold values from 2.8257016e-16 to 1.1302807e-15
- row_average: float32 [2, 5, 768, 768], P(None, None, 'mp', 'dp'), may hold values from -3 to 3
- column_biases: float32 [2, 6, 768], P(None, None, 'mp'), may hold values from -0.6 to 0.6
- bias_first: float32 [2, 6, 768], P(None, None, 'mp'), may hold values from -1.4305115e-06 to 1.4305115e-06
- bias_second: float32 [2, 6, 768], P(None, None, 'mp'), may hold values from 4.5211226e-15 to 1.808449e-14
- bias_average: float32 [2, 6, 768], P(None, None, 'mp'), may hold values from -0.6 to 0.6
- norm_vectors: float32 [2, 6, 768], replicated, may hold values from -0.6 to 1.875
- vector_first: float32 [2, 6, 768], replicated, may hold values from -1.4305115e-06 to 1.4305115e-06
- vector_second: float32 [2, 6, 768], replicated, may hold values from 4.5211226e-15 to 1.808449e-14
- vector_average: float32 [2, 6, 768], replicated, may hold values from -0.6 to 1.875
- final_norm: float32 [2, 768], replicated, may hold values from -0.6 to 1.875
- final_first: float32 [2, 768], replicated, may hold values from -1.4305115e-06 to 1.4305115e-06
- final_second: float32 [2, 768], replicated, may hold values from 4.5211226e-15 to 1.808449e-14
- final_average: float32 [2, 768], replicated, may hold values from -0.6 to 1.875
Outputs:
- loss: float32 [], replicated
- grad_norm: float32 [], replicated
- input_grad: float32 [4096, 768], P('dp')
- column_new: float32 [2, 768, 7, 768], P(None, 'dp', None, 'mp')
- column_first_new: float32 [2, 768, 7, 768], P(None, 'dp', None, 'mp')
- column_second_new: float32 [2, 768, 7, 768], P(None, 'dp', None, 'mp')
- column_average_new: float32 [2, 768, 7, 768], P(None, 'dp', None, 'mp')
- row_new: float32 [2, 5, 768, 768], P(None, None, 'mp', 'dp')
- row_first_new: float32 [2, 5, 768, 768], P(None, None, 'mp', 'dp')
- row_second_new: float32 [2, 5, 768, 768], P(None, None, 'mp', 'dp')
- row_average_new: float32 [2, 5, 768, 768], P(None, None, 'mp', 'dp')
- bias_new: float32 [2, 6, 768], P(None, None, 'mp')
- bias_first_new: float32 [2, 6, 768], P(None, None, 'mp')
- bias_second_new: float32 [2, 6, 768], P(None, None, 'mp')
- bias_average_new: float32 [2, 6, 768], P(None, None, 'mp')
- vector_new: float32 [2, 6, 768], replicated
- vector_first_new: float32 [2, 6, 768], replicated
- vector_second_new: float32 [2, 6, 768], replicated
- vector_average_new: float32 [2, 6, 768], replicated
- final_new: float32 [2, 768], replicated
- final_first_new: float32 [2, 768], replicated
- final_second_new: float32 [2, 768], replicated
- final_average_new: float32 [2, 768], replicated
The draws below stay inside these ranges and needn't reach their ends.
Inputs may be any that keep to these rules, and one draw needn't show every extreme that they name: `lengths`: one row has exactly 500 counted positions and one exactly 16.
All inputs are finite; a program needn't handle non-finite values.
Results may differ from the reference program's by a relative error of at most 0.025.
Values may be sent and summed in bfloat16 or wider, within the bound.
No kernel may reach another device: no remote copies, remote signals or barrier semaphores. Data moves between devices by JAX's collectives and lax.ppermute only.
A program may use at most 256 MiB of HBM per device.

```python
import math
import jax
import jax.numpy as jnp
from jax import lax

D = 768
HEADS = 12
HD = 64
FF = 3072
TD = 1600
THEADS = 25
THD = 64
TFF = 6400
VOCAB = 25600
SEQ = 512
LAYERS = 2
STEP = 4
SHORTEST = 16
LONGEST = 500
ROWS = 8
TOKENS = 4096
N_MP = 4


def gain_rows(key, count, width):
    ramp = jnp.exp(jnp.log(0.5) + jnp.log(3.0) * jnp.arange(width, dtype=jnp.float32) / (width - 1))
    factor = jax.random.uniform(key, (count, width), jnp.float32, 0.8, 1.25)
    return ramp[None, :] * factor


def shift_rows(key, count, width, spread, edge):
    return jnp.clip(spread * jax.random.normal(key, (count, width), jnp.float32), -edge, edge)


def vector_stack(key):
    gains = gain_rows(jax.random.fold_in(key, 11), LAYERS * 6, D).reshape(LAYERS, 6, D)
    shifts = shift_rows(jax.random.fold_in(key, 12), LAYERS * 6, D, 0.1, 0.6).reshape(LAYERS, 6, D)
    is_gain = (jnp.arange(6) % 3 == 0)[None, :, None]
    return jnp.where(is_gain, gains, shifts)


def final_stack(key):
    gains = gain_rows(jax.random.fold_in(key, 21), 1, D)
    shifts = shift_rows(jax.random.fold_in(key, 22), 1, D, 0.1, 0.6)
    return jnp.concatenate([gains, shifts], axis=0)


def row_stack(key):
    scales = jnp.where(jnp.arange(1 + FF // D) == 0, 0.5, FF ** (-0.5)).astype(jnp.float32)
    values = jnp.clip(jax.random.normal(key, (LAYERS, 1 + FF // D, D, D), jnp.float32), -6.0, 6.0)
    return values * scales[None, :, None, None]


def draw_lengths(key, part):
    values = jax.random.randint(jax.random.fold_in(key, 5), (ROWS,), SHORTEST, LONGEST + 1)
    order = jax.random.permutation(jax.random.fold_in(key, 6), ROWS)
    values = values.at[order[0]].set(LONGEST)
    values = values.at[order[1]].set(SHORTEST)
    return values.astype(jnp.int32)


def draw_teacher_vectors(key, part):
    gains = gain_rows(jax.random.fold_in(key, 61), 10, TD)
    shifts = shift_rows(jax.random.fold_in(key, 62), 10, TD, 0.3, 1.8)
    rows = jnp.arange(10)
    is_gain = ((rows == 0) | (rows == 5) | (rows == 8))[:, None]
    return jnp.where(is_gain, gains, shifts)


def draw_row_weights(key, part):
    return row_stack(jax.random.fold_in(key, 31))


def draw_row_average(key, part):
    return row_stack(jax.random.fold_in(key, 32))


def draw_norm_vectors(key, part):
    return vector_stack(jax.random.fold_in(key, 41))


def draw_vector_average(key, part):
    return vector_stack(jax.random.fold_in(key, 42))


def draw_final_norm(key, part):
    return final_stack(jax.random.fold_in(key, 51))


def draw_final_average(key, part):
    return final_stack(jax.random.fold_in(key, 52))


def block_levels(stream_key, shape, cuts, smallest, high):
    level, own = 1.0, jax.random.fold_in(stream_key, 6)
    for axis_at, parts in cuts:
        steps = jnp.exp(jax.random.uniform(jax.random.fold_in(own, axis_at), (parts,), jnp.float32, smallest / len(cuts), high / len(cuts)))
        level = level * jnp.repeat(steps, shape[axis_at] // parts).reshape([-1 if axis == axis_at else 1 for axis in range(len(shape))])
    return level


def centred(key, extent, scale, bound, cuts=(), kind=jnp.bfloat16):
    level = block_levels(key, extent, cuts, -0.22, 0.18) if cuts else 1.0
    drawn = jax.random.normal(key, extent, jnp.float32) * scale * level
    return jnp.minimum(jnp.maximum(drawn, -bound), bound).astype(kind)


def setup_inputs(seed: int = 0) -> dict:
    splits = jax.random.split(jax.random.key(seed), 32)
    return {
        "inputs": centred(splits[0], (TOKENS, D), 1.0, 6.0, ((0, 8),)),
        "lengths": draw_lengths(jax.random.fold_in(splits[31], 71), 0),
        "teacher_inputs": centred(splits[2], (TOKENS, TD), 1.0, 6.0, ((0, 8),)),
        "teacher_qkv": centred(splits[3], (TD, 3, TD), TD ** -0.5, 0.15625, ((0, 8),)),
        "teacher_proj": centred(splits[4], (TD, TD), 4 ** -0.5, 3.0, ((1, 8),)),
        "teacher_up": centred(splits[5], (TD, TFF), TD ** -0.5, 0.15625, ((0, 8), (1, 4))),
        "teacher_up_bias": centred(splits[6], (TFF,), 0.3, 1.8, ((0, 4),), jnp.float32),
        "teacher_down": centred(splits[7], (TFF, TD), TFF ** -0.5, 0.078125, ((0, 4), (1, 8))),
        "teacher_vectors": draw_teacher_vectors(jax.random.fold_in(splits[31], 71), 0),
        "teacher_head": centred(splits[9], (TD, VOCAB), (TD // 4) ** -0.5, 0.3125, ((0, 8), (1, 4))),
        "head": centred(splits[10], (D, VOCAB), (D // 2) ** -0.5, 0.3125, ((0, 8), (1, 4))),
        "column_weights": centred(splits[11], (LAYERS, D, 3 + FF // D, D), D ** -0.5, 0.21875, ((1, 8), (3, 4)), jnp.float32),
        "column_first": centred(splits[12], (LAYERS, D, 3 + FF // D, D), (0.11 * 0.002 * (LAYERS * 12 * D * D) ** -0.5), 3.5762786865234375e-07, ((1, 8), (3, 4)), jnp.float32),
        "column_second": jnp.clip(jnp.exp(math.log(1.13028065893702e-15) - 1.3862944 * jax.random.uniform(splits[13], (LAYERS, D, 3 + FF // D, D), jnp.float32) ** block_levels(splits[13], (LAYERS, D, 3 + FF // D, D), ((1, 8), (3, 4)), -0.2, 0.2)), 2.82570164734255e-16, 1.13028065893702e-15),
        "column_average": centred(splits[14], (LAYERS, D, 3 + FF // D, D), D ** -0.5, 0.21875, ((1, 8), (3, 4)), jnp.float32),
        "row_weights": draw_row_weights(jax.random.fold_in(splits[31], 71), 0),
        "row_first": centred(splits[16], (LAYERS, 1 + FF // D, D, D), (0.11 * 0.002 * (LAYERS * 12 * D * D) ** -0.5), 3.5762786865234375e-07, ((2, 4), (3, 8)), jnp.float32),
        "row_second": jnp.clip(jnp.exp(math.log(1.13028065893702e-15) - 1.3862944 * jax.random.uniform(splits[17], (LAYERS, 1 + FF // D, D, D), jnp.float32) ** block_levels(splits[17], (LAYERS, 1 + FF // D, D, D), ((2, 4), (3, 8)), -0.2, 0.2)), 2.82570164734255e-16, 1.13028065893702e-15),
        "row_average": draw_row_average(jax.random.fold_in(splits[31], 71), 0),
        "column_biases": centred(splits[19], (LAYERS, 2 + FF // D, D), 0.1, 0.6, ((2, 4),), jnp.float32),
        "bias_first": centred(splits[20], (LAYERS, 2 + FF // D, D), (0.44 * 0.002 * (LAYERS * 12 * D * D) ** -0.5), 1.430511474609375e-06, ((2, 4),), jnp.float32),
        "bias_second": jnp.clip(jnp.exp(math.log(1.808449054299232e-14) - 1.3862944 * jax.random.uniform(splits[21], (LAYERS, 2 + FF // D, D), jnp.float32) ** block_levels(splits[21], (LAYERS, 2 + FF // D, D), ((2, 4),), -0.2, 0.2)), 4.52112263574808e-15, 1.808449054299232e-14),
        "bias_average": centred(splits[22], (LAYERS, 2 + FF // D, D), 0.1, 0.6, ((2, 4),), jnp.float32),
        "norm_vectors": draw_norm_vectors(jax.random.fold_in(splits[31], 71), 0),
        "vector_first": centred(splits[24], (LAYERS, 6, D), (0.44 * 0.002 * (LAYERS * 12 * D * D) ** -0.5), 1.430511474609375e-06, (), jnp.float32),
        "vector_second": jnp.clip(jnp.exp(jax.random.uniform(splits[25], (LAYERS, 6, D), jnp.float32, math.log(4.52112263574808e-15), math.log(1.808449054299232e-14))), 4.52112263574808e-15, 1.808449054299232e-14),
        "vector_average": draw_vector_average(jax.random.fold_in(splits[31], 71), 0),
        "final_norm": draw_final_norm(jax.random.fold_in(splits[31], 71), 0),
        "final_first": centred(splits[28], (2, D), (0.44 * 0.002 * (LAYERS * 12 * D * D) ** -0.5), 1.430511474609375e-06, (), jnp.float32),
        "final_second": jnp.clip(jnp.exp(jax.random.uniform(splits[29], (2, D), jnp.float32, math.log(4.52112263574808e-15), math.log(1.808449054299232e-14))), 4.52112263574808e-15, 1.808449054299232e-14),
        "final_average": draw_final_average(jax.random.fold_in(splits[31], 71), 0),
    }


EPSILON = 1e-05
GELU_COEFF = 0.7978845608028654
BETA_ONE = 0.9
BETA_TWO = 0.999
ADAM_EPSILON = 1e-08
CLIP_LIMIT = 0.002
PRECISE = lax.Precision.HIGHEST

@jax.custom_vjp
def low(v):
    return lax.optimization_barrier(v.astype(jnp.bfloat16)).astype(jnp.float32)

@jax.custom_vjp
def low_back(v):
    return v

def low_keep(v):
    return (low(v), None)

def low_pass(kept, grad):
    return (grad,)

def back_keep(v):
    return (v, None)

def back_low(kept, grad):
    return (low(grad),)
low.defvjp(low_keep, low_pass)
low_back.defvjp(back_keep, back_low)

def norm_rows(values, gain, shift):
    centered = values - lax.optimization_barrier(jnp.mean(values, axis=-1, keepdims=True))
    variance = lax.optimization_barrier(jnp.mean(centered * centered, axis=-1, keepdims=True))
    return centered * lax.rsqrt(variance + EPSILON) * gain + shift

def gelu_tanh(values):
    return 0.5 * values * (1.0 + jnp.tanh(GELU_COEFF * (values + 0.044715 * values * values * values)))

def lse_rows(values):
    highest = lax.optimization_barrier(jnp.max(values, axis=-1, keepdims=True))
    return highest + jnp.log(lax.optimization_barrier(jnp.sum(jnp.exp(values - highest), axis=-1, keepdims=True)))

def attention(queries, key_rows, value_rows, head_size):
    raw = low_back(jnp.einsum('qhd,khd->hqk', queries, key_rows, precision=PRECISE))
    scores = raw * head_size ** (-0.5)
    positions = jnp.arange(SEQ, dtype=jnp.int32)
    allowed = positions[None, :] <= positions[:, None]
    scores = jnp.where(allowed[None], scores, -jnp.inf)
    weights = low(jnp.exp(scores - lse_rows(scores)))
    return jnp.einsum('hqk,khd->qhd', weights, value_rows, precision=PRECISE)

def teacher_forward(stream, qkv_w, proj_w, up_w, up_bias, down_w, vectors, head_w):
    normed = low(norm_rows(stream, vectors[0], vectors[1]))
    projected = jnp.einsum('sd,dkc->skc', normed, qkv_w, precision=PRECISE)
    layout = (SEQ, THEADS, THD)
    queries = low(projected[:, 0] + vectors[2]).reshape(layout)
    key_rows = low(projected[:, 1]).reshape(layout)
    value_rows = low(projected[:, 2] + vectors[3]).reshape(layout)
    attended = low(attention(queries, key_rows, value_rows, THD).reshape(SEQ, TD))
    base = THEADS // N_MP
    extra = THEADS % N_MP
    branch = jnp.zeros((SEQ, TD), jnp.float32)
    for group in range(N_MP):
        begin = (group * base + min(group, extra)) * THD
        finish = ((group + 1) * base + min(group + 1, extra)) * THD
        branch = branch + low(jnp.dot(attended[:, begin:finish], proj_w[begin:finish], precision=PRECISE))
    middle = stream + branch + vectors[4]
    normed = low(norm_rows(middle, vectors[5], vectors[6]))
    part = TFF // N_MP
    branch = jnp.zeros((SEQ, TD), jnp.float32)
    for group in range(N_MP):
        cols = slice(group * part, (group + 1) * part)
        hidden = low(gelu_tanh(jnp.dot(normed, up_w[:, cols], precision=PRECISE) + up_bias[cols]))
        branch = branch + low(jnp.dot(hidden, down_w[cols], precision=PRECISE))
    result = middle + branch + vectors[7]
    final = low(norm_rows(result, vectors[8], vectors[9]))
    return jnp.dot(final, head_w, precision=PRECISE)

def block(stream, cols, rows, biases, vector):
    part = D // N_MP
    up_blocks = FF // D
    cols = cols.reshape(D, 3 + up_blocks, N_MP, part)
    rows = rows.reshape(1 + up_blocks, N_MP, part, D)
    biases = biases.reshape(2 + up_blocks, N_MP, part)
    normed = low(norm_rows(stream, vector[0], vector[1]))
    query_parts, key_parts, value_parts = ([], [], [])
    for group in range(N_MP):
        projected = jnp.einsum('sd,dkc->skc', low_back(normed), cols[:, 0:3, group], precision=PRECISE)
        query_parts.append(low(low_back(projected[:, 0] + biases[0, group])))
        key_parts.append(low(low_back(projected[:, 1])))
        value_parts.append(low(low_back(projected[:, 2] + biases[1, group])))
    layout = (SEQ, HEADS, HD)
    attended = attention(jnp.concatenate(query_parts, 1).reshape(layout), jnp.concatenate(key_parts, 1).reshape(layout), jnp.concatenate(value_parts, 1).reshape(layout), HD)
    attended = low(low_back(attended.reshape(SEQ, D)))
    branch = jnp.zeros((SEQ, D), jnp.float32)
    for group in range(N_MP):
        piece = attended[:, group * part:(group + 1) * part]
        branch = branch + low(low_back(jnp.dot(piece, rows[0, group], precision=PRECISE)))
    middle = stream + branch + vector[2]
    normed = low(norm_rows(middle, vector[3], vector[4]))
    branch = jnp.zeros((SEQ, D), jnp.float32)
    for group in range(N_MP):
        pre_act = jnp.einsum('sd,dkc->skc', low_back(normed), cols[:, 3:, group], precision=PRECISE) + biases[2:, group]
        hidden = low(gelu_tanh(low_back(pre_act)))
        branch = branch + low(low_back(jnp.einsum('skc,kcd->sd', hidden, rows[1:, group], precision=PRECISE)))
    return middle + branch + vector[5]

def row_loss(stream, teacher_stream, length, cols, rows, biases, vectors, final, head_wide, teacher_set):
    teacher = teacher_forward(teacher_stream, *teacher_set)
    for layer in range(LAYERS):
        stream = block(stream, cols[layer], rows[layer], biases[layer], vectors[layer])
    normed = low(norm_rows(stream, final[0], final[1]))
    part = VOCAB // N_MP
    pieces = []
    for group in range(N_MP):
        pieces.append(low_back(jnp.dot(low_back(normed), head_wide[:, group * part:(group + 1) * part], precision=PRECISE)))
    logits = jnp.concatenate(pieces, axis=1)
    student_log = logits - lse_rows(logits)
    teacher_log = teacher - lse_rows(teacher)
    divergence = lax.optimization_barrier(jnp.sum(jnp.exp(teacher_log) * (teacher_log - student_log), axis=-1))
    counted = jnp.arange(SEQ, dtype=jnp.int32) < length
    return jnp.sum(jnp.where(counted, divergence, 0.0))

def adam_update(weight, first, second, average, grad, clip, rate, decay):
    keep = min(0.995, (1.0 + STEP) / (10.0 + STEP))
    grad = grad * clip
    first_new = BETA_ONE * first + (1.0 - BETA_ONE) * grad
    second_new = BETA_TWO * second + (1.0 - BETA_TWO) * grad * grad
    first_hat = first_new / (1.0 - BETA_ONE ** STEP)
    second_hat = second_new / (1.0 - BETA_TWO ** STEP)
    weight_new = weight - rate * (first_hat / (jnp.sqrt(second_hat) + ADAM_EPSILON) + decay * weight)
    average_new = keep * average + (1.0 - keep) * weight_new
    return (weight_new, first_new, second_new, average_new)

def reference(inputs, lengths, teacher_inputs, teacher_qkv, teacher_proj, teacher_up, teacher_up_bias, teacher_down, teacher_vectors, teacher_head, head, column_weights, column_first, column_second, column_average, row_weights, row_first, row_second, row_average, column_biases, bias_first, bias_second, bias_average, norm_vectors, vector_first, vector_second, vector_average, final_norm, final_first, final_second, final_average):
    head_wide = head.astype(jnp.float32)
    teacher_set = (teacher_qkv.astype(jnp.float32), teacher_proj.astype(jnp.float32), teacher_up.astype(jnp.float32), teacher_up_bias, teacher_down.astype(jnp.float32), teacher_vectors, teacher_head.astype(jnp.float32))
    teacher_rows = teacher_inputs.astype(jnp.float32).reshape(ROWS, SEQ, TD)
    counted_total = jnp.sum(lengths).astype(jnp.float32)
    row_fn = jax.checkpoint(row_loss)

    def total_loss(stream, cols, rows, biases, vectors, final):
        cols_low = low(cols)
        rows_low = low(rows)

        def one_row(carry, pieces):
            row_stream, row_teacher, row_length = pieces
            value = row_fn(row_stream, row_teacher, row_length, cols_low, rows_low, biases, vectors, final, head_wide, teacher_set)
            return (carry + value, None)
        total, _ = lax.scan(one_row, jnp.zeros((), jnp.float32), (stream.reshape(ROWS, SEQ, D), teacher_rows, lengths))
        return total / counted_total
    loss, pullback = jax.vjp(total_loss, inputs.astype(jnp.float32), column_weights, row_weights, column_biases, norm_vectors, final_norm)
    input_grad, grad_cols, grad_rows, grad_bias, grad_vectors, grad_final = pullback(jnp.ones((), jnp.float32))
    squares = jnp.sum(grad_cols * grad_cols) + jnp.sum(grad_rows * grad_rows) + jnp.sum(grad_bias * grad_bias) + jnp.sum(grad_vectors * grad_vectors) + jnp.sum(grad_final * grad_final)
    grad_norm = jnp.sqrt(squares)
    clip = CLIP_LIMIT / jnp.maximum(grad_norm, CLIP_LIMIT)
    column_out = adam_update(column_weights, column_first, column_second, column_average, grad_cols, clip, 0.1, 0.1)
    row_out = adam_update(row_weights, row_first, row_second, row_average, grad_rows, clip, 0.2, 0.1)
    bias_out = adam_update(column_biases, bias_first, bias_second, bias_average, grad_bias, clip, 0.1, 0.0)
    vector_out = adam_update(norm_vectors, vector_first, vector_second, vector_average, grad_vectors, clip, 0.5, 0.0)
    final_out = adam_update(final_norm, final_first, final_second, final_average, grad_final, clip, 0.5, 0.0)
    return (loss, grad_norm, input_grad, column_out[0], column_out[1], column_out[2], column_out[3], row_out[0], row_out[1], row_out[2], row_out[3], bias_out[0], bias_out[1], bias_out[2], bias_out[3], vector_out[0], vector_out[1], vector_out[2], vector_out[3], final_out[0], final_out[1], final_out[2], final_out[3])
```

```python
import jax
import jax.numpy as jnp
from jax import lax
from jax.sharding import PartitionSpec as P

HD = 64
THEADS = 25
THD = 64
SEQ = 512
STEP = 4
MAJOR = 4

EPSILON = 1e-05
GELU_COEFF = 0.7978845608028654
BETA_ONE = 0.9
BETA_TWO = 0.999
ADAM_EPSILON = 1e-08
CLIP_LIMIT = 0.002

BF = jnp.bfloat16
F32 = jnp.float32


def dot(a, b):
    return jnp.dot(a, b, preferred_element_type=F32)


def dot_nt(a, b):
    return lax.dot_general(a, b, (((1,), (1,)), ((), ())), preferred_element_type=F32)


def dot_tn(a, b):
    return lax.dot_general(a, b, (((0,), (0,)), ((), ())), preferred_element_type=F32)


def layer_norm(values, gain, shift):
    centered = values - jnp.mean(values, axis=-1, keepdims=True)
    variance = jnp.mean(centered * centered, axis=-1, keepdims=True)
    return centered * lax.rsqrt(variance + EPSILON) * gain + shift


def layer_norm_back(values, gain, grad):
    centered = values - jnp.mean(values, axis=-1, keepdims=True)
    variance = jnp.mean(centered * centered, axis=-1, keepdims=True)
    scale = lax.rsqrt(variance + EPSILON)
    unit = centered * scale
    inner = grad * gain
    back = scale * (
        inner
        - jnp.mean(inner, axis=-1, keepdims=True)
        - unit * jnp.mean(inner * unit, axis=-1, keepdims=True)
    )
    return back, jnp.sum(grad * unit, axis=0), jnp.sum(grad, axis=0)


def gelu_tanh(values):
    return (
        0.5 * values * (1.0 + jnp.tanh(GELU_COEFF * (values + 0.044715 * values * values * values)))
    )


def heads_of(rows, size):
    return rows.reshape(rows.shape[0], rows.shape[1] // size, size)


def block_scores(queries, key_rows):
    scale = queries.shape[-1] ** (-0.5)
    scores = jnp.einsum("qhd,khd->hqk", queries, key_rows, preferred_element_type=F32) * scale
    query_pos = jnp.arange(queries.shape[0], dtype=jnp.int32)
    key_pos = jnp.arange(key_rows.shape[0], dtype=jnp.int32)
    return jnp.where((key_pos[None, :] <= query_pos[:, None])[None], scores, -jnp.inf)


def attend(queries, key_rows, value_rows, size):
    scores = block_scores(heads_of(queries, size), heads_of(key_rows, size))
    highest = jnp.max(scores, axis=-1, keepdims=True)
    totals = highest + jnp.log(jnp.sum(jnp.exp(scores - highest), axis=-1, keepdims=True))
    weights = jnp.exp(scores - totals).astype(BF)
    result = jnp.einsum(
        "hqk,khd->qhd", weights, heads_of(value_rows, size), preferred_element_type=F32
    )
    return result.reshape(queries.shape), totals


def attend_back(queries, key_rows, value_rows, grad_out, totals, size):
    shape = queries.shape
    scale = size ** (-0.5)
    queries, key_rows, value_rows, grad_out = (
        heads_of(part, size) for part in (queries, key_rows, value_rows, grad_out)
    )
    probs = jnp.exp(block_scores(queries, key_rows) - totals)
    weights = probs.astype(BF)
    grad_probs = jnp.einsum("qhd,khd->hqk", grad_out, value_rows, preferred_element_type=F32)
    inner = jnp.sum(probs * grad_probs, axis=-1, keepdims=True)
    grad_scores = (probs * (grad_probs - inner) * scale).astype(BF)
    grad_query = jnp.einsum("hqk,khd->qhd", grad_scores, key_rows, preferred_element_type=F32)
    grad_key = jnp.einsum("hqk,qhd->khd", grad_scores, queries, preferred_element_type=F32)
    grad_value = jnp.einsum("hqk,qhd->khd", weights, grad_out, preferred_element_type=F32)
    return tuple(part.astype(BF).reshape(shape) for part in (grad_query, grad_key, grad_value))


def adam_update(weight, first, second, average, grad, clip, rate, decay):
    keep = min(0.995, (1.0 + STEP) / (10.0 + STEP))
    grad = grad * clip
    first_new = BETA_ONE * first + (1.0 - BETA_ONE) * grad
    second_new = BETA_TWO * second + (1.0 - BETA_TWO) * grad * grad
    first_hat = first_new / (1.0 - BETA_ONE**STEP)
    second_hat = second_new / (1.0 - BETA_TWO**STEP)
    weight_new = weight - rate * (
        first_hat / (jnp.sqrt(second_hat) + ADAM_EPSILON) + decay * weight
    )
    average_new = keep * average + (1.0 - keep) * weight_new
    return (weight_new, first_new, second_new, average_new)


class Wires:
    def __init__(self):
        self.dp = lax.axis_size("dp")
        self.mp = lax.axis_size("mp")
        self.minors = self.dp // MAJOR
        self.dp_at = lax.axis_index("dp")
        self.mp_at = lax.axis_index("mp")
        self.major = self.dp_at // self.minors
        self.minor = self.dp_at % self.minors
        self.near_at = self.mp_at % 2
        self.near_pairs = [(i, i ^ 1) for i in range(self.mp)]
        self.far_pairs = [(i, i ^ 2) for i in range(self.mp)]
        self.over_major = [
            [k * self.minors + j for k in range(MAJOR)] for j in range(self.minors)
        ]
        self.over_minor = [
            [k * self.minors + j for j in range(self.minors)] for k in range(MAJOR)
        ]

    def near(self, part):
        return lax.ppermute(part, "mp", self.near_pairs)

    def far(self, part):
        return lax.ppermute(part, "mp", self.far_pairs)

    def natural(self, own, other):
        first = self.near_at == 0
        return jnp.concatenate([jnp.where(first, own, other), jnp.where(first, other, own)], axis=0)

    def own_first(self, whole):
        half = whole.shape[0] // 2
        own = lax.dynamic_slice_in_dim(whole, self.near_at * half, half, 0)
        other = lax.dynamic_slice_in_dim(whole, (1 - self.near_at) * half, half, 0)
        return own, other

    def summed(self, other, own):
        pair = (own + self.near(other.astype(BF)).astype(F32)).astype(BF)
        return pair.astype(F32) + self.far(pair).astype(F32)

    def minor_stack(self, part, axis):
        if self.minors == 2:
            swap = [(i, i ^ 1) for i in range(self.dp)]
            other = lax.ppermute(part, "dp", swap)
            first = self.minor == 0
            return jnp.stack(
                [jnp.where(first, part, other), jnp.where(first, other, part)], axis=axis
            )
        return lax.all_gather(part, "dp", axis=axis, axis_index_groups=self.over_minor)

    def major_gather(self, part):
        return lax.all_gather(
            part, "dp", axis=0, tiled=True, axis_index_groups=self.over_major
        )

    def rows_major_first(self, part):
        rows, cols = part.shape
        held = self.major_gather(part).reshape(MAJOR, rows, cols)
        return self.minor_stack(held, 1).reshape(self.dp * rows, cols)

    def rows_minor_first(self, part):
        rows, cols = part.shape
        return self.major_gather(self.minor_stack(part, 0).reshape(self.minors * rows, cols))

    def major_swap(self, part):
        return lax.all_to_all(part, "dp", 0, 0, axis_index_groups=self.over_major)

    def scattered(self, grad):
        rows, cols = grad.shape[0] // self.dp, grad.shape[1]
        split = grad.reshape(MAJOR, self.minors, rows, cols)
        if self.minors == 2:
            swap = [(i, i ^ 1) for i in range(self.dp)]
            mine = lax.dynamic_index_in_dim(split, self.minor, 1, keepdims=False)
            theirs = lax.dynamic_index_in_dim(split, 1 - self.minor, 1, keepdims=False)
            held = (mine + lax.ppermute(theirs.astype(BF), "dp", swap).astype(F32)).astype(BF)
        else:
            held = lax.psum_scatter(
                split.astype(BF), "dp", scatter_dimension=1, axis_index_groups=self.over_minor
            )
        return lax.psum_scatter(
            held.reshape(MAJOR * rows, cols),
            "dp",
            scatter_dimension=0,
            tiled=True,
            axis_index_groups=self.over_major,
        ).astype(F32)


def local(
    inputs,
    lengths,
    teacher_inputs,
    teacher_qkv,
    teacher_proj,
    teacher_up,
    teacher_up_bias,
    teacher_down,
    teacher_vectors,
    teacher_head,
    head,
    column_weights,
    column_first,
    column_second,
    column_average,
    row_weights,
    row_first,
    row_second,
    row_average,
    column_biases,
    bias_first,
    bias_second,
    bias_average,
    norm_vectors,
    vector_first,
    vector_second,
    vector_average,
    final_norm,
    final_first,
    final_second,
    final_average,
):
    wires = Wires()
    token_count, width = inputs.shape
    half = token_count // 2
    teacher_width = teacher_inputs.shape[1]
    layers, shard_rows, col_blocks, part = column_weights.shape
    up_blocks = col_blocks - 3
    units = up_blocks * part

    slots = -(-THEADS // wires.mp)
    base_heads = THEADS // wires.mp
    extra_heads = THEADS % wires.mp
    own_start = wires.mp_at * base_heads + jnp.minimum(wires.mp_at, extra_heads)
    own_stop = own_start + base_heads + jnp.where(wires.mp_at < extra_heads, 1, 0)
    slot_start = jnp.minimum(own_start, THEADS - slots)
    head_ids = slot_start + jnp.arange(slots, dtype=jnp.int32)
    owned = ((head_ids >= own_start) & (head_ids < own_stop)).astype(F32)
    slot_width = slots * THD
    first_col = slot_start * THD

    qkv_shard = lax.dynamic_slice_in_dim(teacher_qkv, first_col, slot_width, 2)
    proj_shard = lax.dynamic_slice_in_dim(teacher_proj, first_col, slot_width, 0).T
    teacher_attn = wires.rows_major_first(
        jnp.concatenate([qkv_shard.reshape(-1, 3 * slot_width), proj_shard], axis=1)
    )
    teacher_qkv_full = teacher_attn[:, : 3 * slot_width]
    teacher_proj_full = teacher_attn[:, 3 * slot_width :]
    teacher_up_full = wires.rows_major_first(teacher_up)
    teacher_down_full = wires.rows_major_first(teacher_down.T)
    layer_full = []
    for layer in range(layers):
        cols = column_weights[layer].astype(BF)
        rows = row_weights[layer].astype(BF)
        layer_full.append(
            wires.rows_minor_first(
                jnp.concatenate(
                    [
                        cols[:, 3:].reshape(shard_rows, units),
                        rows[1:].reshape(units, shard_rows).T,
                        cols[:, :3].reshape(shard_rows, 3 * part),
                        rows[0].T,
                    ],
                    axis=1,
                )
            )
        )
    vocab_part = head.shape[1] // MAJOR
    head_rows = teacher_head.shape[0] + head.shape[0]
    both = jnp.concatenate([teacher_head, head], axis=0)
    both = jnp.swapaxes(both.reshape(head_rows, MAJOR, vocab_part), 0, 1)
    both = wires.minor_stack(wires.major_swap(both), 1)
    teacher_head_part = both[:, :, : teacher_head.shape[0]].reshape(teacher_width, vocab_part)
    head_part = both[:, :, teacher_head.shape[0] :].reshape(width, vocab_part)

    own_at = wires.near_at * half
    tv = teacher_vectors
    teacher_stream = lax.dynamic_slice_in_dim(teacher_inputs, own_at, half, 0).astype(F32)
    teacher_normed = layer_norm(teacher_inputs.astype(F32), tv[0], tv[1]).astype(BF)
    projected = dot(teacher_normed, teacher_qkv_full)
    teacher_query = (
        projected[:, :slot_width] + lax.dynamic_slice_in_dim(tv[2], first_col, slot_width)
    ).astype(BF)
    teacher_key = projected[:, slot_width : 2 * slot_width].astype(BF)
    teacher_value = (
        projected[:, 2 * slot_width :] + lax.dynamic_slice_in_dim(tv[3], first_col, slot_width)
    ).astype(BF)
    teacher_att, _ = attend(teacher_query, teacher_key, teacher_value, THD)
    teacher_att = (teacher_att * jnp.repeat(owned, THD)[None, :]).astype(BF)
    att_own, att_other = wires.own_first(teacher_att)
    teacher_mid = (
        teacher_stream
        + wires.summed(dot_nt(att_other, teacher_proj_full), dot_nt(att_own, teacher_proj_full))
        + tv[4]
    )
    normed_own = layer_norm(teacher_mid, tv[5], tv[6]).astype(BF)
    normed = jnp.concatenate([normed_own, wires.near(normed_own)], axis=0)
    hidden = gelu_tanh(dot(normed, teacher_up_full) + teacher_up_bias).astype(BF)
    teacher_top = (
        teacher_mid
        + wires.summed(
            dot_nt(hidden[half:], teacher_down_full), dot_nt(hidden[:half], teacher_down_full)
        )
        + tv[7]
    )
    teacher_final = layer_norm(teacher_top, tv[8], tv[9]).astype(BF)

    def all_rows(own):
        mine = wires.major_gather(own)
        return jnp.concatenate([mine, wires.near(mine)], axis=0)

    teacher_logits = dot(all_rows(teacher_final), teacher_head_part)

    stream = lax.dynamic_slice_in_dim(inputs, own_at, half, 0).astype(F32)
    saved = []
    for layer in range(layers):
        vector = norm_vectors[layer]
        full = layer_full[layer]
        up_cols = full[:, :units]
        down_rows = full[:, units : 2 * units]
        attn_cols = full[:, 2 * units : 2 * units + 3 * part]
        proj_rows = full[:, 2 * units + 3 * part :]
        one_own = layer_norm(stream, vector[0], vector[1]).astype(BF)
        one_other = wires.near(one_own)
        projected = wires.natural(dot(one_own, attn_cols), dot(one_other, attn_cols))
        queries = (projected[:, :part] + column_biases[layer, 0]).astype(BF)
        key_rows = projected[:, part : 2 * part].astype(BF)
        value_rows = (projected[:, 2 * part :] + column_biases[layer, 1]).astype(BF)
        attended, totals = attend(queries, key_rows, value_rows, HD)
        attended = attended.astype(BF)
        att_own, att_other = wires.own_first(attended)
        middle = (
            stream
            + wires.summed(dot_nt(att_other, proj_rows), dot_nt(att_own, proj_rows))
            + vector[2]
        )
        two_own = layer_norm(middle, vector[3], vector[4]).astype(BF)
        two = jnp.concatenate([two_own, wires.near(two_own)], axis=0)
        pre_act = dot(two, up_cols) + column_biases[layer, 2:].reshape(units)
        hidden = gelu_tanh(pre_act).astype(BF)
        saved.append(
            (
                stream,
                wires.natural(one_own, one_other),
                queries,
                key_rows,
                value_rows,
                totals,
                attended,
                middle,
                two,
                pre_act,
                hidden,
            )
        )
        stream = (
            middle
            + wires.summed(dot_nt(hidden[half:], down_rows), dot_nt(hidden[:half], down_rows))
            + vector[5]
        )

    final_out = layer_norm(stream, final_norm[0], final_norm[1]).astype(BF)
    logits = dot(all_rows(final_out), head_part)
    teacher_peak = jnp.max(teacher_logits, axis=-1)
    student_peak = jnp.max(logits, axis=-1)
    teacher_exp = jnp.exp(teacher_logits - teacher_peak[:, None])
    stats = jnp.stack(
        [
            teacher_peak,
            jnp.sum(teacher_exp, axis=-1),
            jnp.sum(teacher_exp * (teacher_logits - logits), axis=-1),
            student_peak,
            jnp.sum(jnp.exp(logits - student_peak[:, None]), axis=-1),
        ]
    )

    def combined(many):
        t_peak, t_mass, t_gap, s_peak, s_mass = (many[:, i] for i in range(5))
        t_high = jnp.max(t_peak, axis=0)
        s_high = jnp.max(s_peak, axis=0)
        t_scale = jnp.exp(t_peak - t_high)
        s_scale = jnp.exp(s_peak - s_high)
        return jnp.stack(
            [
                t_high,
                jnp.sum(t_mass * t_scale, axis=0),
                jnp.sum(t_gap * t_scale, axis=0),
                s_high,
                jnp.sum(s_mass * s_scale, axis=0),
            ]
        )

    def flipped(rows):
        halves = rows.reshape(rows.shape[0], 2, -1)
        return jnp.where(wires.near_at == 0, halves, halves[:, ::-1]).reshape(rows.shape)

    stats = combined(lax.all_gather(flipped(stats), "mp"))
    stats = combined(
        wires.major_swap(jnp.broadcast_to(stats[None], (MAJOR, *stats.shape)))
    )
    stats = flipped(stats)
    teacher_total = stats[0] + jnp.log(stats[1])
    student_total = stats[3] + jnp.log(stats[4])
    divergence = stats[2] / stats[1] - teacher_total + student_total
    row_ids = jnp.arange(MAJOR, dtype=jnp.int32) * wires.minors + wires.minor
    row_lengths = jnp.sum(
        jnp.where(
            row_ids[:, None] == jnp.arange(lengths.shape[0], dtype=jnp.int32)[None, :],
            lengths[None, :],
            0,
        ),
        axis=1,
    )
    own_pos = own_at + jnp.arange(half, dtype=jnp.int32)
    other_pos = (half - own_at) + jnp.arange(half, dtype=jnp.int32)
    positions = jnp.stack([own_pos, other_pos])
    counted = (positions[:, None, :] < row_lengths[None, :, None]).reshape(-1)
    token_weight = jnp.where(counted, 1.0, 0.0) / jnp.sum(lengths).astype(F32)
    loss_part = jnp.sum(divergence * token_weight) * (1.0 / (MAJOR * wires.mp))
    grad_logits = (
        (
            jnp.exp(logits - student_total[:, None])
            - jnp.exp(teacher_logits - teacher_total[:, None])
        )
        * token_weight[:, None]
    ).astype(BF)

    rows_half = MAJOR * half
    share_other = dot_nt(grad_logits[rows_half:], head_part).astype(BF)
    share = dot_nt(grad_logits[:rows_half], head_part) + wires.near(share_other).astype(F32)
    share = wires.major_swap(share.astype(BF).reshape(MAJOR, half, width))
    share = jnp.sum(share.astype(F32), axis=0).astype(BF)
    grad_final = share.astype(F32) + wires.far(share).astype(F32)
    grad_stream, final_gain_grad, final_shift_grad = layer_norm_back(
        stream, final_norm[0], grad_final
    )
    bias_grads = [None] * layers
    vector_grads = [None] * layers
    mlp_shards = [None] * layers
    attn_shards = [None] * layers
    for layer in reversed(range(layers)):
        (
            layer_in,
            one,
            queries,
            key_rows,
            value_rows,
            totals,
            attended,
            middle,
            two,
            pre_act,
            hidden,
        ) = saved[layer]
        vector = norm_vectors[layer]
        full = layer_full[layer]
        up_cols = full[:, :units]
        down_rows = full[:, units : 2 * units]
        attn_cols = full[:, 2 * units : 2 * units + 3 * part]
        proj_rows = full[:, 2 * units + 3 * part :]
        grad_top = grad_stream
        out_own = grad_top.astype(BF)
        out = jnp.concatenate([out_own, wires.near(out_own)], axis=0)
        grad_hidden = dot(out, down_rows)
        grad_pre = jax.vjp(gelu_tanh, pre_act)[1](grad_hidden)[0].astype(BF)
        grad_two = wires.summed(
            dot_nt(grad_pre[half:], up_cols), dot_nt(grad_pre[:half], up_cols)
        )
        mlp_shards[layer] = wires.scattered(
            jnp.concatenate([dot_tn(two, grad_pre), dot_tn(out, hidden)], axis=1)
        )
        back, gain_two_grad, shift_two_grad = layer_norm_back(middle, vector[3], grad_two)
        grad_middle = grad_top + back
        mid_own = grad_middle.astype(BF)
        grad_attn = wires.natural(mid_own, wires.near(mid_own))
        grad_attended = dot(grad_attn, proj_rows).astype(BF)
        grad_proj = jnp.concatenate(
            attend_back(queries, key_rows, value_rows, grad_attended, totals, HD), axis=1
        )
        proj_own, proj_other = wires.own_first(grad_proj)
        grad_one = wires.summed(dot_nt(proj_other, attn_cols), dot_nt(proj_own, attn_cols))
        attn_shards[layer] = wires.scattered(
            jnp.concatenate([dot_tn(one, grad_proj), dot_tn(grad_attn, attended)], axis=1)
        )
        back, gain_one_grad, shift_one_grad = layer_norm_back(layer_in, vector[0], grad_one)
        grad_stream = grad_middle + back
        bias_grads[layer] = jnp.concatenate(
            [
                jnp.sum(grad_proj[:, :part], axis=0, dtype=F32)[None],
                jnp.sum(grad_proj[:, 2 * part :], axis=0, dtype=F32)[None],
                jnp.sum(grad_pre, axis=0, dtype=F32).reshape(up_blocks, part),
            ],
            axis=0,
        )
        vector_grads[layer] = jnp.stack(
            [
                gain_one_grad,
                shift_one_grad,
                jnp.sum(grad_middle, axis=0),
                gain_two_grad,
                shift_two_grad,
                jnp.sum(grad_top, axis=0),
            ]
        )
    input_grad = wires.natural(grad_stream, wires.near(grad_stream))

    everyone = wires.dp * wires.mp
    vectors = jnp.concatenate(
        [jnp.stack(vector_grads).reshape(-1), final_gain_grad, final_shift_grad]
    )
    biases = jnp.stack(bias_grads).reshape(wires.dp, 1, -1)
    mine = (jnp.arange(wires.mp, dtype=jnp.int32) == wires.mp_at)[None, :, None]
    biases = jnp.where(mine, biases, 0.0).reshape(everyone, -1)
    vector_cut = vectors.shape[0] // everyone
    small = jnp.concatenate([0.5 * vectors.reshape(everyone, vector_cut), biases], axis=1)
    small = jnp.sum(lax.all_to_all(small, ("dp", "mp"), 0, 0), axis=0)

    col_shard = jnp.stack(
        [
            jnp.concatenate(
                [
                    attn_shards[layer][:, : 3 * part].reshape(shard_rows, 3, part),
                    mlp_shards[layer][:, :units].reshape(shard_rows, up_blocks, part),
                ],
                axis=1,
            )
            for layer in range(layers)
        ]
    )
    row_shard = jnp.stack(
        [
            jnp.concatenate(
                [
                    attn_shards[layer][:, 3 * part :].T.reshape(1, part, shard_rows),
                    mlp_shards[layer][:, units:].T.reshape(up_blocks, part, shard_rows),
                ],
                axis=0,
            )
            for layer in range(layers)
        ]
    )
    squares = sum(
        jnp.sum(shard * shard) for shard in (*mlp_shards, *attn_shards)
    ) + jnp.sum(small * small)
    packet = jnp.concatenate([small, jnp.stack([squares, loss_part])])
    packet = lax.all_to_all(
        jnp.broadcast_to(packet[None], (everyone, packet.shape[0])), ("dp", "mp"), 0, 0
    )
    totals = jnp.sum(packet[:, -2:], axis=0)
    loss_total = totals[1]
    grad_norm = jnp.sqrt(totals[0])
    vectors = packet[:, :vector_cut].reshape(-1)
    vector_count = layers * 6 * width
    vector_sum = vectors[:vector_count].reshape(layers, 6, width)
    final_sum = vectors[vector_count:].reshape(2, width)
    bias_sum = jnp.sum(
        jnp.where(mine, packet[:, vector_cut:-2].reshape(wires.dp, wires.mp, -1), 0.0), axis=1
    ).reshape(column_biases.shape)

    clip = CLIP_LIMIT / jnp.maximum(grad_norm, CLIP_LIMIT)
    column_out = adam_update(
        column_weights, column_first, column_second, column_average, col_shard, clip, 0.1, 0.1
    )
    row_out = adam_update(
        row_weights, row_first, row_second, row_average, row_shard, clip, 0.2, 0.1
    )
    bias_out = adam_update(
        column_biases, bias_first, bias_second, bias_average, bias_sum, clip, 0.1, 0.0
    )
    vector_out = adam_update(
        norm_vectors, vector_first, vector_second, vector_average, vector_sum, clip, 0.5, 0.0
    )
    final_state = adam_update(
        final_norm, final_first, final_second, final_average, final_sum, clip, 0.5, 0.0
    )
    return (
        loss_total,
        grad_norm,
        input_grad,
        *column_out,
        *row_out,
        *bias_out,
        *vector_out,
        *final_state,
    )


def solution(mesh):
    tokens, copied = P("dp", None), P()
    columns, rows, biases = P(None, "dp", None, "mp"), P(None, None, "mp", "dp"), P(None, None, "mp")
    placed = (
        tokens,
        copied,
        tokens,
        P("dp", None, None),
        P(None, "dp"),
        P("dp", "mp"),
        P("mp"),
        P("mp", "dp"),
        copied,
        P("dp", "mp"),
        P("dp", "mp"),
        *[columns] * 4,
        *[rows] * 4,
        *[biases] * 4,
        *[copied] * 8,
    )
    return jax.shard_map(
        local,
        mesh=mesh,
        in_specs=placed,
        out_specs=(
            copied,
            copied,
            tokens,
            *[columns] * 4,
            *[rows] * 4,
            *[biases] * 4,
            *[copied] * 8,
        ),
        check_vma=False,
    )
```

```python
import functools

import jax
import jax.numpy as jnp
from jax import lax
from jax.experimental import pallas as pl
from jax.experimental.pallas import tpu as pltpu
from jax.sharding import PartitionSpec as P

HD = 64
THEADS = 25
THD = 64
SEQ = 512
STEP = 4
MAJOR = 4

EPSILON = 1e-05
GELU_COEFF = 0.7978845608028654
BETA_ONE = 0.9
BETA_TWO = 0.999
ADAM_EPSILON = 1e-08
CLIP_LIMIT = 0.002

BF = jnp.bfloat16
F32 = jnp.float32


def dot(a, b):
    return jnp.dot(a, b, preferred_element_type=F32)


def dot_nt(a, b):
    return lax.dot_general(a, b, (((1,), (1,)), ((), ())), preferred_element_type=F32)


def dot_tn(a, b):
    return lax.dot_general(a, b, (((0,), (0,)), ((), ())), preferred_element_type=F32)


def layer_norm(values, gain, shift):
    centered = values - jnp.mean(values, axis=-1, keepdims=True)
    variance = jnp.mean(centered * centered, axis=-1, keepdims=True)
    return centered * lax.rsqrt(variance + EPSILON) * gain + shift


def gelu_tanh(values):
    return (
        0.5 * values * (1.0 + jnp.tanh(GELU_COEFF * (values + 0.044715 * values * values * values)))
    )


def kernel_call(body, outs, blocks, scratch=(), vmem=24 << 20, flops=10**6):
    specs, operands = [], []
    for entry in blocks:
        if isinstance(entry, tuple):
            array, shape, index = entry
            specs.append(pl.BlockSpec(shape, functools.partial(lambda at, _: at, index)))
            operands.append(array)
        elif entry.dtype == jnp.int32:
            specs.append(pl.BlockSpec(memory_space=pltpu.SMEM))
            operands.append(entry)
        else:
            whole = (0,) * entry.ndim
            specs.append(pl.BlockSpec(entry.shape, functools.partial(lambda at, _: at, whole)))
            operands.append(entry)
    return pl.pallas_call(
        body,
        grid=(1,),
        out_shape=[jax.ShapeDtypeStruct(shape, kind) for shape, kind in outs],
        in_specs=specs,
        out_specs=[
            pl.BlockSpec(shape, functools.partial(lambda at, _: at, (0,) * len(shape)))
            for shape, _ in outs
        ],
        scratch_shapes=list(scratch),
        compiler_params=pltpu.CompilerParams(vmem_limit_bytes=vmem),
        cost_estimate=pl.CostEstimate(flops=flops, transcendentals=0, bytes_accessed=10**5),
    )(*operands)


def masked_scores(queries, key_rows, start):
    scores = dot_nt(queries, key_rows) * (queries.shape[1] ** (-0.5))
    query_pos = start + lax.broadcasted_iota(jnp.int32, scores.shape, 0)
    key_pos = lax.broadcasted_iota(jnp.int32, scores.shape, 1)
    return jnp.where(key_pos <= query_pos, scores, -jnp.inf)


def attention_forward_body(
    heads, size, near_ref, kept_ref, own_ref, other_ref, weight_ref, bias_ref,
    share_ref, own_share_ref, out_ref, qkv_ref, total_ref,
):
    half, part = own_ref.shape[0], heads * size
    first = near_ref[0] == 0
    attn = weight_ref[:, : 3 * part]
    own = dot(own_ref[...], attn) + bias_ref[...]
    other = dot(other_ref[...], attn) + bias_ref[...]
    qkv_ref[:half, :] = jnp.where(first, own, other).astype(BF)
    qkv_ref[half:, :] = jnp.where(first, other, own).astype(BF)
    lane = lax.broadcasted_iota(jnp.int32, (half, total_ref.shape[1]), 1)
    for block in range(2):
        rows = slice(block * half, (block + 1) * half)
        seen = (block + 1) * half
        to = pl.multiple_of((near_ref[0] ^ block) * half, half)
        totals = jnp.zeros(lane.shape, F32)
        for head in range(heads):
            q = qkv_ref[rows, head * size : (head + 1) * size]
            k = qkv_ref[:seen, part + head * size : part + (head + 1) * size]
            v = qkv_ref[:seen, 2 * part + head * size : 2 * part + (head + 1) * size]
            scores = masked_scores(q, k, block * half)
            highest = jnp.max(scores, axis=-1, keepdims=True)
            mass = jnp.exp(scores - highest)
            whole = jnp.sum(mass, axis=-1, keepdims=True)
            weights = (mass * (1.0 / whole)).astype(BF)
            result = jnp.where(kept_ref[head] == 1, dot(weights, v), 0.0)
            out_ref[pl.ds(to, half), head * size : (head + 1) * size] = result.astype(BF)
            totals = jnp.where(lane == head, highest + jnp.log(whole), totals)
        total_ref[rows, :] = totals
    proj = weight_ref[:, 3 * part : 4 * part]
    put(share_ref, dot_nt(out_ref[half:, :], proj))
    put(own_share_ref, dot_nt(out_ref[:half, :], proj))


def mlp_forward_body(
    own_ref, other_ref, up_ref, down_ref, bias_ref, pre_ref, hidden_ref, share_ref, own_share_ref
):
    half = own_ref.shape[0]
    for rows, from_ref in ((slice(half, None), other_ref), (slice(0, half), own_ref)):
        pre = dot(from_ref[...], up_ref[...]) + bias_ref[...]
        pre_ref[rows, :] = pre
        hidden = gelu_tanh(pre).astype(BF)
        hidden_ref[rows, :] = hidden
        share = dot_nt(hidden, down_ref[...])
        if from_ref is other_ref:
            share_ref[...] = share.astype(BF)
        else:
            own_share_ref[...] = share


def gelu_slope(values):
    inner = jnp.tanh(GELU_COEFF * (values + 0.044715 * values * values * values))
    slope = GELU_COEFF * (1.0 + 3.0 * 0.044715 * values * values)
    return 0.5 * (1.0 + inner) + 0.5 * values * (1.0 - inner * inner) * slope


def mlp_backward_body(
    own_ref, other_ref, up_ref, down_ref, pre_ref, grad_ref, bias_ref, share_ref, own_share_ref
):
    half = own_ref.shape[0]
    total = jnp.zeros(bias_ref.shape, F32)
    for rows, from_ref in ((slice(half, None), other_ref), (slice(0, half), own_ref)):
        grad = (dot(from_ref[...], down_ref[...]) * gelu_slope(pre_ref[rows, :])).astype(BF)
        grad_ref[rows, :] = grad
        total = total + jnp.sum(grad.astype(F32), axis=0, keepdims=True)
        share = dot_nt(grad, up_ref[...])
        if from_ref is other_ref:
            share_ref[...] = share.astype(BF)
        else:
            own_share_ref[...] = share
    bias_ref[...] = total


def attention_backward_body(
    heads, size, near_ref, own_ref, other_ref, weight_ref, qkv_ref, total_ref,
    grad_ref, bias_ref, share_ref, own_share_ref, grad_out_ref, key_ref, value_ref,
):
    half, part = own_ref.shape[0], heads * size
    scale = size ** (-0.5)
    first = near_ref[0] == 0
    proj = weight_ref[:, 3 * part : 4 * part]
    own = dot(own_ref[...], proj)
    other = dot(other_ref[...], proj)
    grad_out_ref[:half, :] = jnp.where(first, own, other).astype(BF)
    grad_out_ref[half:, :] = jnp.where(first, other, own).astype(BF)
    spots = [pl.multiple_of((near_ref[0] ^ block) * half, half) for block in range(2)]
    for head in range(heads):
        at = [slice(i * part + head * size, i * part + (head + 1) * size) for i in range(3)]
        for block in range(2):
            rows = slice(block * half, (block + 1) * half)
            seen = (block + 1) * half
            q = qkv_ref[rows, at[0]]
            k = qkv_ref[:seen, at[1]]
            v = qkv_ref[:seen, at[2]]
            grad_out = grad_out_ref[rows, at[0]]
            probs = jnp.exp(masked_scores(q, k, block * half) - total_ref[rows, head : head + 1])
            grad_probs = dot_nt(grad_out, v)
            inner = jnp.sum(probs * grad_probs, axis=-1, keepdims=True)
            grad_scores = (probs * (grad_probs - inner) * scale).astype(BF)
            grad_ref[pl.ds(spots[block], half), at[0]] = dot(grad_scores, k).astype(BF)
            grad_k = dot_tn(grad_scores, q)
            grad_v = dot_tn(probs.astype(BF), grad_out)
            if block == 0:
                key_ref[...] = grad_k
                value_ref[...] = grad_v
            else:
                for side in range(2):
                    part_rows = slice(side * half, (side + 1) * half)
                    whole_k, whole_v = grad_k[part_rows], grad_v[part_rows]
                    if side == 0:
                        whole_k = whole_k + key_ref[...]
                        whole_v = whole_v + value_ref[...]
                    grad_ref[pl.ds(spots[side], half), at[1]] = whole_k.astype(BF)
                    grad_ref[pl.ds(spots[side], half), at[2]] = whole_v.astype(BF)
    bias_ref[...] = jnp.sum(grad_ref[...].astype(F32), axis=0, keepdims=True)
    attn = weight_ref[:, : 3 * part]
    share_ref[...] = dot_nt(grad_ref[half:, :], attn).astype(BF)
    own_share_ref[...] = dot_nt(grad_ref[:half, :], attn)


def padded_width(width):
    return -(-width // 128) * 128


def put(out_ref, value):
    width = value.shape[1]
    out_ref[:, :width] = value.astype(out_ref.dtype)
    if out_ref.shape[1] > width:
        out_ref[:, width:] = jnp.zeros((value.shape[0], out_ref.shape[1] - width), out_ref.dtype)


def weave_body(minor_ref, mine_ref, theirs_ref, out_ref):
    first = minor_ref[0] == 0
    out_ref[0, 0] = jnp.where(first, mine_ref[0], theirs_ref[0])
    out_ref[0, 1] = jnp.where(first, theirs_ref[0], mine_ref[0])


def weave_call(minor, mine, theirs, start, rows):
    majors, _, cols = mine.shape
    block = pl.BlockSpec(
        (pl.Element(1), pl.Element(rows), pl.Element(cols)), lambda k: (k, start, 0)
    )
    return pl.pallas_call(
        weave_body,
        grid=(majors,),
        out_shape=jax.ShapeDtypeStruct((majors, 2, rows, cols), mine.dtype),
        in_specs=[pl.BlockSpec(memory_space=pltpu.SMEM), block, block],
        out_specs=pl.BlockSpec((1, 2, rows, cols), lambda k: (k, 0, 0, 0)),
        compiler_params=pltpu.CompilerParams(vmem_limit_bytes=16 << 20),
        cost_estimate=pl.CostEstimate(flops=10**5, transcendentals=0, bytes_accessed=10**5),
    )(minor, mine, theirs).reshape(majors * 2 * rows, cols)


def up_body(own_ref, other_ref, weight_ref, bias_ref, out_ref):
    half = own_ref.shape[0]
    depth = weight_ref.shape[0]
    for rows, from_ref in ((slice(half, None), other_ref), (slice(0, half), own_ref)):
        pre = dot(from_ref[:, :depth], weight_ref[...]) + bias_ref[...]
        out_ref[rows, :] = gelu_tanh(pre).astype(BF)


def down_body(hidden_ref, weight_ref, share_ref, own_share_ref):
    half = share_ref.shape[0]
    put(share_ref, dot_nt(hidden_ref[half:, :], weight_ref[...]))
    put(own_share_ref, dot_nt(hidden_ref[:half, :], weight_ref[...]))


def norm_forward_body(stream_ref, pair_ref, far_ref, bias_ref, gain_ref, shift_ref, new_ref, out_ref):
    width = stream_ref.shape[1]
    new = (
        stream_ref[...]
        + (pair_ref[:, :width].astype(F32) + far_ref[:, :width].astype(F32))
        + bias_ref[...]
    )
    new_ref[...] = new
    put(out_ref, layer_norm(new, gain_ref[...], shift_ref[...]))


def norm_backward_body(values_ref, gain_ref, pair_ref, far_ref, *refs):
    *top_ref, new_ref, low_ref, sums_ref = refs
    grad = pair_ref[...].astype(F32) + far_ref[...].astype(F32)
    values = values_ref[...]
    centered = values - jnp.mean(values, axis=-1, keepdims=True)
    variance = jnp.mean(centered * centered, axis=-1, keepdims=True)
    scale = lax.rsqrt(variance + EPSILON)
    unit = centered * scale
    inner = grad * gain_ref[...]
    new = scale * (
        inner
        - jnp.mean(inner, axis=-1, keepdims=True)
        - unit * jnp.mean(inner * unit, axis=-1, keepdims=True)
    )
    if top_ref:
        new = top_ref[0][...] + new
    new_ref[...] = new
    low_ref[...] = new.astype(BF)
    sums_ref[0:1, :] = jnp.sum(grad * unit, axis=0, keepdims=True)
    sums_ref[1:2, :] = jnp.sum(grad, axis=0, keepdims=True)
    sums_ref[2:3, :] = jnp.sum(new, axis=0, keepdims=True)
    sums_ref[3:, :] = jnp.zeros_like(sums_ref[3:, :])


def norm_forward(stream, pair, far, bias, gain, shift):
    return kernel_call(
        norm_forward_body,
        [(stream.shape, F32), (pair.shape, BF)],
        [stream, pair, far, bias[None], gain[None], shift[None]],
        vmem=16 << 20,
    )


def norm_backward(values, gain, pair, far, *top):
    return kernel_call(
        norm_backward_body,
        [(values.shape, F32), (values.shape, BF), ((8, values.shape[1]), F32)],
        [values, gain[None], pair, far, *top],
        vmem=16 << 20,
    )


def weight_grad_body(shape, count, minor_ref, *refs):
    majors, minors, rows = shape
    operands, (mine_ref, theirs_ref, sum_ref) = refs[: 3 * count], refs[3 * count :]
    start = 0
    for at in range(count):
        own, other, grad = operands[3 * at : 3 * at + 3]
        half, cols = own.shape[0], grad.shape[1]
        sum_ref[:, start : start + cols] = dot_tn(own[...], grad[:half, :]) + dot_tn(
            other[...], grad[half:, :]
        )
        start += cols
    for k in range(majors):
        to = slice(k * rows, (k + 1) * rows)
        here = pl.multiple_of((k * minors + minor_ref[0]) * rows, 8)
        there = pl.multiple_of((k * minors + 1 - minor_ref[0]) * rows, 8)
        mine_ref[to, :] = sum_ref[pl.ds(here, rows), :]
        theirs_ref[to, :] = sum_ref[pl.ds(there, rows), :].astype(BF)


STATS = 8


def logits_body(
    place_ref, teacher_ref, student_ref, teacher_head_ref, head_ref, t_ref, z_ref, stats_ref
):
    counted = place_ref[1 + pl.program_id(0)] > place_ref[0]

    @pl.when(counted)
    def _():
        t = dot(teacher_ref[:, : teacher_head_ref.shape[0]], teacher_head_ref[...])
        t_ref[...] = t
        z = dot(student_ref[...], head_ref[...])
        z_ref[...] = z
        t_peak = jnp.max(t, axis=-1, keepdims=True)
        t_exp = jnp.exp(t - t_peak)
        z_peak = jnp.max(z, axis=-1, keepdims=True)
        columns = (
            t_peak,
            jnp.sum(t_exp, axis=-1, keepdims=True),
            jnp.sum(t_exp * (t - z), axis=-1, keepdims=True),
            z_peak,
            jnp.sum(jnp.exp(z - z_peak), axis=-1, keepdims=True),
        )
        lane = lax.broadcasted_iota(jnp.int32, (t.shape[0], 128), 1)
        packed = jnp.zeros(lane.shape, F32)
        for at, column in enumerate(columns):
            packed = jnp.where(lane == at, column, packed)
        stats_ref[...] = packed.T[:STATS, :]

    @pl.when(jnp.logical_not(counted))
    def _():
        row = lax.broadcasted_iota(jnp.int32, stats_ref.shape, 0)
        stats_ref[...] = jnp.where((row == 1) | (row == 4), 1.0, 0.0)


def merge_body(*refs):
    *in_refs, out_ref = refs
    many = [ref[...] for ref in in_refs]
    if many[0].ndim == 3:
        many = [many[0][k] for k in range(many[0].shape[0])]
    t_high = functools.reduce(jnp.maximum, [one[0:1] for one in many])
    z_high = functools.reduce(jnp.maximum, [one[3:4] for one in many])
    t_scale = [jnp.exp(one[0:1] - t_high) for one in many]
    z_scale = [jnp.exp(one[3:4] - z_high) for one in many]
    out_ref[0:1, :] = t_high
    out_ref[1:2, :] = sum(one[1:2] * scale for one, scale in zip(many, t_scale))
    out_ref[2:3, :] = sum(one[2:3] * scale for one, scale in zip(many, t_scale))
    out_ref[3:4, :] = z_high
    out_ref[4:5, :] = sum(one[4:5] * scale for one, scale in zip(many, z_scale))
    out_ref[5:, :] = jnp.zeros_like(out_ref[5:, :])


def logits_back_body(place_ref, weight_ref, t_ref, z_ref, stats_ref, head_ref, *refs):
    out_ref = refs[-1]
    length = place_ref[1 + pl.program_id(0)]

    @pl.when(length > place_ref[0])
    def _():
        stats = stats_ref[...]
        row = lax.broadcasted_iota(jnp.int32, stats.shape, 0)
        logs = jnp.log(jnp.where((row == 1) | (row == 4), stats, 1.0))
        totals = stats + pltpu.roll(logs, STATS - 1, 0)
        totals = jnp.concatenate([totals] * (128 // STATS), axis=0).T
        rows = t_ref.shape[0]
        position = place_ref[0] + lax.broadcasted_iota(jnp.int32, (rows, 1), 0)
        weight = jnp.where(position < length, weight_ref[0], 0.0)
        grad = (jnp.exp(z_ref[...] - totals[:, 3:4]) - jnp.exp(t_ref[...] - totals[:, 0:1])) * weight
        share = dot_nt(grad.astype(BF), head_ref[...])
        if len(refs) == 2:
            share = share + refs[0][...].astype(F32)
        out_ref[...] = share.astype(BF)

    @pl.when(length <= place_ref[0])
    def _():
        out_ref[...] = jnp.zeros_like(out_ref) if len(refs) == 1 else refs[0][...]


def row_blocks(rows, cols):
    return pl.BlockSpec((rows, cols), lambda i: (i, 0))


def held_block(array):
    return pl.BlockSpec(array.shape, lambda i: (0, 0), pipeline_mode=pl.Buffered(1))


def stat_blocks(rows):
    return pl.BlockSpec((STATS, rows), lambda i: (0, i))


SCALAR = pl.BlockSpec(memory_space=pltpu.SMEM)


def logits_call(place, teacher, student, teacher_head, head):
    tokens = teacher.shape[0]
    rows, vocab = tokens // MAJOR, head.shape[1]
    return pl.pallas_call(
        logits_body,
        grid=(MAJOR,),
        out_shape=[
            jax.ShapeDtypeStruct((tokens, vocab), F32),
            jax.ShapeDtypeStruct((tokens, vocab), F32),
            jax.ShapeDtypeStruct((STATS, tokens), F32),
        ],
        in_specs=[
            SCALAR,
            row_blocks(rows, teacher.shape[1]),
            row_blocks(rows, student.shape[1]),
            held_block(teacher_head),
            held_block(head),
        ],
        out_specs=[row_blocks(rows, vocab), row_blocks(rows, vocab), stat_blocks(rows)],
        compiler_params=pltpu.CompilerParams(vmem_limit_bytes=44 << 20),
        cost_estimate=pl.CostEstimate(
            flops=10**6,
            transcendentals=0,
            bytes_accessed=10**5,
        ),
    )(place, teacher, student, teacher_head, head)


def logits_back_call(place, weight, t, z, stats, head, *more):
    tokens, vocab = t.shape
    rows, width = tokens // MAJOR, head.shape[0]
    return pl.pallas_call(
        logits_back_body,
        grid=(MAJOR,),
        out_shape=jax.ShapeDtypeStruct((tokens, width), BF),
        in_specs=[
            SCALAR,
            SCALAR,
            row_blocks(rows, vocab),
            row_blocks(rows, vocab),
            stat_blocks(rows),
            held_block(head),
            *[row_blocks(rows, width) for _ in more],
        ],
        out_specs=row_blocks(rows, width),
        compiler_params=pltpu.CompilerParams(vmem_limit_bytes=40 << 20),
        cost_estimate=pl.CostEstimate(
            flops=10**6,
            transcendentals=0,
            bytes_accessed=10**5,
        ),
    )(place, weight, t, z, stats, head, *more)


def merged(*many):
    return pl.pallas_call(
        merge_body, out_shape=jax.ShapeDtypeStruct(many[0].shape[-2:], F32)
    )(*many)


def adam_update(weight, first, second, average, grad, clip, rate, decay):
    keep = min(0.995, (1.0 + STEP) / (10.0 + STEP))
    grad = grad * clip
    first_new = BETA_ONE * first + (1.0 - BETA_ONE) * grad
    second_new = BETA_TWO * second + (1.0 - BETA_TWO) * grad * grad
    first_hat = first_new / (1.0 - BETA_ONE**STEP)
    second_hat = second_new / (1.0 - BETA_TWO**STEP)
    weight_new = weight - rate * (
        first_hat / (jnp.sqrt(second_hat) + ADAM_EPSILON) + decay * weight
    )
    average_new = keep * average + (1.0 - keep) * weight_new
    return (weight_new, first_new, second_new, average_new)


def tie(first, second):
    return lax.optimization_barrier((first, second))


class Wires:
    def __init__(self):
        self.dp = lax.axis_size("dp")
        self.mp = lax.axis_size("mp")
        self.minors = self.dp // MAJOR
        self.dp_at = lax.axis_index("dp")
        self.mp_at = lax.axis_index("mp")
        self.major = self.dp_at // self.minors
        self.minor = self.dp_at % self.minors
        self.near_at = self.mp_at % 2
        self.near_ref = self.near_at.reshape(1).astype(jnp.int32)
        self.minor_ref = self.minor.reshape(1).astype(jnp.int32)
        self.near_pairs = [(i, i ^ 1) for i in range(self.mp)]
        self.far_pairs = [(i, i ^ 2) for i in range(self.mp)]
        self.over_major = [
            [k * self.minors + j for k in range(MAJOR)] for j in range(self.minors)
        ]
        self.over_minor = [
            [k * self.minors + j for j in range(self.minors)] for k in range(MAJOR)
        ]

    def near(self, part):
        return lax.ppermute(part, "mp", self.near_pairs)

    def far(self, part):
        return lax.ppermute(part, "mp", self.far_pairs)

    def natural(self, own, other):
        first = self.near_at == 0
        return jnp.concatenate([jnp.where(first, own, other), jnp.where(first, other, own)], axis=0)

    def own_first(self, whole):
        half = whole.shape[0] // 2
        own = lax.dynamic_slice_in_dim(whole, self.near_at * half, half, 0)
        other = lax.dynamic_slice_in_dim(whole, (1 - self.near_at) * half, half, 0)
        return own, other

    def shares(self, other, own):
        pair = (own + self.near(other.astype(BF)).astype(F32)).astype(BF)
        return pair, self.far(pair)

    def minor_parts(self, part):
        if self.minors == 2:
            return lax.ppermute(part, "dp", [(i, i ^ 1) for i in range(self.dp)])
        return lax.all_gather(part, "dp", axis=0, axis_index_groups=self.over_minor)

    def minor_stack(self, part, others, axis):
        if self.minors == 2:
            first = self.minor == 0
            return jnp.stack(
                [jnp.where(first, part, others), jnp.where(first, others, part)], axis=axis
            )
        return jnp.moveaxis(others, 0, axis)

    def major_gather(self, part):
        return lax.all_gather(
            part, "dp", axis=0, tiled=True, axis_index_groups=self.over_major
        )

    def minor_joined(self, part):
        return self.minor_stack(part, self.minor_parts(part), 0).reshape(-1, part.shape[-1])

    def minor_woven(self, part, others, start=0, rows=None):
        rows = part.shape[1] if rows is None else rows
        if self.minors == 2:
            return weave_call(self.minor_ref, part, others, start, rows)
        stacked = self.minor_stack(part, others, 1)[:, :, start : start + rows]
        return stacked.reshape(-1, part.shape[-1])

    def major_swap(self, part):
        return lax.all_to_all(part, "dp", 0, 0, axis_index_groups=self.over_major)

    def grad_started(self, *products):
        width, cols = products[0][0].shape[1], sum(grad.shape[1] for _, _, grad in products)
        rows = width // self.dp
        if self.minors == 2 and rows % 8 == 0:
            mine, theirs = kernel_call(
                functools.partial(
                    weight_grad_body, (MAJOR, self.minors, rows), len(products)
                ),
                [((MAJOR * rows, cols), F32), ((MAJOR * rows, cols), BF)],
                [self.minor_ref, *sum(([*product] for product in products), [])],
                scratch=[pltpu.VMEM((width, cols), F32)],
                vmem=40 << 20,
                flops=2 * 2 * products[0][0].shape[0] * width * cols,
            )
            return mine, self.minor_parts(theirs)
        total = jnp.concatenate(
            [dot_tn(jnp.concatenate(product[:2]), product[2]) for product in products], axis=1
        )
        held = lax.psum_scatter(
            total.reshape(MAJOR, self.minors, rows, cols).astype(BF),
            "dp",
            scatter_dimension=1,
            axis_index_groups=self.over_minor,
        )
        return held.reshape(-1, cols).astype(F32), None

    def grad_ended(self, mine, theirs, direct=False):
        held = (mine if theirs is None else mine + theirs.astype(F32)).astype(BF)
        if direct:
            held = self.major_swap(held.reshape(MAJOR, -1, held.shape[-1]))
            return jnp.sum(held.astype(F32), axis=0)
        return lax.psum_scatter(
            held, "dp", scatter_dimension=0, tiled=True, axis_index_groups=self.over_major
        ).astype(F32)


def local(
    inputs,
    lengths,
    teacher_inputs,
    teacher_qkv,
    teacher_proj,
    teacher_up,
    teacher_up_bias,
    teacher_down,
    teacher_vectors,
    teacher_head,
    head,
    column_weights,
    column_first,
    column_second,
    column_average,
    row_weights,
    row_first,
    row_second,
    row_average,
    column_biases,
    bias_first,
    bias_second,
    bias_average,
    norm_vectors,
    vector_first,
    vector_second,
    vector_average,
    final_norm,
    final_first,
    final_second,
    final_average,
):
    wires = Wires()
    token_count, width = inputs.shape
    half = token_count // 2
    teacher_width = teacher_inputs.shape[1]
    layers, shard_rows, col_blocks, part = column_weights.shape
    up_blocks = col_blocks - 3
    units = up_blocks * part

    slots = -(-THEADS // wires.mp)
    base_heads = THEADS // wires.mp
    extra_heads = THEADS % wires.mp
    own_start = wires.mp_at * base_heads + jnp.minimum(wires.mp_at, extra_heads)
    own_stop = own_start + base_heads + jnp.where(wires.mp_at < extra_heads, 1, 0)
    slot_start = jnp.minimum(own_start, THEADS - slots)
    head_ids = slot_start + jnp.arange(slots, dtype=jnp.int32)
    owned = ((head_ids >= own_start) & (head_ids < own_stop)).astype(jnp.int32)
    slot_width = slots * THD
    first_col = slot_start * THD

    qkv_shard = lax.dynamic_slice_in_dim(teacher_qkv, first_col, slot_width, 2)
    proj_shard = lax.dynamic_slice_in_dim(teacher_proj, first_col, slot_width, 0).T
    shards = []
    for layer in range(layers):
        cols = column_weights[layer].astype(BF)
        rows = row_weights[layer].astype(BF)
        shards.append(
            jnp.concatenate(
                [
                    cols[:, 3:].reshape(shard_rows, units),
                    rows[1:].reshape(units, shard_rows).T,
                    cols[:, :3].reshape(shard_rows, 3 * part),
                    rows[0].T,
                ],
                axis=1,
            )
        )
    shards.extend(
        [
            jnp.concatenate([qkv_shard.reshape(-1, 3 * slot_width), proj_shard], axis=1),
            teacher_up,
            teacher_down.T,
        ]
    )
    held, rows, others = [], [], []

    def launch(mark):
        shard = shards[len(held)]
        if mark is not None:
            shard, mark = tie(shard, mark)
        if held:
            shard, rows[-1] = tie(shard, held[-1])
        held.append(wires.major_gather(shard).reshape(MAJOR, *shard.shape))
        rows.append(held[-1])
        others.append(wires.minor_parts(held[-1]))
        return mark

    for _ in range(layers):
        launch(None)
    vocab_part = head.shape[1] // MAJOR
    cut = teacher_head.shape[0]
    both = jnp.stack(
        [
            jnp.concatenate(
                [rows_[:, k * vocab_part : (k + 1) * vocab_part] for rows_ in (teacher_head, head)],
                axis=0,
            )
            for k in range(MAJOR)
        ]
    )

    own_at = wires.near_at * half
    stream = lax.dynamic_slice_in_dim(inputs, own_at, half, 0).astype(F32)
    heads = part // HD
    all_heads = jnp.ones((heads,), jnp.int32)

    layer_full = []

    def columns(layer, at):
        return (layer_full[layer], (width, units), (0, at))

    saved = []
    one_own = layer_norm(stream, norm_vectors[0, 0], norm_vectors[0, 1]).astype(BF)
    for layer in range(layers):
        vector = norm_vectors[layer]
        layer_full.append(wires.minor_woven(rows[layer], others[layer]))
        one = (one_own, wires.near(one_own))
        bias = column_biases[layer]
        share, own_share, attended, qkv, totals = kernel_call(
            functools.partial(attention_forward_body, heads, HD),
            [
                ((half, width), BF),
                ((half, width), F32),
                ((token_count, part), BF),
                ((token_count, 3 * part), BF),
                ((token_count, 128), F32),
            ],
            [
                wires.near_ref,
                all_heads,
                *one,
                columns(layer, 2),
                jnp.concatenate([bias[0], jnp.zeros_like(bias[0]), bias[1]])[None],
            ],
        )
        if len(held) < len(shards):
            share = launch(share)
        middle, two_own = norm_forward(
            stream, *wires.shares(share, own_share), vector[2], vector[3], vector[4]
        )
        two = (two_own, wires.near(two_own))
        pre_act, hidden, share, own_share = kernel_call(
            mlp_forward_body,
            [
                ((token_count, units), F32),
                ((token_count, units), BF),
                ((half, width), BF),
                ((half, width), F32),
            ],
            [*two, columns(layer, 0), columns(layer, 1), bias[2:].reshape(1, units)],
        )
        saved.append((stream, one, qkv, totals, attended, middle, two, pre_act, hidden))
        later = norm_vectors[layer + 1] if layer + 1 < layers else final_norm
        parts, others[layer + 1] = tie(wires.shares(share, own_share), others[layer + 1])
        stream, one_own = norm_forward(middle, *parts, vector[5], later[0], later[1])
        if len(held) < len(shards):
            one_own = launch(one_own)
    final_out = one_own
    while len(held) < len(shards):
        launch(None)
    both, final_out = tie(both, final_out)
    both, rows[-2] = tie(both, rows[-2])
    both = wires.major_swap(both)
    both_others = wires.minor_parts(both)
    final_out, rows[-1] = tie(final_out, rows[-1])
    student_rows = wires.major_gather(final_out)

    tv = teacher_vectors
    teacher_pad = padded_width(teacher_width)
    teacher_stream, teacher_other = (
        lax.dynamic_slice_in_dim(teacher_inputs, at, half, 0).astype(F32)
        for at in (own_at, half - own_at)
    )
    query_bias, value_bias = (
        lax.dynamic_slice_in_dim(tv[at], first_col, slot_width) for at in (2, 3)
    )
    (mine, theirs), rows[-2] = tie((rows[-3], others[-3]), rows[-2])
    teacher_attn = wires.minor_woven(mine, theirs)
    teacher_share, teacher_own_share = kernel_call(
        functools.partial(attention_forward_body, slots, THD),
        [((half, teacher_pad), BF), ((half, teacher_pad), F32)],
        [
            wires.near_ref,
            owned,
            layer_norm(teacher_stream, tv[0], tv[1]).astype(BF),
            layer_norm(teacher_other, tv[0], tv[1]).astype(BF),
            teacher_attn,
            jnp.concatenate([query_bias, jnp.zeros_like(query_bias), value_bias])[None],
        ],
        scratch=[
            pltpu.VMEM((token_count, slot_width), BF),
            pltpu.VMEM((token_count, 3 * slot_width), BF),
            pltpu.VMEM((token_count, 128), F32),
        ],
        vmem=36 << 20,
    )
    parts, (others[-2], rows[-1]) = tie(
        wires.shares(teacher_share, teacher_own_share), (others[-2], rows[-1])
    )
    teacher_up_full = wires.minor_woven(rows[-2], others[-2])
    teacher_mid, normed_own = norm_forward(teacher_stream, *parts, tv[4], tv[5], tv[6])
    (hidden,) = kernel_call(
        up_body,
        [((token_count, teacher_up.shape[1]), BF)],
        [normed_own, wires.near(normed_own), teacher_up_full, teacher_up_bias[None]],
        vmem=32 << 20,
    )
    (mine, theirs), both = tie((rows[-1], others[-1]), both)
    share, own_share = kernel_call(
        down_body,
        [((half, teacher_pad), BF), ((half, teacher_pad), F32)],
        [hidden, wires.minor_woven(mine, theirs)],
        vmem=32 << 20,
    )
    _, teacher_final = norm_forward(
        teacher_mid, *wires.shares(share, own_share), tv[7], tv[8], tv[9]
    )
    teacher_final, student_rows = tie(teacher_final, student_rows)
    teacher_rows = wires.major_gather(teacher_final)
    teacher_head_part = wires.minor_woven(both, both_others, 0, cut)
    head_part = wires.minor_woven(both, both_others, cut, head.shape[0])

    teacher_sides = (teacher_rows, wires.near(teacher_rows))
    student_sides = (student_rows, wires.near(student_rows))
    row_ids = jnp.arange(MAJOR, dtype=jnp.int32) * wires.minors + wires.minor
    row_lengths = jnp.sum(
        jnp.where(
            row_ids[:, None] == jnp.arange(lengths.shape[0], dtype=jnp.int32)[None, :],
            lengths[None, :],
            0,
        ),
        axis=1,
    )
    places = [
        jnp.concatenate([start.reshape(1).astype(jnp.int32), row_lengths])
        for start in (own_at, half - own_at)
    ]
    row_weight = 1.0 / jnp.sum(lengths).astype(F32)
    sides = [
        logits_call(place, teacher, student, teacher_head_part, head_part)
        for place, teacher, student in zip(places, teacher_sides, student_sides)
    ]
    stats = merged(sides[0][2], wires.near(sides[1][2]))
    stats = merged(stats, wires.far(stats))
    stats = merged(
        wires.major_swap(jnp.broadcast_to(stats[None], (MAJOR, *stats.shape)))
    )
    other_stats = wires.near(stats)
    divergence = (
        stats[2] / stats[1] - (stats[0] + jnp.log(stats[1])) + (stats[3] + jnp.log(stats[4]))
    ).reshape(MAJOR, half)
    counted = own_at + jnp.arange(half, dtype=jnp.int32)[None, :] < row_lengths[:, None]
    loss_part = jnp.sum(jnp.where(counted, divergence, 0.0)) * (
        row_weight * (2.0 / (MAJOR * wires.mp))
    )

    weight = row_weight.reshape(1)
    share = logits_back_call(places[1], weight, *sides[1][:2], other_stats, head_part)
    share = logits_back_call(
        places[0], weight, *sides[0][:2], stats, head_part, wires.near(share)
    )
    share = wires.major_swap(share.reshape(MAJOR, half, width))
    share = jnp.sum(share.astype(F32), axis=0).astype(BF)
    grad_stream, out_own, final_sums = norm_backward(
        stream, final_norm[0], share, wires.far(share)
    )
    bias_grads, vector_grads = [], []
    products, started, ended = [], [], []

    def start():
        started.append(wires.grad_started(*products))
        products.clear()

    def passed(parts, count):
        for mine, theirs in started[len(ended) : count]:
            if theirs is not None:
                parts, theirs = tie(parts, theirs)
            ended.append(wires.grad_ended(mine, theirs))
        return parts

    above = final_sums
    for layer in reversed(range(layers)):
        layer_in, one, qkv, totals, attended, middle, two, pre_act, hidden = saved[layer]
        vector = norm_vectors[layer]
        out = (out_own, wires.near(out_own))
        grad_pre, up_sums, share, own_share = kernel_call(
            mlp_backward_body,
            [
                ((token_count, units), BF),
                ((1, units), F32),
                ((half, width), BF),
                ((half, width), F32),
            ],
            [*out, columns(layer, 0), columns(layer, 1), pre_act],
        )
        parts = wires.shares(share, own_share)
        products.extend([(*two, grad_pre), (*out, hidden)])
        above_started = len(started)
        if layer == 0:
            start()
        grad_middle, mid_own, middle_sums = norm_backward(
            middle, vector[3], *parts, grad_stream
        )
        mid = (mid_own, wires.near(mid_own))
        grad_qkv, qkv_sums, share, own_share = kernel_call(
            functools.partial(attention_backward_body, heads, HD),
            [
                ((token_count, 3 * part), BF),
                ((1, 3 * part), F32),
                ((half, width), BF),
                ((half, width), F32),
            ],
            [wires.near_ref, *mid, columns(layer, 2), qkv, totals],
            scratch=[
                pltpu.VMEM((token_count, part), BF),
                pltpu.VMEM((half, HD), F32),
                pltpu.VMEM((half, HD), F32),
            ],
        )
        parts = passed(wires.shares(share, own_share), above_started)
        products.extend([(*one, grad_qkv), (*mid, attended)])
        start()
        grad_stream, out_own, in_sums = norm_backward(
            layer_in, vector[0], *parts, grad_middle
        )
        bias_grads.insert(
            0, [qkv_sums[:, :part], qkv_sums[:, 2 * part :], up_sums.reshape(up_blocks, part)]
        )
        vector_grads.insert(
            0, [in_sums[:2], middle_sums[2:3], middle_sums[:2], above[2:3]]
        )
        above = in_sums
    input_grad = wires.natural(grad_stream, wires.near(grad_stream))
    ended.extend(
        wires.grad_ended(*halves, direct=at == layers)
        for at, halves in enumerate(started)
        if at >= len(ended)
    )
    cuts = [units, 2 * units, 2 * units + 3 * part]
    ended = [*ended[: layers - 1], jnp.concatenate(ended[layers - 1 :], axis=1)][::-1]
    up_shards, down_shards, attn_shards, proj_shards = zip(
        *[jnp.split(whole, cuts, axis=1) for whole in ended]
    )

    everyone = wires.dp * wires.mp
    vectors = jnp.concatenate([*sum(vector_grads, []), final_sums[:2]], axis=0).reshape(-1)
    biases = jnp.concatenate(sum(bias_grads, []), axis=0).reshape(wires.dp, 1, -1)
    mine = (jnp.arange(wires.mp, dtype=jnp.int32) == wires.mp_at)[None, :, None]
    biases = jnp.where(mine, biases, 0.0).reshape(everyone, -1)
    vector_cut = vectors.shape[0] // everyone
    small = jnp.concatenate([0.5 * vectors.reshape(everyone, vector_cut), biases], axis=1)
    small = jnp.sum(lax.all_to_all(small, ("dp", "mp"), 0, 0), axis=0)

    col_shard = jnp.stack(
        [
            jnp.concatenate(
                [
                    attn_shards[layer].reshape(shard_rows, 3, part),
                    up_shards[layer].reshape(shard_rows, up_blocks, part),
                ],
                axis=1,
            )
            for layer in range(layers)
        ]
    )
    row_shard = jnp.stack(
        [
            jnp.concatenate(
                [
                    proj_shards[layer].T.reshape(1, part, shard_rows),
                    down_shards[layer].T.reshape(up_blocks, part, shard_rows),
                ],
                axis=0,
            )
            for layer in range(layers)
        ]
    )
    squares = sum(jnp.sum(whole * whole) for whole in ended) + jnp.sum(small * small)
    packet = jnp.concatenate([small, jnp.stack([squares, loss_part])])
    packet = lax.all_to_all(
        jnp.broadcast_to(packet[None], (everyone, packet.shape[0])), ("dp", "mp"), 0, 0
    )
    totals = jnp.sum(packet[:, -2:], axis=0)
    loss_total = totals[1]
    grad_norm = jnp.sqrt(totals[0])
    vectors = packet[:, :vector_cut].reshape(-1)
    vector_count = layers * 6 * width
    vector_sum = vectors[:vector_count].reshape(layers, 6, width)
    final_sum = vectors[vector_count:].reshape(2, width)
    bias_sum = jnp.sum(
        jnp.where(mine, packet[:, vector_cut:-2].reshape(wires.dp, wires.mp, -1), 0.0), axis=1
    ).reshape(column_biases.shape)

    clip = CLIP_LIMIT / jnp.maximum(grad_norm, CLIP_LIMIT)
    column_out = adam_update(
        column_weights, column_first, column_second, column_average, col_shard, clip, 0.1, 0.1
    )
    row_out = adam_update(
        row_weights, row_first, row_second, row_average, row_shard, clip, 0.2, 0.1
    )
    bias_out = adam_update(
        column_biases, bias_first, bias_second, bias_average, bias_sum, clip, 0.1, 0.0
    )
    vector_out = adam_update(
        norm_vectors, vector_first, vector_second, vector_average, vector_sum, clip, 0.5, 0.0
    )
    final_state = adam_update(
        final_norm, final_first, final_second, final_average, final_sum, clip, 0.5, 0.0
    )
    return (
        loss_total,
        grad_norm,
        input_grad,
        *column_out,
        *row_out,
        *bias_out,
        *vector_out,
        *final_state,
    )


def solution(mesh):
    tokens, copied = P("dp", None), P()
    columns, rows, biases = P(None, "dp", None, "mp"), P(None, None, "mp", "dp"), P(None, None, "mp")
    placed = (
        tokens,
        copied,
        tokens,
        P("dp", None, None),
        P(None, "dp"),
        P("dp", "mp"),
        P("mp"),
        P("mp", "dp"),
        copied,
        P("dp", "mp"),
        P("dp", "mp"),
        *[columns] * 4,
        *[rows] * 4,
        *[biases] * 4,
        *[copied] * 8,
    )
    return jax.shard_map(
        local,
        mesh=mesh,
        in_specs=placed,
        out_specs=(
            copied,
            copied,
            tokens,
            *[columns] * 4,
            *[rows] * 4,
            *[biases] * 4,
            *[copied] * 8,
        ),
        check_vma=False,
    )
```

```python
import functools

import jax
import jax.numpy as jnp
from jax import lax
from jax.experimental import pallas as pl
from jax.experimental.pallas import tpu as pltpu
from jax.sharding import PartitionSpec as P

HD = 64
THEADS = 25
THD = 64
SEQ = 512
STEP = 4
MAJOR = 4

EPSILON = 1e-05
GELU_COEFF = 0.7978845608028654
BETA_ONE = 0.9
BETA_TWO = 0.999
ADAM_EPSILON = 1e-08
CLIP_LIMIT = 0.002

BF = jnp.bfloat16
F32 = jnp.float32


def dot(a, b):
    return jnp.dot(a, b, preferred_element_type=F32)


def dot_nt(a, b):
    return lax.dot_general(a, b, (((1,), (1,)), ((), ())), preferred_element_type=F32)


def dot_tn(a, b):
    return lax.dot_general(a, b, (((0,), (0,)), ((), ())), preferred_element_type=F32)


def layer_norm(values, gain, shift):
    centered = values - jnp.mean(values, axis=-1, keepdims=True)
    variance = jnp.mean(centered * centered, axis=-1, keepdims=True)
    return centered * lax.rsqrt(variance + EPSILON) * gain + shift


def gelu_tanh(values):
    return (
        0.5 * values * (1.0 + jnp.tanh(GELU_COEFF * (values + 0.044715 * values * values * values)))
    )


def kernel_call(body, outs, blocks, scratch=(), vmem=24 << 20, flops=10**6):
    specs, operands = [], []
    for entry in blocks:
        if isinstance(entry, tuple):
            array, shape, index = entry
            specs.append(pl.BlockSpec(shape, functools.partial(lambda at, _: at, index)))
            operands.append(array)
        elif entry.ndim == 1:
            specs.append(pl.BlockSpec(memory_space=pltpu.SMEM))
            operands.append(entry)
        else:
            whole = (0,) * entry.ndim
            specs.append(pl.BlockSpec(entry.shape, functools.partial(lambda at, _: at, whole)))
            operands.append(entry)
    return pl.pallas_call(
        body,
        grid=(1,),
        out_shape=[jax.ShapeDtypeStruct(shape, kind) for shape, kind in outs],
        in_specs=specs,
        out_specs=[
            pl.BlockSpec(shape, functools.partial(lambda at, _: at, (0,) * len(shape)))
            for shape, _ in outs
        ],
        scratch_shapes=list(scratch),
        compiler_params=pltpu.CompilerParams(vmem_limit_bytes=vmem),
        cost_estimate=pl.CostEstimate(flops=flops, transcendentals=0, bytes_accessed=10**5),
    )(*operands)


def masked_scores(queries, key_rows, start):
    scores = dot_nt(queries, key_rows) * (queries.shape[1] ** (-0.5))
    query_pos = start + lax.broadcasted_iota(jnp.int32, scores.shape, 0)
    key_pos = lax.broadcasted_iota(jnp.int32, scores.shape, 1)
    return jnp.where(key_pos <= query_pos, scores, -jnp.inf)


def attention_forward_body(
    heads, size, near_ref, kept_ref, own_ref, other_ref, weight_ref, bias_ref,
    share_ref, own_share_ref, out_ref, qkv_ref, total_ref,
):
    half, part = own_ref.shape[0], heads * size
    first = near_ref[0] == 0
    attn = weight_ref[:, : 3 * part]
    own = dot(own_ref[...], attn) + bias_ref[...]
    other = dot(other_ref[...], attn) + bias_ref[...]
    qkv_ref[:half, :] = jnp.where(first, own, other).astype(BF)
    qkv_ref[half:, :] = jnp.where(first, other, own).astype(BF)
    lane = lax.broadcasted_iota(jnp.int32, (half, total_ref.shape[1]), 1)
    for block in range(2):
        rows = slice(block * half, (block + 1) * half)
        seen = (block + 1) * half
        to = pl.multiple_of((near_ref[0] ^ block) * half, half)
        totals = jnp.zeros(lane.shape, F32)
        for head in range(heads):
            q = qkv_ref[rows, head * size : (head + 1) * size]
            k = qkv_ref[:seen, part + head * size : part + (head + 1) * size]
            v = qkv_ref[:seen, 2 * part + head * size : 2 * part + (head + 1) * size]
            scores = masked_scores(q, k, block * half)
            highest = jnp.max(scores, axis=-1, keepdims=True)
            mass = jnp.exp(scores - highest)
            whole = jnp.sum(mass, axis=-1, keepdims=True)
            weights = (mass * (1.0 / whole)).astype(BF)
            result = jnp.where(kept_ref[head] == 1, dot(weights, v), 0.0)
            out_ref[pl.ds(to, half), head * size : (head + 1) * size] = result.astype(BF)
            totals = jnp.where(lane == head, highest + jnp.log(whole), totals)
        total_ref[rows, :] = totals
    proj = weight_ref[:, 3 * part : 4 * part]
    put(share_ref, dot_nt(out_ref[half:, :], proj))
    put(own_share_ref, dot_nt(out_ref[:half, :], proj))


def mlp_forward_body(
    own_ref, other_ref, up_ref, down_ref, bias_ref, pre_ref, hidden_ref, share_ref, own_share_ref
):
    half = own_ref.shape[0]
    for rows, from_ref in ((slice(half, None), other_ref), (slice(0, half), own_ref)):
        pre = dot(from_ref[...], up_ref[...]) + bias_ref[...]
        pre_ref[rows, :] = pre
        hidden = gelu_tanh(pre).astype(BF)
        hidden_ref[rows, :] = hidden
        share = dot_nt(hidden, down_ref[...])
        if from_ref is other_ref:
            share_ref[...] = share.astype(BF)
        else:
            own_share_ref[...] = share


def gelu_slope(values):
    inner = jnp.tanh(GELU_COEFF * (values + 0.044715 * values * values * values))
    slope = GELU_COEFF * (1.0 + 3.0 * 0.044715 * values * values)
    return 0.5 * (1.0 + inner) + 0.5 * values * (1.0 - inner * inner) * slope


def mlp_backward_body(
    own_ref, other_ref, up_ref, down_ref, pre_ref, grad_ref, bias_ref, share_ref, own_share_ref
):
    half = own_ref.shape[0]
    total = jnp.zeros(bias_ref.shape, F32)
    for rows, from_ref in ((slice(half, None), other_ref), (slice(0, half), own_ref)):
        grad = (dot(from_ref[...], down_ref[...]) * gelu_slope(pre_ref[rows, :])).astype(BF)
        grad_ref[rows, :] = grad
        total = total + jnp.sum(grad.astype(F32), axis=0, keepdims=True)
        share = dot_nt(grad, up_ref[...])
        if from_ref is other_ref:
            share_ref[...] = share.astype(BF)
        else:
            own_share_ref[...] = share
    bias_ref[...] = total


def attention_backward_body(
    heads, size, near_ref, own_ref, other_ref, weight_ref, qkv_ref, total_ref,
    grad_ref, bias_ref, share_ref, own_share_ref, grad_out_ref, key_ref, value_ref,
):
    half, part = own_ref.shape[0], heads * size
    scale = size ** (-0.5)
    first = near_ref[0] == 0
    proj = weight_ref[:, 3 * part : 4 * part]
    own = dot(own_ref[...], proj)
    other = dot(other_ref[...], proj)
    grad_out_ref[:half, :] = jnp.where(first, own, other).astype(BF)
    grad_out_ref[half:, :] = jnp.where(first, other, own).astype(BF)
    spots = [pl.multiple_of((near_ref[0] ^ block) * half, half) for block in range(2)]
    for head in range(heads):
        at = [slice(i * part + head * size, i * part + (head + 1) * size) for i in range(3)]
        for block in range(2):
            rows = slice(block * half, (block + 1) * half)
            seen = (block + 1) * half
            q = qkv_ref[rows, at[0]]
            k = qkv_ref[:seen, at[1]]
            v = qkv_ref[:seen, at[2]]
            grad_out = grad_out_ref[rows, at[0]]
            probs = jnp.exp(masked_scores(q, k, block * half) - total_ref[rows, head : head + 1])
            grad_probs = dot_nt(grad_out, v)
            inner = jnp.sum(probs * grad_probs, axis=-1, keepdims=True)
            grad_scores = (probs * (grad_probs - inner) * scale).astype(BF)
            grad_ref[pl.ds(spots[block], half), at[0]] = dot(grad_scores, k).astype(BF)
            grad_k = dot_tn(grad_scores, q)
            grad_v = dot_tn(probs.astype(BF), grad_out)
            if block == 0:
                key_ref[...] = grad_k
                value_ref[...] = grad_v
            else:
                for side in range(2):
                    part_rows = slice(side * half, (side + 1) * half)
                    whole_k, whole_v = grad_k[part_rows], grad_v[part_rows]
                    if side == 0:
                        whole_k = whole_k + key_ref[...]
                        whole_v = whole_v + value_ref[...]
                    grad_ref[pl.ds(spots[side], half), at[1]] = whole_k.astype(BF)
                    grad_ref[pl.ds(spots[side], half), at[2]] = whole_v.astype(BF)
    bias_ref[...] = jnp.sum(grad_ref[...].astype(F32), axis=0, keepdims=True)
    attn = weight_ref[:, : 3 * part]
    share_ref[...] = dot_nt(grad_ref[half:, :], attn).astype(BF)
    own_share_ref[...] = dot_nt(grad_ref[:half, :], attn)


def padded_width(width):
    return -(-width // 128) * 128


def put(out_ref, value):
    width = value.shape[1]
    out_ref[:, :width] = value.astype(out_ref.dtype)
    if out_ref.shape[1] > width:
        out_ref[:, width:] = jnp.zeros((value.shape[0], out_ref.shape[1] - width), out_ref.dtype)


def weave_body(minor_ref, mine_ref, theirs_ref, out_ref):
    first = minor_ref[0] == 0
    out_ref[0, 0] = jnp.where(first, mine_ref[0], theirs_ref[0])
    out_ref[0, 1] = jnp.where(first, theirs_ref[0], mine_ref[0])


def weave_call(minor, mine, theirs, start, rows, moved):
    majors, _, cols = mine.shape
    block = pl.BlockSpec(
        (pl.Element(1), pl.Element(rows), pl.Element(cols)), lambda k: (k, start, 0)
    )
    return pl.pallas_call(
        weave_body,
        grid=(majors,),
        out_shape=jax.ShapeDtypeStruct((majors, 2, rows, cols), mine.dtype),
        in_specs=[pl.BlockSpec(memory_space=pltpu.SMEM), block, block],
        out_specs=pl.BlockSpec((1, 2, rows, cols), lambda k: (k, 0, 0, 0)),
        compiler_params=pltpu.CompilerParams(vmem_limit_bytes=16 << 20),
        cost_estimate=pl.CostEstimate(flops=10**5, transcendentals=0, bytes_accessed=moved),
    )(minor, mine, theirs).reshape(majors * 2 * rows, cols)


def up_body(own_ref, other_ref, weight_ref, bias_ref, out_ref):
    half = own_ref.shape[0]
    depth = weight_ref.shape[0]
    for rows, from_ref in ((slice(half, None), other_ref), (slice(0, half), own_ref)):
        pre = dot(from_ref[:, :depth], weight_ref[...]) + bias_ref[...]
        out_ref[rows, :] = gelu_tanh(pre).astype(BF)


def down_body(hidden_ref, weight_ref, share_ref, own_share_ref):
    half = share_ref.shape[0]
    put(share_ref, dot_nt(hidden_ref[half:, :], weight_ref[...]))
    put(own_share_ref, dot_nt(hidden_ref[:half, :], weight_ref[...]))


def norm_forward_body(stream_ref, pair_ref, far_ref, bias_ref, gain_ref, shift_ref, new_ref, out_ref):
    width = stream_ref.shape[1]
    new = (
        stream_ref[...]
        + (pair_ref[:, :width].astype(F32) + far_ref[:, :width].astype(F32))
        + bias_ref[...]
    )
    new_ref[...] = new
    put(out_ref, layer_norm(new, gain_ref[...], shift_ref[...]))


def norm_backward_body(values_ref, gain_ref, pair_ref, far_ref, *refs):
    *top_ref, new_ref, low_ref, sums_ref = refs
    grad = pair_ref[...].astype(F32) + far_ref[...].astype(F32)
    values = values_ref[...]
    centered = values - jnp.mean(values, axis=-1, keepdims=True)
    variance = jnp.mean(centered * centered, axis=-1, keepdims=True)
    scale = lax.rsqrt(variance + EPSILON)
    unit = centered * scale
    inner = grad * gain_ref[...]
    new = scale * (
        inner
        - jnp.mean(inner, axis=-1, keepdims=True)
        - unit * jnp.mean(inner * unit, axis=-1, keepdims=True)
    )
    if top_ref:
        new = top_ref[0][...] + new
    new_ref[...] = new
    low_ref[...] = new.astype(BF)
    sums_ref[0:1, :] = jnp.sum(grad * unit, axis=0, keepdims=True)
    sums_ref[1:2, :] = jnp.sum(grad, axis=0, keepdims=True)
    sums_ref[2:3, :] = jnp.sum(new, axis=0, keepdims=True)
    sums_ref[3:, :] = jnp.zeros_like(sums_ref[3:, :])


def norm_forward(stream, pair, far, bias, gain, shift):
    return kernel_call(
        norm_forward_body,
        [(stream.shape, F32), (pair.shape, BF)],
        [stream, pair, far, bias[None], gain[None], shift[None]],
        vmem=16 << 20,
    )


def norm_backward(values, gain, pair, far, *top):
    return kernel_call(
        norm_backward_body,
        [(values.shape, F32), (values.shape, BF), ((8, values.shape[1]), F32)],
        [values, gain[None], pair, far, *top],
        vmem=16 << 20,
    )


def weight_grad_body(shape, count, minor_ref, *refs):
    majors, minors, rows = shape
    operands, (mine_ref, theirs_ref, sum_ref) = refs[: 3 * count], refs[3 * count :]
    start = 0
    for at in range(count):
        own, other, grad = operands[3 * at : 3 * at + 3]
        half, cols = own.shape[0], grad.shape[1]
        sum_ref[:, start : start + cols] = dot_tn(own[...], grad[:half, :]) + dot_tn(
            other[...], grad[half:, :]
        )
        start += cols
    for k in range(majors):
        to = slice(k * rows, (k + 1) * rows)
        here = pl.multiple_of((k * minors + minor_ref[0]) * rows, 8)
        there = pl.multiple_of((k * minors + 1 - minor_ref[0]) * rows, 8)
        mine_ref[to, :] = sum_ref[pl.ds(here, rows), :]
        theirs_ref[to, :] = sum_ref[pl.ds(there, rows), :].astype(BF)


STATS = 8


def logits_body(
    place_ref, teacher_ref, student_ref, teacher_head_ref, head_ref, t_ref, z_ref, stats_ref
):
    counted = place_ref[1 + pl.program_id(0)] > place_ref[0]

    @pl.when(counted)
    def _():
        t = dot(teacher_ref[:, : teacher_head_ref.shape[0]], teacher_head_ref[...])
        t_ref[...] = t
        z = dot(student_ref[...], head_ref[...])
        z_ref[...] = z
        t_peak = jnp.max(t, axis=-1, keepdims=True)
        t_exp = jnp.exp(t - t_peak)
        z_peak = jnp.max(z, axis=-1, keepdims=True)
        columns = (
            t_peak,
            jnp.sum(t_exp, axis=-1, keepdims=True),
            jnp.sum(t_exp * (t - z), axis=-1, keepdims=True),
            z_peak,
            jnp.sum(jnp.exp(z - z_peak), axis=-1, keepdims=True),
        )
        lane = lax.broadcasted_iota(jnp.int32, (t.shape[0], 128), 1)
        packed = jnp.zeros(lane.shape, F32)
        for at, column in enumerate(columns):
            packed = jnp.where(lane == at, column, packed)
        stats_ref[...] = packed.T[:STATS, :]

    @pl.when(jnp.logical_not(counted))
    def _():
        row = lax.broadcasted_iota(jnp.int32, stats_ref.shape, 0)
        stats_ref[...] = jnp.where((row == 1) | (row == 4), 1.0, 0.0)


def merge_body(*refs):
    *in_refs, out_ref = refs
    many = [ref[...] for ref in in_refs]
    if many[0].ndim == 3:
        many = [many[0][k] for k in range(many[0].shape[0])]
    t_high = functools.reduce(jnp.maximum, [one[0:1] for one in many])
    z_high = functools.reduce(jnp.maximum, [one[3:4] for one in many])
    t_scale = [jnp.exp(one[0:1] - t_high) for one in many]
    z_scale = [jnp.exp(one[3:4] - z_high) for one in many]
    out_ref[0:1, :] = t_high
    out_ref[1:2, :] = sum(one[1:2] * scale for one, scale in zip(many, t_scale))
    out_ref[2:3, :] = sum(one[2:3] * scale for one, scale in zip(many, t_scale))
    out_ref[3:4, :] = z_high
    out_ref[4:5, :] = sum(one[4:5] * scale for one, scale in zip(many, z_scale))
    out_ref[5:, :] = jnp.zeros_like(out_ref[5:, :])


def logits_back_body(place_ref, weight_ref, t_ref, z_ref, stats_ref, head_ref, *refs):
    out_ref = refs[-1]
    length = place_ref[1 + pl.program_id(0)]

    @pl.when(length > place_ref[0])
    def _():
        stats = stats_ref[...]
        row = lax.broadcasted_iota(jnp.int32, stats.shape, 0)
        logs = jnp.log(jnp.where((row == 1) | (row == 4), stats, 1.0))
        totals = stats + pltpu.roll(logs, STATS - 1, 0)
        totals = jnp.concatenate([totals] * (128 // STATS), axis=0).T
        rows = t_ref.shape[0]
        position = place_ref[0] + lax.broadcasted_iota(jnp.int32, (rows, 1), 0)
        weight = jnp.where(position < length, weight_ref[0], 0.0)
        grad = (jnp.exp(z_ref[...] - totals[:, 3:4]) - jnp.exp(t_ref[...] - totals[:, 0:1])) * weight
        share = dot_nt(grad.astype(BF), head_ref[...])
        if len(refs) == 2:
            share = share + refs[0][...].astype(F32)
        out_ref[...] = share.astype(BF)

    @pl.when(length <= place_ref[0])
    def _():
        out_ref[...] = jnp.zeros_like(out_ref) if len(refs) == 1 else refs[0][...]


def row_blocks(rows, cols):
    return pl.BlockSpec((rows, cols), lambda i: (i, 0))


def held_block(array):
    return pl.BlockSpec(array.shape, lambda i: (0, 0), pipeline_mode=pl.Buffered(1))


def stat_blocks(rows):
    return pl.BlockSpec((STATS, rows), lambda i: (0, i))


SCALAR = pl.BlockSpec(memory_space=pltpu.SMEM)


def logits_call(place, teacher, student, teacher_head, head):
    tokens = teacher.shape[0]
    rows, vocab = tokens // MAJOR, head.shape[1]
    return pl.pallas_call(
        logits_body,
        grid=(MAJOR,),
        out_shape=[
            jax.ShapeDtypeStruct((tokens, vocab), F32),
            jax.ShapeDtypeStruct((tokens, vocab), F32),
            jax.ShapeDtypeStruct((STATS, tokens), F32),
        ],
        in_specs=[
            SCALAR,
            row_blocks(rows, teacher.shape[1]),
            row_blocks(rows, student.shape[1]),
            held_block(teacher_head),
            held_block(head),
        ],
        out_specs=[row_blocks(rows, vocab), row_blocks(rows, vocab), stat_blocks(rows)],
        compiler_params=pltpu.CompilerParams(vmem_limit_bytes=44 << 20),
        cost_estimate=pl.CostEstimate(
            flops=10**6,
            transcendentals=0,
            bytes_accessed=10**5,
        ),
    )(place, teacher, student, teacher_head, head)


def logits_back_call(place, weight, t, z, stats, head, *more):
    tokens, vocab = t.shape
    rows, width = tokens // MAJOR, head.shape[0]
    return pl.pallas_call(
        logits_back_body,
        grid=(MAJOR,),
        out_shape=jax.ShapeDtypeStruct((tokens, width), BF),
        in_specs=[
            SCALAR,
            SCALAR,
            row_blocks(rows, vocab),
            row_blocks(rows, vocab),
            stat_blocks(rows),
            held_block(head),
            *[row_blocks(rows, width) for _ in more],
        ],
        out_specs=row_blocks(rows, width),
        compiler_params=pltpu.CompilerParams(vmem_limit_bytes=40 << 20),
        cost_estimate=pl.CostEstimate(
            flops=10**6,
            transcendentals=0,
            bytes_accessed=10**5,
        ),
    )(place, weight, t, z, stats, head, *more)


def merged(*many):
    return pl.pallas_call(
        merge_body, out_shape=jax.ShapeDtypeStruct(many[0].shape[-2:], F32)
    )(*many)


def adam_update(weight, first, second, average, grad, clip, rate, decay):
    keep = min(0.995, (1.0 + STEP) / (10.0 + STEP))
    grad = grad * clip
    first_new = BETA_ONE * first + (1.0 - BETA_ONE) * grad
    second_new = BETA_TWO * second + (1.0 - BETA_TWO) * grad * grad
    first_hat = first_new / (1.0 - BETA_ONE**STEP)
    second_hat = second_new / (1.0 - BETA_TWO**STEP)
    weight_new = weight - rate * (
        first_hat / (jnp.sqrt(second_hat) + ADAM_EPSILON) + decay * weight
    )
    average_new = keep * average + (1.0 - keep) * weight_new
    return (weight_new, first_new, second_new, average_new)


def tie(first, second):
    return lax.optimization_barrier((first, second))


SCALARS = 6


def pack_body(mp, mp_ref, final_ref, *refs):
    *layer_refs, out_ref, line_ref = refs
    devices, groups = out_ref.shape[0], out_ref.shape[0] // mp
    rows, lines = [], len(layer_refs) // 5
    for at in range(lines):
        middle, inner, above, qkv, up = layer_refs[5 * at : 5 * at + 5]
        rows += [(inner, 0), (inner, 1), (middle, 2), (middle, 0), (middle, 1), (above, 2)]
        part = qkv.shape[1] // 3
        line_ref[at : at + 1, :part] = qkv[:, :part]
        line_ref[at : at + 1, part : 2 * part] = qkv[:, 2 * part :]
        line_ref[at : at + 1, 2 * part :] = up[...]
    rows += [(final_ref, 0), (final_ref, 1)]
    out_ref[...] = jnp.zeros_like(out_ref)
    blocks = final_ref.shape[1] // 128
    each = -(-len(rows) * blocks // devices)
    for at, (ref, row) in enumerate(rows):
        for block in range(blocks):
            to = at * blocks + block
            out_ref[to // each, to % each : to % each + 1, :] = (
                0.5 * ref[row : row + 1, 128 * block : 128 * (block + 1)]
            )
    blocks = line_ref.shape[1] // 128
    own_each = -(-lines * blocks // groups)
    for at in range(lines * blocks):
        line, block = divmod(at, blocks)
        value = line_ref[line : line + 1, 128 * block : 128 * (block + 1)]
        row = each + at % own_each
        for m in range(mp):
            out_ref[at // own_each * mp + m, row : row + 1, :] = jnp.where(
                mp_ref[0] == m, value, 0.0
            )


def square_body(loss_ref, packets_ref, *refs):
    *grad_refs, out_ref = refs
    devices = packets_ref.shape[0]
    total = packets_ref[0]
    for at in range(1, devices):
        total = total + packets_ref[at]
    squares = jnp.sum(total * total)
    for ref in grad_refs:
        grad = ref[...].astype(F32)
        squares = squares + jnp.sum(grad * grad)
    row = lax.broadcasted_iota(jnp.int32, total.shape, 0)
    lane = lax.broadcasted_iota(jnp.int32, total.shape, 1)
    total = jnp.where((row == SCALARS) & (lane == 0), squares, total)
    total = jnp.where((row == SCALARS) & (lane == 1), loss_ref[0], total)
    for at in range(devices):
        out_ref[at] = total


def scalar_body(packets_ref, scalar_ref):
    devices = packets_ref.shape[0]
    sums = packets_ref[0, SCALARS : SCALARS + 1, :]
    for at in range(1, devices):
        sums = sums + packets_ref[at, SCALARS : SCALARS + 1, :]
    norm = jnp.sqrt(sums[:, 0:1])
    clip = CLIP_LIMIT / jnp.maximum(norm, CLIP_LIMIT)
    row = lax.broadcasted_iota(jnp.int32, scalar_ref.shape, 0)
    scalar_ref[...] = jnp.where(row == 0, clip, jnp.where(row == 1, norm, sums[:, 1:2]))


def small_update_body(mp, mp_ref, packets_ref, scalar_ref, *refs):
    states, outs = refs[:12], refs[12:24]
    line_ref, grad_ref = refs[24:]
    devices, groups = packets_ref.shape[0], packets_ref.shape[0] // mp
    clip = scalar_ref[0:1, 0:1]
    layers, kinds, width = states[0].shape
    blocks = width // 128
    each = -(-(layers * kinds + 2) * blocks // devices)
    for at in range(layers * kinds + 2):
        for block in range(blocks):
            source = at * blocks + block
            grad_ref[at : at + 1, 128 * block : 128 * (block + 1)] = packets_ref[
                source // each, source % each : source % each + 1, :
            ]

    def update(kind, pick, grad, rate):
        values = [ref[pick] for ref in states[4 * kind : 4 * kind + 4]]
        for ref, value in zip(
            outs[4 * kind : 4 * kind + 4], adam_update(*values, grad, clip, rate, 0.0)
        ):
            ref[pick] = value

    for layer in range(layers):
        update(0, layer, grad_ref[layer * kinds : (layer + 1) * kinds, :], 0.5)
    update(1, slice(None), grad_ref[layers * kinds : layers * kinds + 2, :], 0.5)
    part = states[8].shape[2]
    blocks = line_ref.shape[1] // 128
    own_each = -(-layers * blocks // groups)
    for at in range(layers * blocks):
        line, block = divmod(at, blocks)
        source = at // own_each * mp + mp_ref[0]
        from_row = each + at % own_each
        line_ref[line : line + 1, 128 * block : 128 * (block + 1)] = packets_ref[
            pl.ds(source, 1), from_row : from_row + 1, :
        ].reshape(1, 128)
    for layer in range(layers):
        grad = jnp.concatenate(
            [
                line_ref[layer : layer + 1, part * at : part * (at + 1)]
                for at in range(states[8].shape[1])
            ],
            axis=0,
        )
        update(2, layer, grad, 0.1)


class Wires:
    def __init__(self):
        self.dp = lax.axis_size("dp")
        self.mp = lax.axis_size("mp")
        self.minors = self.dp // MAJOR
        self.dp_at = lax.axis_index("dp")
        self.mp_at = lax.axis_index("mp")
        self.major = self.dp_at // self.minors
        self.minor = self.dp_at % self.minors
        self.near_at = self.mp_at % 2
        self.near_ref = self.near_at.reshape(1).astype(jnp.int32)
        self.minor_ref = self.minor.reshape(1).astype(jnp.int32)
        self.near_pairs = [(i, i ^ 1) for i in range(self.mp)]
        self.far_pairs = [(i, i ^ 2) for i in range(self.mp)]
        self.over_major = [
            [k * self.minors + j for k in range(MAJOR)] for j in range(self.minors)
        ]
        self.over_minor = [
            [k * self.minors + j for j in range(self.minors)] for k in range(MAJOR)
        ]

    def near(self, part):
        return lax.ppermute(part, "mp", self.near_pairs)

    def far(self, part):
        return lax.ppermute(part, "mp", self.far_pairs)

    def natural(self, own, other):
        first = self.near_at == 0
        return jnp.concatenate([jnp.where(first, own, other), jnp.where(first, other, own)], axis=0)

    def own_first(self, whole):
        half = whole.shape[0] // 2
        own = lax.dynamic_slice_in_dim(whole, self.near_at * half, half, 0)
        other = lax.dynamic_slice_in_dim(whole, (1 - self.near_at) * half, half, 0)
        return own, other

    def shares(self, other, own):
        pair = (own + self.near(other.astype(BF)).astype(F32)).astype(BF)
        return pair, self.far(pair)

    def minor_parts(self, part):
        if self.minors == 2:
            return lax.ppermute(part, "dp", [(i, i ^ 1) for i in range(self.dp)])
        return lax.all_gather(part, "dp", axis=0, axis_index_groups=self.over_minor)

    def minor_stack(self, part, others, axis):
        if self.minors == 2:
            first = self.minor == 0
            return jnp.stack(
                [jnp.where(first, part, others), jnp.where(first, others, part)], axis=axis
            )
        return jnp.moveaxis(others, 0, axis)

    def major_gather(self, part):
        return lax.all_gather(
            part, "dp", axis=0, tiled=True, axis_index_groups=self.over_major
        )

    def minor_joined(self, part):
        return self.minor_stack(part, self.minor_parts(part), 0).reshape(-1, part.shape[-1])

    def minor_woven(self, part, others, start=0, rows=None, moved=10**5):
        rows = part.shape[1] if rows is None else rows
        if self.minors == 2:
            return weave_call(self.minor_ref, part, others, start, rows, moved)
        stacked = self.minor_stack(part, others, 1)[:, :, start : start + rows]
        return stacked.reshape(-1, part.shape[-1])

    def major_swap(self, part):
        return lax.all_to_all(part, "dp", 0, 0, axis_index_groups=self.over_major)

    def grad_started(self, *products):
        width, cols = products[0][0].shape[1], sum(grad.shape[1] for _, _, grad in products)
        rows = width // self.dp
        if self.minors == 2 and rows % 8 == 0:
            mine, theirs = kernel_call(
                functools.partial(
                    weight_grad_body, (MAJOR, self.minors, rows), len(products)
                ),
                [((MAJOR * rows, cols), F32), ((MAJOR * rows, cols), BF)],
                [self.minor_ref, *sum(([*product] for product in products), [])],
                scratch=[pltpu.VMEM((width, cols), F32)],
                vmem=40 << 20,
                flops=2 * 2 * products[0][0].shape[0] * width * cols,
            )
            return mine, self.minor_parts(theirs)
        total = jnp.concatenate(
            [dot_tn(jnp.concatenate(product[:2]), product[2]) for product in products], axis=1
        )
        held = lax.psum_scatter(
            total.reshape(MAJOR, self.minors, rows, cols).astype(BF),
            "dp",
            scatter_dimension=1,
            axis_index_groups=self.over_minor,
        )
        return held.reshape(-1, cols).astype(F32), None

    def grad_ended(self, mine, theirs, direct=False):
        held = (mine if theirs is None else mine + theirs.astype(F32)).astype(BF)
        if direct:
            held = self.major_swap(held.reshape(MAJOR, -1, held.shape[-1]))
            return jnp.sum(held.astype(F32), axis=0)
        return lax.psum_scatter(
            held, "dp", scatter_dimension=0, tiled=True, axis_index_groups=self.over_major
        )


def local(
    inputs,
    lengths,
    teacher_inputs,
    teacher_qkv,
    teacher_proj,
    teacher_up,
    teacher_up_bias,
    teacher_down,
    teacher_vectors,
    teacher_head,
    head,
    column_weights,
    column_first,
    column_second,
    column_average,
    row_weights,
    row_first,
    row_second,
    row_average,
    column_biases,
    bias_first,
    bias_second,
    bias_average,
    norm_vectors,
    vector_first,
    vector_second,
    vector_average,
    final_norm,
    final_first,
    final_second,
    final_average,
):
    wires = Wires()
    token_count, width = inputs.shape
    half = token_count // 2
    teacher_width = teacher_inputs.shape[1]
    layers, shard_rows, col_blocks, part = column_weights.shape
    up_blocks = col_blocks - 3
    units = up_blocks * part

    slots = -(-THEADS // wires.mp)
    base_heads = THEADS // wires.mp
    extra_heads = THEADS % wires.mp
    own_start = wires.mp_at * base_heads + jnp.minimum(wires.mp_at, extra_heads)
    own_stop = own_start + base_heads + jnp.where(wires.mp_at < extra_heads, 1, 0)
    slot_start = jnp.minimum(own_start, THEADS - slots)
    head_ids = slot_start + jnp.arange(slots, dtype=jnp.int32)
    owned = ((head_ids >= own_start) & (head_ids < own_stop)).astype(jnp.int32)
    slot_width = slots * THD
    first_col = slot_start * THD

    qkv_shard = lax.dynamic_slice_in_dim(teacher_qkv, first_col, slot_width, 2)
    proj_shard = lax.dynamic_slice_in_dim(teacher_proj, first_col, slot_width, 0).T
    shards = []
    for layer in range(layers):
        cols = column_weights[layer].astype(BF)
        rows = row_weights[layer].astype(BF)
        shards.append(
            jnp.concatenate(
                [
                    cols[:, 3:].reshape(shard_rows, units),
                    rows[1:].reshape(units, shard_rows).T,
                    cols[:, :3].reshape(shard_rows, 3 * part),
                    rows[0].T,
                ],
                axis=1,
            )
        )
    shards.extend(
        [
            jnp.concatenate([qkv_shard.reshape(-1, 3 * slot_width), proj_shard], axis=1),
            teacher_up,
            teacher_down.T,
        ]
    )
    own_at = wires.near_at * half
    tv = teacher_vectors
    teacher_pad = padded_width(teacher_width)
    teacher_stream, teacher_other = (
        lax.dynamic_slice_in_dim(teacher_inputs, at, half, 0).astype(F32)
        for at in (own_at, half - own_at)
    )
    query_bias, value_bias = (
        lax.dynamic_slice_in_dim(tv[at], first_col, slot_width) for at in (2, 3)
    )
    teacher_start = (
        layer_norm(teacher_stream, tv[0], tv[1]).astype(BF),
        layer_norm(teacher_other, tv[0], tv[1]).astype(BF),
        jnp.concatenate([query_bias, jnp.zeros_like(query_bias), value_bias])[None],
    )

    held, rows, others = [], [], []

    def launch(mark):
        shard = shards[len(held)]
        if mark is not None:
            shard, mark = tie(shard, mark)
        if held:
            shard, rows[-1] = tie(shard, held[-1])
        held.append(wires.major_gather(shard).reshape(MAJOR, *shard.shape))
        rows.append(held[-1])
        others.append(wires.minor_parts(held[-1]))
        return mark

    for _ in range(layers):
        launch(None)
    vocab_part = head.shape[1] // MAJOR
    cut = teacher_head.shape[0]
    both = jnp.stack(
        [
            jnp.concatenate(
                [rows_[:, k * vocab_part : (k + 1) * vocab_part] for rows_ in (teacher_head, head)],
                axis=0,
            )
            for k in range(MAJOR)
        ]
    )

    stream = lax.dynamic_slice_in_dim(inputs, own_at, half, 0).astype(F32)
    heads = part // HD
    all_heads = jnp.ones((heads,), jnp.int32)

    layer_full = []

    def columns(layer, at):
        return (layer_full[layer], (width, units), (0, at))

    saved = []
    one_own = layer_norm(stream, norm_vectors[0, 0], norm_vectors[0, 1]).astype(BF)
    one_own, (teacher_stream, teacher_start, both, *shards[layers:]) = tie(
        one_own, (teacher_stream, teacher_start, both, *shards[layers:])
    )
    for layer in range(layers):
        vector = norm_vectors[layer]
        layer_full.append(wires.minor_woven(rows[layer], others[layer]))
        if layer == 0:
            layer_full[0] = launch(layer_full[0])
        one = (one_own, wires.near(one_own))
        bias = column_biases[layer]
        share, own_share, attended, qkv, totals = kernel_call(
            functools.partial(attention_forward_body, heads, HD),
            [
                ((half, width), BF),
                ((half, width), F32),
                ((token_count, part), BF),
                ((token_count, 3 * part), BF),
                ((token_count, 128), F32),
            ],
            [
                wires.near_ref,
                all_heads,
                *one,
                columns(layer, 2),
                jnp.concatenate([bias[0], jnp.zeros_like(bias[0]), bias[1]])[None],
            ],
        )
        middle, two_own = norm_forward(
            stream, *wires.shares(share, own_share), vector[2], vector[3], vector[4]
        )
        two = (two_own, wires.near(two_own))
        pre_act, hidden, share, own_share = kernel_call(
            mlp_forward_body,
            [
                ((token_count, units), F32),
                ((token_count, units), BF),
                ((half, width), BF),
                ((half, width), F32),
            ],
            [*two, columns(layer, 0), columns(layer, 1), bias[2:].reshape(1, units)],
        )
        saved.append((stream, one, qkv, totals, attended, middle, two, pre_act, hidden))
        later = norm_vectors[layer + 1] if layer + 1 < layers else final_norm
        parts, others[layer + 1] = tie(wires.shares(share, own_share), others[layer + 1])
        stream, one_own = norm_forward(middle, *parts, vector[5], later[0], later[1])
        if len(held) < len(shards):
            one_own = launch(one_own)
    final_out = one_own
    while len(held) < len(shards):
        launch(None)
    (mine, theirs), rows[-2] = tie((rows[-3], others[-3]), rows[-2])
    teacher_attn = wires.minor_woven(mine, theirs)
    teacher_share, teacher_own_share = kernel_call(
        functools.partial(attention_forward_body, slots, THD),
        [((half, teacher_pad), BF), ((half, teacher_pad), F32)],
        [
            wires.near_ref,
            owned,
            *teacher_start[:2],
            teacher_attn,
            teacher_start[2],
        ],
        scratch=[
            pltpu.VMEM((token_count, slot_width), BF),
            pltpu.VMEM((token_count, 3 * slot_width), BF),
            pltpu.VMEM((token_count, 128), F32),
        ],
        vmem=36 << 20,
    )
    parts, others[-2] = tie(wires.shares(teacher_share, teacher_own_share), others[-2])
    both, others[-2] = tie(both, others[-2])
    both, rows[-1] = tie(both, rows[-1])
    both = wires.major_swap(both)
    both_others = wires.minor_parts(both)
    final_out, rows[-1] = tie(final_out, rows[-1])
    student_rows = wires.major_gather(final_out)
    teacher_up_full = wires.minor_woven(rows[-2], others[-2])
    teacher_mid, normed_own = norm_forward(teacher_stream, *parts, tv[4], tv[5], tv[6])
    (hidden,) = kernel_call(
        up_body,
        [((token_count, teacher_up.shape[1]), BF)],
        [normed_own, wires.near(normed_own), teacher_up_full, teacher_up_bias[None]],
        vmem=32 << 20,
    )
    share, own_share = kernel_call(
        down_body,
        [((half, teacher_pad), BF), ((half, teacher_pad), F32)],
        [hidden, wires.minor_woven(rows[-1], others[-1])],
        vmem=32 << 20,
    )
    _, teacher_final = norm_forward(
        teacher_mid, *wires.shares(share, own_share), tv[7], tv[8], tv[9]
    )
    teacher_final, student_rows = tie(teacher_final, student_rows)
    teacher_rows, both_others = tie(wires.major_gather(teacher_final), both_others)
    teacher_head_part = wires.minor_woven(both, both_others, 0, cut)
    head_part = wires.minor_woven(both, both_others, cut, head.shape[0])

    teacher_sides = (teacher_rows, wires.near(teacher_rows))
    student_sides = (student_rows, wires.near(student_rows))
    row_ids = jnp.arange(MAJOR, dtype=jnp.int32) * wires.minors + wires.minor
    row_lengths = jnp.sum(
        jnp.where(
            row_ids[:, None] == jnp.arange(lengths.shape[0], dtype=jnp.int32)[None, :],
            lengths[None, :],
            0,
        ),
        axis=1,
    )
    places = [
        jnp.concatenate([start.reshape(1).astype(jnp.int32), row_lengths])
        for start in (own_at, half - own_at)
    ]
    row_weight = 1.0 / jnp.sum(lengths).astype(F32)
    sides = [
        logits_call(place, teacher, student, teacher_head_part, head_part)
        for place, teacher, student in zip(places, teacher_sides, student_sides)
    ]
    stats = merged(sides[0][2], wires.near(sides[1][2]))
    stats = merged(stats, wires.far(stats))
    stats = merged(
        wires.major_swap(jnp.broadcast_to(stats[None], (MAJOR, *stats.shape)))
    )
    other_stats = wires.near(stats)
    divergence = (
        stats[2] / stats[1] - (stats[0] + jnp.log(stats[1])) + (stats[3] + jnp.log(stats[4]))
    ).reshape(MAJOR, half)
    counted = own_at + jnp.arange(half, dtype=jnp.int32)[None, :] < row_lengths[:, None]
    loss_part = jnp.sum(jnp.where(counted, divergence, 0.0)) * (
        row_weight * (2.0 / (MAJOR * wires.mp))
    )

    weight = row_weight.reshape(1)
    share = logits_back_call(places[1], weight, *sides[1][:2], other_stats, head_part)
    share = logits_back_call(
        places[0], weight, *sides[0][:2], stats, head_part, wires.near(share)
    )
    share = wires.major_swap(share.reshape(MAJOR, half, width))
    share = jnp.sum(share.astype(F32), axis=0).astype(BF)
    grad_stream, out_own, final_sums = norm_backward(
        stream, final_norm[0], share, wires.far(share)
    )
    small_sums = []
    products, started, ended = [], [], []

    def start(parts):
        mine, theirs = wires.grad_started(*products)
        parts, mine = tie(parts, mine)
        started.append((mine, theirs))
        products.clear()
        return parts

    def passed(parts, count):
        for mine, theirs in started[len(ended) : count]:
            if theirs is not None:
                parts, theirs = tie(parts, theirs)
            if ended:
                mine, ended[-1] = tie(mine, ended[-1])
            ended.append(wires.grad_ended(mine, theirs))
        return parts

    above = final_sums
    for layer in reversed(range(layers)):
        layer_in, one, qkv, totals, attended, middle, two, pre_act, hidden = saved[layer]
        vector = norm_vectors[layer]
        out = (out_own, wires.near(out_own))
        grad_pre, up_sums, share, own_share = kernel_call(
            mlp_backward_body,
            [
                ((token_count, units), BF),
                ((1, units), F32),
                ((half, width), BF),
                ((half, width), F32),
            ],
            [*out, columns(layer, 0), columns(layer, 1), pre_act],
        )
        share = passed(share, 2 * (layers - 1 - layer) - 1)
        parts = wires.shares(share, own_share)
        products.extend([(*two, grad_pre), (*out, hidden)])
        parts = start(parts)
        grad_middle, mid_own, middle_sums = norm_backward(
            middle, vector[3], *parts, grad_stream
        )
        mid = (mid_own, wires.near(mid_own))
        grad_qkv, qkv_sums, share, own_share = kernel_call(
            functools.partial(attention_backward_body, heads, HD),
            [
                ((token_count, 3 * part), BF),
                ((1, 3 * part), F32),
                ((half, width), BF),
                ((half, width), F32),
            ],
            [wires.near_ref, *mid, columns(layer, 2), qkv, totals],
            scratch=[
                pltpu.VMEM((token_count, part), BF),
                pltpu.VMEM((half, HD), F32),
                pltpu.VMEM((half, HD), F32),
            ],
        )
        share = passed(share, 2 * (layers - 1 - layer))
        parts = wires.shares(share, own_share)
        products.extend([(*one, grad_qkv), (*mid, attended)])
        parts = start(parts)
        grad_stream, out_own, in_sums = norm_backward(
            layer_in, vector[0], *parts, grad_middle
        )
        small_sums.insert(0, [middle_sums, in_sums, above, qkv_sums, up_sums])
        above = in_sums
    input_grad = wires.natural(grad_stream, wires.near(grad_stream))
    everyone = wires.dp * wires.mp
    mp_ref = wires.mp_at.reshape(1).astype(jnp.int32)
    packet = (everyone, 8, 128)
    (packets,) = kernel_call(
        functools.partial(pack_body, wires.mp),
        [(packet, F32)],
        [mp_ref, final_sums, *sum(small_sums, [])],
        scratch=[pltpu.VMEM((layers, (2 + up_blocks) * part), F32)],
        vmem=8 << 20,
    )
    packets = lax.all_to_all(packets, ("dp", "mp"), 0, 0)
    for at in range(len(ended), len(started)):
        mine, theirs = started[at]
        if at == 2 * layers - 2:
            mine, ended[-1] = tie(mine, ended[-1])
            mine, packets = tie(mine, packets)
        ended.append(wires.grad_ended(mine, theirs, direct=at >= 2 * layers - 2))
    squared = ended
    cuts = [units, 2 * units, 2 * units + 3 * part]
    ended = [part_grad.astype(F32) for part_grad in ended]
    ended = [jnp.concatenate(pair, axis=1) for pair in zip(ended[0::2], ended[1::2])][::-1]
    up_shards, down_shards, attn_shards, proj_shards = zip(
        *[jnp.split(whole, cuts, axis=1) for whole in ended]
    )

    (packets,) = kernel_call(
        square_body, [(packet, F32)], [loss_part.reshape(1), packets, *squared], vmem=16 << 20
    )
    packets = lax.all_to_all(packets, ("dp", "mp"), 0, 0)
    states = (
        *(norm_vectors, vector_first, vector_second, vector_average),
        *(final_norm, final_first, final_second, final_average),
        *(column_biases, bias_first, bias_second, bias_average),
    )
    (scalars,) = kernel_call(scalar_body, [((8, 128), F32)], [packets], vmem=8 << 20)
    small_out = kernel_call(
        functools.partial(small_update_body, wires.mp),
        [(state.shape, F32) for state in states],
        [mp_ref, packets, scalars, *states],
        scratch=[
            pltpu.VMEM((layers, (2 + up_blocks) * part), F32),
            pltpu.VMEM((layers * 6 + 2, width), F32),
        ],
        vmem=16 << 20,
    )
    clip, grad_norm, loss_total = scalars[0, 0], scalars[1, 0], scalars[2, 0]

    col_shard = jnp.stack(
        [
            jnp.concatenate(
                [
                    attn_shards[layer].reshape(shard_rows, 3, part),
                    up_shards[layer].reshape(shard_rows, up_blocks, part),
                ],
                axis=1,
            )
            for layer in range(layers)
        ]
    )
    row_shard = jnp.stack(
        [
            jnp.concatenate(
                [
                    proj_shards[layer].T.reshape(1, part, shard_rows),
                    down_shards[layer].T.reshape(up_blocks, part, shard_rows),
                ],
                axis=0,
            )
            for layer in range(layers)
        ]
    )
    column_out = adam_update(
        column_weights, column_first, column_second, column_average, col_shard, clip, 0.1, 0.1
    )
    row_out = adam_update(
        row_weights, row_first, row_second, row_average, row_shard, clip, 0.2, 0.1
    )
    return (
        loss_total,
        grad_norm,
        input_grad,
        *column_out,
        *row_out,
        *small_out[8:],
        *small_out[:8],
    )


def solution(mesh):
    tokens, copied = P("dp", None), P()
    columns, rows, biases = P(None, "dp", None, "mp"), P(None, None, "mp", "dp"), P(None, None, "mp")
    placed = (
        tokens,
        copied,
        tokens,
        P("dp", None, None),
        P(None, "dp"),
        P("dp", "mp"),
        P("mp"),
        P("mp", "dp"),
        copied,
        P("dp", "mp"),
        P("dp", "mp"),
        *[columns] * 4,
        *[rows] * 4,
        *[biases] * 4,
        *[copied] * 8,
    )
    return jax.shard_map(
        local,
        mesh=mesh,
        in_specs=placed,
        out_specs=(
            copied,
            copied,
            tokens,
            *[columns] * 4,
            *[rows] * 4,
            *[biases] * 4,
            *[copied] * 8,
        ),
        check_vma=False,
    )
```

```python
import functools

import jax
import jax.numpy as jnp
from jax import lax
from jax.experimental import pallas as pl
from jax.experimental.pallas import tpu as pltpu
from jax.sharding import PartitionSpec as P

HD = 64
THEADS = 25
THD = 64
SEQ = 512
STEP = 4
MAJOR = 4

EPSILON = 1e-05
GELU_COEFF = 0.7978845608028654
BETA_ONE = 0.9
BETA_TWO = 0.999
ADAM_EPSILON = 1e-08
CLIP_LIMIT = 0.002

BF = jnp.bfloat16
F32 = jnp.float32


def dot(a, b):
    return jnp.dot(a, b, preferred_element_type=F32)


def dot_nt(a, b):
    return lax.dot_general(a, b, (((1,), (1,)), ((), ())), preferred_element_type=F32)


def dot_tn(a, b):
    return lax.dot_general(a, b, (((0,), (0,)), ((), ())), preferred_element_type=F32)


def layer_norm(values, gain, shift):
    centered = values - jnp.mean(values, axis=-1, keepdims=True)
    variance = jnp.mean(centered * centered, axis=-1, keepdims=True)
    return centered * lax.rsqrt(variance + EPSILON) * gain + shift


def gelu_tanh(values):
    return (
        0.5 * values * (1.0 + jnp.tanh(GELU_COEFF * (values + 0.044715 * values * values * values)))
    )


def kernel_call(body, outs, blocks, scratch=(), vmem=24 << 20, flops=10**6):
    specs, operands = [], []
    for entry in blocks:
        if isinstance(entry, tuple):
            array, shape, index = entry
            specs.append(pl.BlockSpec(shape, functools.partial(lambda at, _: at, index)))
            operands.append(array)
        elif entry.ndim == 1:
            specs.append(pl.BlockSpec(memory_space=pltpu.SMEM))
            operands.append(entry)
        else:
            whole = (0,) * entry.ndim
            specs.append(pl.BlockSpec(entry.shape, functools.partial(lambda at, _: at, whole)))
            operands.append(entry)
    return pl.pallas_call(
        body,
        grid=(1,),
        out_shape=[jax.ShapeDtypeStruct(shape, kind) for shape, kind in outs],
        in_specs=specs,
        out_specs=[
            pl.BlockSpec(shape, functools.partial(lambda at, _: at, (0,) * len(shape)))
            for shape, _ in outs
        ],
        scratch_shapes=list(scratch),
        compiler_params=pltpu.CompilerParams(vmem_limit_bytes=vmem),
        cost_estimate=pl.CostEstimate(flops=flops, transcendentals=0, bytes_accessed=10**5),
    )(*operands)


def masked_scores(queries, key_rows, start):
    scores = dot_nt(queries, key_rows) * (queries.shape[1] ** (-0.5))
    query_pos = start + lax.broadcasted_iota(jnp.int32, scores.shape, 0)
    key_pos = lax.broadcasted_iota(jnp.int32, scores.shape, 1)
    return jnp.where(key_pos <= query_pos, scores, -jnp.inf)


def attention_forward_body(
    heads, size, near_ref, kept_ref, own_ref, other_ref, weight_ref, bias_ref,
    share_ref, own_share_ref, out_ref, qkv_ref, total_ref,
):
    half, part = own_ref.shape[0], heads * size
    first = near_ref[0] == 0
    attn = weight_ref[:, : 3 * part]
    own = dot(own_ref[...], attn) + bias_ref[...]
    other = dot(other_ref[...], attn) + bias_ref[...]
    qkv_ref[:half, :] = jnp.where(first, own, other).astype(BF)
    qkv_ref[half:, :] = jnp.where(first, other, own).astype(BF)
    lane = lax.broadcasted_iota(jnp.int32, (half, total_ref.shape[1]), 1)
    for block in range(2):
        rows = slice(block * half, (block + 1) * half)
        seen = (block + 1) * half
        to = pl.multiple_of((near_ref[0] ^ block) * half, half)
        totals = jnp.zeros(lane.shape, F32)
        for head in range(heads):
            q = qkv_ref[rows, head * size : (head + 1) * size]
            k = qkv_ref[:seen, part + head * size : part + (head + 1) * size]
            v = qkv_ref[:seen, 2 * part + head * size : 2 * part + (head + 1) * size]
            scores = masked_scores(q, k, block * half)
            highest = jnp.max(scores, axis=-1, keepdims=True)
            mass = jnp.exp(scores - highest)
            whole = jnp.sum(mass, axis=-1, keepdims=True)
            weights = (mass * (1.0 / whole)).astype(BF)
            result = jnp.where(kept_ref[head] == 1, dot(weights, v), 0.0)
            out_ref[pl.ds(to, half), head * size : (head + 1) * size] = result.astype(BF)
            totals = jnp.where(lane == head, highest + jnp.log(whole), totals)
        total_ref[rows, :] = totals
    proj = weight_ref[:, 3 * part : 4 * part]
    put(share_ref, dot_nt(out_ref[half:, :], proj))
    put(own_share_ref, dot_nt(out_ref[:half, :], proj))


def mlp_forward_body(
    own_ref, other_ref, up_ref, down_ref, bias_ref, pre_ref, hidden_ref, share_ref, own_share_ref
):
    half = own_ref.shape[0]
    for rows, from_ref in ((slice(half, None), other_ref), (slice(0, half), own_ref)):
        pre = dot(from_ref[...], up_ref[...]) + bias_ref[...]
        pre_ref[rows, :] = pre
        hidden = gelu_tanh(pre).astype(BF)
        hidden_ref[rows, :] = hidden
        share = dot_nt(hidden, down_ref[...])
        if from_ref is other_ref:
            share_ref[...] = share.astype(BF)
        else:
            own_share_ref[...] = share


def gelu_slope(values):
    inner = jnp.tanh(GELU_COEFF * (values + 0.044715 * values * values * values))
    slope = GELU_COEFF * (1.0 + 3.0 * 0.044715 * values * values)
    return 0.5 * (1.0 + inner) + 0.5 * values * (1.0 - inner * inner) * slope


def mlp_backward_body(
    own_ref, other_ref, up_ref, down_ref, pre_ref, grad_ref, bias_ref, share_ref, own_share_ref
):
    half = own_ref.shape[0]
    total = jnp.zeros(bias_ref.shape, F32)
    for rows, from_ref in ((slice(half, None), other_ref), (slice(0, half), own_ref)):
        grad = (dot(from_ref[...], down_ref[...]) * gelu_slope(pre_ref[rows, :])).astype(BF)
        grad_ref[rows, :] = grad
        total = total + jnp.sum(grad.astype(F32), axis=0, keepdims=True)
        share = dot_nt(grad, up_ref[...])
        if from_ref is other_ref:
            share_ref[...] = share.astype(BF)
        else:
            own_share_ref[...] = share
    bias_ref[...] = total


def attention_backward_body(
    heads, size, near_ref, own_ref, other_ref, weight_ref, qkv_ref, total_ref,
    grad_ref, bias_ref, share_ref, own_share_ref, grad_out_ref, key_ref, value_ref,
):
    half, part = own_ref.shape[0], heads * size
    scale = size ** (-0.5)
    first = near_ref[0] == 0
    proj = weight_ref[:, 3 * part : 4 * part]
    own = dot(own_ref[...], proj)
    other = dot(other_ref[...], proj)
    grad_out_ref[:half, :] = jnp.where(first, own, other).astype(BF)
    grad_out_ref[half:, :] = jnp.where(first, other, own).astype(BF)
    spots = [pl.multiple_of((near_ref[0] ^ block) * half, half) for block in range(2)]
    for head in range(heads):
        at = [slice(i * part + head * size, i * part + (head + 1) * size) for i in range(3)]
        for block in range(2):
            rows = slice(block * half, (block + 1) * half)
            seen = (block + 1) * half
            q = qkv_ref[rows, at[0]]
            k = qkv_ref[:seen, at[1]]
            v = qkv_ref[:seen, at[2]]
            grad_out = grad_out_ref[rows, at[0]]
            probs = jnp.exp(masked_scores(q, k, block * half) - total_ref[rows, head : head + 1])
            grad_probs = dot_nt(grad_out, v)
            inner = jnp.sum(probs * grad_probs, axis=-1, keepdims=True)
            grad_scores = (probs * (grad_probs - inner) * scale).astype(BF)
            grad_ref[pl.ds(spots[block], half), at[0]] = dot(grad_scores, k).astype(BF)
            grad_k = dot_tn(grad_scores, q)
            grad_v = dot_tn(probs.astype(BF), grad_out)
            if block == 0:
                key_ref[...] = grad_k
                value_ref[...] = grad_v
            else:
                for side in range(2):
                    part_rows = slice(side * half, (side + 1) * half)
                    whole_k, whole_v = grad_k[part_rows], grad_v[part_rows]
                    if side == 0:
                        whole_k = whole_k + key_ref[...]
                        whole_v = whole_v + value_ref[...]
                    grad_ref[pl.ds(spots[side], half), at[1]] = whole_k.astype(BF)
                    grad_ref[pl.ds(spots[side], half), at[2]] = whole_v.astype(BF)
    bias_ref[...] = jnp.sum(grad_ref[...].astype(F32), axis=0, keepdims=True)
    attn = weight_ref[:, : 3 * part]
    share_ref[...] = dot_nt(grad_ref[half:, :], attn).astype(BF)
    own_share_ref[...] = dot_nt(grad_ref[:half, :], attn)


def padded_width(width):
    return -(-width // 128) * 128


def put(out_ref, value):
    width = value.shape[1]
    out_ref[:, :width] = value.astype(out_ref.dtype)
    if out_ref.shape[1] > width:
        out_ref[:, width:] = jnp.zeros((value.shape[0], out_ref.shape[1] - width), out_ref.dtype)


def weave_body(minor_ref, mine_ref, theirs_ref, out_ref):
    first = minor_ref[0] == 0
    out_ref[0, 0] = jnp.where(first, mine_ref[0], theirs_ref[0])
    out_ref[0, 1] = jnp.where(first, theirs_ref[0], mine_ref[0])


def weave_call(minor, mine, theirs, start, rows, moved):
    majors, _, cols = mine.shape
    block = pl.BlockSpec(
        (pl.Element(1), pl.Element(rows), pl.Element(cols)), lambda k: (k, start, 0)
    )
    return pl.pallas_call(
        weave_body,
        grid=(majors,),
        out_shape=jax.ShapeDtypeStruct((majors, 2, rows, cols), mine.dtype),
        in_specs=[pl.BlockSpec(memory_space=pltpu.SMEM), block, block],
        out_specs=pl.BlockSpec((1, 2, rows, cols), lambda k: (k, 0, 0, 0)),
        compiler_params=pltpu.CompilerParams(vmem_limit_bytes=16 << 20),
        cost_estimate=pl.CostEstimate(flops=10**5, transcendentals=0, bytes_accessed=moved),
    )(minor, mine, theirs).reshape(majors * 2 * rows, cols)


def up_body(own_ref, other_ref, weight_ref, bias_ref, out_ref):
    half = own_ref.shape[0]
    depth = weight_ref.shape[0]
    for rows, from_ref in ((slice(half, None), other_ref), (slice(0, half), own_ref)):
        pre = dot(from_ref[:, :depth], weight_ref[...]) + bias_ref[...]
        out_ref[rows, :] = gelu_tanh(pre).astype(BF)


def down_body(hidden_ref, weight_ref, share_ref, own_share_ref):
    half = share_ref.shape[0]
    put(share_ref, dot_nt(hidden_ref[half:, :], weight_ref[...]))
    put(own_share_ref, dot_nt(hidden_ref[:half, :], weight_ref[...]))


def norm_forward_body(stream_ref, pair_ref, far_ref, bias_ref, gain_ref, shift_ref, new_ref, out_ref):
    width = stream_ref.shape[1]
    new = (
        stream_ref[...]
        + (pair_ref[:, :width].astype(F32) + far_ref[:, :width].astype(F32))
        + bias_ref[...]
    )
    new_ref[...] = new
    put(out_ref, layer_norm(new, gain_ref[...], shift_ref[...]))


def norm_backward_body(values_ref, gain_ref, pair_ref, far_ref, *refs):
    *top_ref, new_ref, low_ref, sums_ref = refs
    grad = pair_ref[...].astype(F32) + far_ref[...].astype(F32)
    values = values_ref[...]
    centered = values - jnp.mean(values, axis=-1, keepdims=True)
    variance = jnp.mean(centered * centered, axis=-1, keepdims=True)
    scale = lax.rsqrt(variance + EPSILON)
    unit = centered * scale
    inner = grad * gain_ref[...]
    new = scale * (
        inner
        - jnp.mean(inner, axis=-1, keepdims=True)
        - unit * jnp.mean(inner * unit, axis=-1, keepdims=True)
    )
    if top_ref:
        new = top_ref[0][...] + new
    new_ref[...] = new
    low_ref[...] = new.astype(BF)
    sums_ref[0:1, :] = jnp.sum(grad * unit, axis=0, keepdims=True)
    sums_ref[1:2, :] = jnp.sum(grad, axis=0, keepdims=True)
    sums_ref[2:3, :] = jnp.sum(new, axis=0, keepdims=True)
    sums_ref[3:, :] = jnp.zeros_like(sums_ref[3:, :])


def norm_forward(stream, pair, far, bias, gain, shift):
    return kernel_call(
        norm_forward_body,
        [(stream.shape, F32), (pair.shape, BF)],
        [stream, pair, far, bias[None], gain[None], shift[None]],
        vmem=16 << 20,
    )


def norm_backward(values, gain, pair, far, *top):
    return kernel_call(
        norm_backward_body,
        [(values.shape, F32), (values.shape, BF), ((8, values.shape[1]), F32)],
        [values, gain[None], pair, far, *top],
        vmem=16 << 20,
    )


def weight_grad_body(shape, count, minor_ref, *refs):
    majors, minors, rows = shape
    operands, (mine_ref, theirs_ref, sum_ref) = refs[: 3 * count], refs[3 * count :]
    start = 0
    for at in range(count):
        own, other, grad = operands[3 * at : 3 * at + 3]
        half, cols = own.shape[0], grad.shape[1]
        sum_ref[:, start : start + cols] = dot_tn(own[...], grad[:half, :]) + dot_tn(
            other[...], grad[half:, :]
        )
        start += cols
    for k in range(majors):
        to = slice(k * rows, (k + 1) * rows)
        here = pl.multiple_of((k * minors + minor_ref[0]) * rows, 8)
        there = pl.multiple_of((k * minors + 1 - minor_ref[0]) * rows, 8)
        mine_ref[to, :] = sum_ref[pl.ds(here, rows), :]
        theirs_ref[to, :] = sum_ref[pl.ds(there, rows), :].astype(BF)


STATS = 8


def logits_body(
    place_ref, teacher_ref, student_ref, teacher_head_ref, head_ref, t_ref, z_ref, stats_ref
):
    counted = place_ref[1 + pl.program_id(0)] > place_ref[0]

    @pl.when(counted)
    def _():
        t = dot(teacher_ref[:, : teacher_head_ref.shape[0]], teacher_head_ref[...])
        t_ref[...] = t
        z = dot(student_ref[...], head_ref[...])
        z_ref[...] = z
        t_peak = jnp.max(t, axis=-1, keepdims=True)
        t_exp = jnp.exp(t - t_peak)
        z_peak = jnp.max(z, axis=-1, keepdims=True)
        columns = (
            t_peak,
            jnp.sum(t_exp, axis=-1, keepdims=True),
            jnp.sum(t_exp * (t - z), axis=-1, keepdims=True),
            z_peak,
            jnp.sum(jnp.exp(z - z_peak), axis=-1, keepdims=True),
        )
        lane = lax.broadcasted_iota(jnp.int32, (t.shape[0], 128), 1)
        packed = jnp.zeros(lane.shape, F32)
        for at, column in enumerate(columns):
            packed = jnp.where(lane == at, column, packed)
        stats_ref[...] = packed.T[:STATS, :]

    @pl.when(jnp.logical_not(counted))
    def _():
        row = lax.broadcasted_iota(jnp.int32, stats_ref.shape, 0)
        stats_ref[...] = jnp.where((row == 1) | (row == 4), 1.0, 0.0)


def merge_body(*refs):
    *in_refs, out_ref = refs
    many = [ref[...] for ref in in_refs]
    if many[0].ndim == 3:
        many = [many[0][k] for k in range(many[0].shape[0])]
    t_high = functools.reduce(jnp.maximum, [one[0:1] for one in many])
    z_high = functools.reduce(jnp.maximum, [one[3:4] for one in many])
    t_scale = [jnp.exp(one[0:1] - t_high) for one in many]
    z_scale = [jnp.exp(one[3:4] - z_high) for one in many]
    out_ref[0:1, :] = t_high
    out_ref[1:2, :] = sum(one[1:2] * scale for one, scale in zip(many, t_scale))
    out_ref[2:3, :] = sum(one[2:3] * scale for one, scale in zip(many, t_scale))
    out_ref[3:4, :] = z_high
    out_ref[4:5, :] = sum(one[4:5] * scale for one, scale in zip(many, z_scale))
    out_ref[5:, :] = jnp.zeros_like(out_ref[5:, :])


def logits_back_body(place_ref, weight_ref, t_ref, z_ref, stats_ref, head_ref, *refs):
    out_ref = refs[-1]
    length = place_ref[1 + pl.program_id(0)]

    @pl.when(length > place_ref[0])
    def _():
        stats = stats_ref[...]
        row = lax.broadcasted_iota(jnp.int32, stats.shape, 0)
        logs = jnp.log(jnp.where((row == 1) | (row == 4), stats, 1.0))
        totals = stats + pltpu.roll(logs, STATS - 1, 0)
        totals = jnp.concatenate([totals] * (128 // STATS), axis=0).T
        rows = t_ref.shape[0]
        position = place_ref[0] + lax.broadcasted_iota(jnp.int32, (rows, 1), 0)
        weight = jnp.where(position < length, weight_ref[0], 0.0)
        grad = (jnp.exp(z_ref[...] - totals[:, 3:4]) - jnp.exp(t_ref[...] - totals[:, 0:1])) * weight
        share = dot_nt(grad.astype(BF), head_ref[...])
        if len(refs) == 2:
            share = share + refs[0][...].astype(F32)
        out_ref[...] = share.astype(BF)

    @pl.when(length <= place_ref[0])
    def _():
        out_ref[...] = jnp.zeros_like(out_ref) if len(refs) == 1 else refs[0][...]


def row_blocks(rows, cols):
    return pl.BlockSpec((rows, cols), lambda i: (i, 0))


def held_block(array):
    return pl.BlockSpec(array.shape, lambda i: (0, 0), pipeline_mode=pl.Buffered(1))


def stat_blocks(rows):
    return pl.BlockSpec((STATS, rows), lambda i: (0, i))


SCALAR = pl.BlockSpec(memory_space=pltpu.SMEM)


def logits_call(place, teacher, student, teacher_head, head):
    tokens = teacher.shape[0]
    rows, vocab = tokens // MAJOR, head.shape[1]
    return pl.pallas_call(
        logits_body,
        grid=(MAJOR,),
        out_shape=[
            jax.ShapeDtypeStruct((tokens, vocab), F32),
            jax.ShapeDtypeStruct((tokens, vocab), F32),
            jax.ShapeDtypeStruct((STATS, tokens), F32),
        ],
        in_specs=[
            SCALAR,
            row_blocks(rows, teacher.shape[1]),
            row_blocks(rows, student.shape[1]),
            held_block(teacher_head),
            held_block(head),
        ],
        out_specs=[row_blocks(rows, vocab), row_blocks(rows, vocab), stat_blocks(rows)],
        compiler_params=pltpu.CompilerParams(vmem_limit_bytes=44 << 20),
        cost_estimate=pl.CostEstimate(
            flops=10**6,
            transcendentals=0,
            bytes_accessed=10**5,
        ),
    )(place, teacher, student, teacher_head, head)


def logits_back_call(place, weight, t, z, stats, head, *more):
    tokens, vocab = t.shape
    rows, width = tokens // MAJOR, head.shape[0]
    return pl.pallas_call(
        logits_back_body,
        grid=(MAJOR,),
        out_shape=jax.ShapeDtypeStruct((tokens, width), BF),
        in_specs=[
            SCALAR,
            SCALAR,
            row_blocks(rows, vocab),
            row_blocks(rows, vocab),
            stat_blocks(rows),
            held_block(head),
            *[row_blocks(rows, width) for _ in more],
        ],
        out_specs=row_blocks(rows, width),
        compiler_params=pltpu.CompilerParams(vmem_limit_bytes=40 << 20),
        cost_estimate=pl.CostEstimate(
            flops=10**6,
            transcendentals=0,
            bytes_accessed=10**5,
        ),
    )(place, weight, t, z, stats, head, *more)


def merged(*many):
    return pl.pallas_call(
        merge_body, out_shape=jax.ShapeDtypeStruct(many[0].shape[-2:], F32)
    )(*many)


def adam_update(weight, first, second, average, grad, clip, rate, decay):
    keep = min(0.995, (1.0 + STEP) / (10.0 + STEP))
    grad = grad * clip
    first_new = BETA_ONE * first + (1.0 - BETA_ONE) * grad
    second_new = BETA_TWO * second + (1.0 - BETA_TWO) * grad * grad
    first_hat = first_new / (1.0 - BETA_ONE**STEP)
    second_hat = second_new / (1.0 - BETA_TWO**STEP)
    weight_new = weight - rate * (
        first_hat / (jnp.sqrt(second_hat) + ADAM_EPSILON) + decay * weight
    )
    average_new = keep * average + (1.0 - keep) * weight_new
    return (weight_new, first_new, second_new, average_new)


def tie(first, second):
    return lax.optimization_barrier((first, second))


SCALARS = 6


def pack_body(mp, mp_ref, final_ref, *refs):
    *layer_refs, out_ref, line_ref = refs
    devices, groups = out_ref.shape[0], out_ref.shape[0] // mp
    rows, lines = [], len(layer_refs) // 5
    for at in range(lines):
        middle, inner, above, qkv, up = layer_refs[5 * at : 5 * at + 5]
        rows += [(inner, 0), (inner, 1), (middle, 2), (middle, 0), (middle, 1), (above, 2)]
        part = qkv.shape[1] // 3
        line_ref[at : at + 1, :part] = qkv[:, :part]
        line_ref[at : at + 1, part : 2 * part] = qkv[:, 2 * part :]
        line_ref[at : at + 1, 2 * part :] = up[...]
    rows += [(final_ref, 0), (final_ref, 1)]
    out_ref[...] = jnp.zeros_like(out_ref)
    blocks = final_ref.shape[1] // 128
    each = -(-len(rows) * blocks // devices)
    for at, (ref, row) in enumerate(rows):
        for block in range(blocks):
            to = at * blocks + block
            out_ref[to // each, to % each : to % each + 1, :] = (
                0.5 * ref[row : row + 1, 128 * block : 128 * (block + 1)]
            )
    blocks = line_ref.shape[1] // 128
    own_each = -(-lines * blocks // groups)
    for at in range(lines * blocks):
        line, block = divmod(at, blocks)
        value = line_ref[line : line + 1, 128 * block : 128 * (block + 1)]
        row = each + at % own_each
        for m in range(mp):
            out_ref[at // own_each * mp + m, row : row + 1, :] = jnp.where(
                mp_ref[0] == m, value, 0.0
            )


def square_body(loss_ref, packets_ref, *refs):
    *grad_refs, out_ref = refs
    devices = packets_ref.shape[0]
    total = packets_ref[0]
    for at in range(1, devices):
        total = total + packets_ref[at]
    squares = jnp.sum(total * total)
    for ref in grad_refs:
        grad = ref[...].astype(F32)
        squares = squares + jnp.sum(grad * grad)
    row = lax.broadcasted_iota(jnp.int32, total.shape, 0)
    lane = lax.broadcasted_iota(jnp.int32, total.shape, 1)
    total = jnp.where((row == SCALARS) & (lane == 0), squares, total)
    total = jnp.where((row == SCALARS) & (lane == 1), loss_ref[0], total)
    for at in range(devices):
        out_ref[at] = total


def scalar_body(packets_ref, scalar_ref):
    devices = packets_ref.shape[0]
    sums = packets_ref[0, SCALARS : SCALARS + 1, :]
    for at in range(1, devices):
        sums = sums + packets_ref[at, SCALARS : SCALARS + 1, :]
    norm = jnp.sqrt(sums[:, 0:1])
    clip = CLIP_LIMIT / jnp.maximum(norm, CLIP_LIMIT)
    row = lax.broadcasted_iota(jnp.int32, scalar_ref.shape, 0)
    scalar_ref[...] = jnp.where(row == 0, clip, jnp.where(row == 1, norm, sums[:, 1:2]))


def small_update_body(mp, mp_ref, packets_ref, scalar_ref, *refs):
    states, outs = refs[:12], refs[12:24]
    line_ref, grad_ref = refs[24:]
    devices, groups = packets_ref.shape[0], packets_ref.shape[0] // mp
    clip = scalar_ref[0:1, 0:1]
    kinds, layers, width = states[0].shape
    blocks = width // 128
    each = -(-(layers * kinds + 2) * blocks // devices)
    for at in range(layers * kinds + 2):
        for block in range(blocks):
            source = at * blocks + block
            grad_ref[at : at + 1, 128 * block : 128 * (block + 1)] = packets_ref[
                source // each, source % each : source % each + 1, :
            ]

    def update(kind, pick, grad, rate):
        values = [ref[pick] for ref in states[4 * kind : 4 * kind + 4]]
        for ref, value in zip(
            outs[4 * kind : 4 * kind + 4], adam_update(*values, grad, clip, rate, 0.0)
        ):
            ref[pick] = value

    for layer in range(layers):
        update(0, (slice(None), layer), grad_ref[layer * kinds : (layer + 1) * kinds, :], 0.5)
    update(1, slice(None), grad_ref[layers * kinds : layers * kinds + 2, :], 0.5)
    part = states[8].shape[2]
    blocks = line_ref.shape[1] // 128
    own_each = -(-layers * blocks // groups)
    for at in range(layers * blocks):
        line, block = divmod(at, blocks)
        source = at // own_each * mp + mp_ref[0]
        from_row = each + at % own_each
        line_ref[line : line + 1, 128 * block : 128 * (block + 1)] = packets_ref[
            pl.ds(source, 1), from_row : from_row + 1, :
        ].reshape(1, 128)
    for layer in range(layers):
        grad = jnp.concatenate(
            [
                line_ref[layer : layer + 1, part * at : part * (at + 1)]
                for at in range(states[8].shape[0])
            ],
            axis=0,
        )
        update(2, (slice(None), layer), grad, 0.1)


class Wires:
    def __init__(self):
        self.dp = lax.axis_size("dp")
        self.mp = lax.axis_size("mp")
        self.minors = self.dp // MAJOR
        self.dp_at = lax.axis_index("dp")
        self.mp_at = lax.axis_index("mp")
        self.major = self.dp_at // self.minors
        self.minor = self.dp_at % self.minors
        self.near_at = self.mp_at % 2
        self.near_ref = self.near_at.reshape(1).astype(jnp.int32)
        self.minor_ref = self.minor.reshape(1).astype(jnp.int32)
        self.near_pairs = [(i, i ^ 1) for i in range(self.mp)]
        self.far_pairs = [(i, i ^ 2) for i in range(self.mp)]
        self.over_major = [
            [k * self.minors + j for k in range(MAJOR)] for j in range(self.minors)
        ]
        self.over_minor = [
            [k * self.minors + j for j in range(self.minors)] for k in range(MAJOR)
        ]

    def near(self, part):
        return lax.ppermute(part, "mp", self.near_pairs)

    def far(self, part):
        return lax.ppermute(part, "mp", self.far_pairs)

    def natural(self, own, other):
        first = self.near_at == 0
        return jnp.concatenate([jnp.where(first, own, other), jnp.where(first, other, own)], axis=0)

    def own_first(self, whole):
        half = whole.shape[0] // 2
        own = lax.dynamic_slice_in_dim(whole, self.near_at * half, half, 0)
        other = lax.dynamic_slice_in_dim(whole, (1 - self.near_at) * half, half, 0)
        return own, other

    def across(self, part):
        return lax.ppermute(part, "mp", [(i, i ^ 3) for i in range(self.mp)])

    def shares(self, other, own):
        pair = (own + self.near(other.astype(BF)).astype(F32)).astype(BF)
        return pair, self.far(pair)

    def minor_parts(self, part):
        if self.minors == 2:
            return lax.ppermute(part, "dp", [(i, i ^ 1) for i in range(self.dp)])
        return lax.all_gather(part, "dp", axis=0, axis_index_groups=self.over_minor)

    def minor_stack(self, part, others, axis):
        if self.minors == 2:
            first = self.minor == 0
            return jnp.stack(
                [jnp.where(first, part, others), jnp.where(first, others, part)], axis=axis
            )
        return jnp.moveaxis(others, 0, axis)

    def major_gather(self, part):
        return lax.all_gather(
            part, "dp", axis=0, tiled=True, axis_index_groups=self.over_major
        )

    def minor_joined(self, part):
        return self.minor_stack(part, self.minor_parts(part), 0).reshape(-1, part.shape[-1])

    def minor_woven(self, part, others, start=0, rows=None, moved=10**5):
        rows = part.shape[1] if rows is None else rows
        if self.minors == 2:
            return weave_call(self.minor_ref, part, others, start, rows, moved)
        stacked = self.minor_stack(part, others, 1)[:, :, start : start + rows]
        return stacked.reshape(-1, part.shape[-1])

    def major_swap(self, part):
        return lax.all_to_all(part, "dp", 0, 0, axis_index_groups=self.over_major)

    def grad_started(self, *products):
        width, cols = products[0][0].shape[1], sum(grad.shape[1] for _, _, grad in products)
        rows = width // self.dp
        if self.minors == 2 and rows % 8 == 0:
            mine, theirs = kernel_call(
                functools.partial(
                    weight_grad_body, (MAJOR, self.minors, rows), len(products)
                ),
                [((MAJOR * rows, cols), F32), ((MAJOR * rows, cols), BF)],
                [self.minor_ref, *sum(([*product] for product in products), [])],
                scratch=[pltpu.VMEM((width, cols), F32)],
                vmem=40 << 20,
                flops=2 * 2 * products[0][0].shape[0] * width * cols,
            )
            return mine, self.minor_parts(theirs)
        total = jnp.concatenate(
            [dot_tn(jnp.concatenate(product[:2]), product[2]) for product in products], axis=1
        )
        held = lax.psum_scatter(
            total.reshape(MAJOR, self.minors, rows, cols).astype(BF),
            "dp",
            scatter_dimension=1,
            axis_index_groups=self.over_minor,
        )
        return held.reshape(-1, cols).astype(F32), None

    def grad_ended(self, mine, theirs, direct=False):
        held = (mine if theirs is None else mine + theirs.astype(F32)).astype(BF)
        if direct:
            held = self.major_swap(held.reshape(MAJOR, -1, held.shape[-1]))
            return jnp.sum(held.astype(F32), axis=0)
        return lax.psum_scatter(
            held, "dp", scatter_dimension=0, tiled=True, axis_index_groups=self.over_major
        )


def local(
    inputs,
    lengths,
    teacher_inputs,
    teacher_qkv,
    teacher_proj,
    teacher_up,
    teacher_up_bias,
    teacher_down,
    teacher_vectors,
    teacher_head,
    head,
    column_weights,
    column_first,
    column_second,
    column_average,
    row_weights,
    row_first,
    row_second,
    row_average,
    column_biases,
    bias_first,
    bias_second,
    bias_average,
    norm_vectors,
    vector_first,
    vector_second,
    vector_average,
    final_norm,
    final_first,
    final_second,
    final_average,
):
    wires = Wires()
    token_count, width = inputs.shape
    half = token_count // 2
    teacher_width = teacher_inputs.shape[1]
    layers, shard_rows, col_blocks, part = column_weights.shape
    up_blocks = col_blocks - 3
    units = up_blocks * part

    slots = -(-THEADS // wires.mp)
    base_heads = THEADS // wires.mp
    extra_heads = THEADS % wires.mp
    own_start = wires.mp_at * base_heads + jnp.minimum(wires.mp_at, extra_heads)
    own_stop = own_start + base_heads + jnp.where(wires.mp_at < extra_heads, 1, 0)
    slot_start = jnp.minimum(own_start, THEADS - slots)
    head_ids = slot_start + jnp.arange(slots, dtype=jnp.int32)
    owned = ((head_ids >= own_start) & (head_ids < own_stop)).astype(jnp.int32)
    slot_width = slots * THD
    first_col = slot_start * THD

    qkv_shard = lax.dynamic_slice_in_dim(teacher_qkv, first_col, slot_width, 2)
    proj_shard = lax.dynamic_slice_in_dim(teacher_proj, first_col, slot_width, 0).T
    shards = []
    for layer in range(layers):
        cols = column_weights[layer].astype(BF)
        rows = row_weights[layer].astype(BF)
        shards.append(
            jnp.concatenate(
                [
                    cols[:, 3:].reshape(shard_rows, units),
                    rows[1:].reshape(units, shard_rows).T,
                    cols[:, :3].reshape(shard_rows, 3 * part),
                    rows[0].T,
                ],
                axis=1,
            )
        )
    shards.extend(
        [
            jnp.concatenate([qkv_shard.reshape(-1, 3 * slot_width), proj_shard], axis=1),
            teacher_up,
            teacher_down.T,
        ]
    )
    own_at = wires.near_at * half
    tv = teacher_vectors
    teacher_pad = padded_width(teacher_width)
    teacher_stream, teacher_other = (
        lax.dynamic_slice_in_dim(teacher_inputs, at, half, 0).astype(F32)
        for at in (own_at, half - own_at)
    )
    query_bias, value_bias = (
        lax.dynamic_slice_in_dim(tv[at], first_col, slot_width) for at in (2, 3)
    )
    teacher_start = (
        layer_norm(teacher_stream, tv[0], tv[1]).astype(BF),
        layer_norm(teacher_other, tv[0], tv[1]).astype(BF),
        jnp.concatenate([query_bias, jnp.zeros_like(query_bias), value_bias])[None],
    )

    held, rows, others = [], [], []

    def launch(mark):
        shard = shards[len(held)]
        if mark is not None:
            shard, mark = tie(shard, mark)
        if held:
            shard, rows[-1] = tie(shard, held[-1])
        held.append(wires.major_gather(shard).reshape(MAJOR, *shard.shape))
        rows.append(held[-1])
        others.append(wires.minor_parts(held[-1]))
        return mark

    for _ in range(layers):
        launch(None)
    vocab_part = head.shape[1] // MAJOR
    cut = teacher_head.shape[0]
    both = jnp.stack(
        [
            jnp.concatenate(
                [rows_[:, k * vocab_part : (k + 1) * vocab_part] for rows_ in (teacher_head, head)],
                axis=0,
            )
            for k in range(MAJOR)
        ]
    )

    stream = lax.dynamic_slice_in_dim(inputs, own_at, half, 0).astype(F32)
    heads = part // HD
    all_heads = jnp.ones((heads,), jnp.int32)

    layer_full = []

    def columns(layer, at):
        return (layer_full[layer], (width, units), (0, at))

    saved = []
    one_own = layer_norm(stream, norm_vectors[0, 0], norm_vectors[0, 1]).astype(BF)
    one_own, (teacher_stream, teacher_start, both, *shards[layers:]) = tie(
        one_own, (teacher_stream, teacher_start, both, *shards[layers:])
    )
    for layer in range(layers):
        vector = norm_vectors[layer]
        layer_full.append(wires.minor_woven(rows[layer], others[layer]))
        if layer == 0:
            layer_full[0] = launch(layer_full[0])
        one = (one_own, wires.near(one_own))
        bias = column_biases[layer]
        share, own_share, attended, qkv, totals = kernel_call(
            functools.partial(attention_forward_body, heads, HD),
            [
                ((half, width), BF),
                ((half, width), F32),
                ((token_count, part), BF),
                ((token_count, 3 * part), BF),
                ((token_count, 128), F32),
            ],
            [
                wires.near_ref,
                all_heads,
                *one,
                columns(layer, 2),
                jnp.concatenate([bias[0], jnp.zeros_like(bias[0]), bias[1]])[None],
            ],
        )
        middle, two_own = norm_forward(
            stream, *wires.shares(share, own_share), vector[2], vector[3], vector[4]
        )
        two = (two_own, wires.near(two_own))
        pre_act, hidden, share, own_share = kernel_call(
            mlp_forward_body,
            [
                ((token_count, units), F32),
                ((token_count, units), BF),
                ((half, width), BF),
                ((half, width), F32),
            ],
            [*two, columns(layer, 0), columns(layer, 1), bias[2:].reshape(1, units)],
        )
        saved.append((stream, one, qkv, totals, attended, middle, two, pre_act, hidden))
        later = norm_vectors[layer + 1] if layer + 1 < layers else final_norm
        parts, others[layer + 1] = tie(wires.shares(share, own_share), others[layer + 1])
        stream, one_own = norm_forward(middle, *parts, vector[5], later[0], later[1])
        if len(held) < len(shards):
            one_own = launch(one_own)
    final_out = one_own
    while len(held) < len(shards):
        launch(None)
    (mine, theirs), rows[-2] = tie((rows[-3], others[-3]), rows[-2])
    teacher_attn = wires.minor_woven(mine, theirs)
    teacher_share, teacher_own_share = kernel_call(
        functools.partial(attention_forward_body, slots, THD),
        [((half, teacher_pad), BF), ((half, teacher_pad), F32)],
        [
            wires.near_ref,
            owned,
            *teacher_start[:2],
            teacher_attn,
            teacher_start[2],
        ],
        scratch=[
            pltpu.VMEM((token_count, slot_width), BF),
            pltpu.VMEM((token_count, 3 * slot_width), BF),
            pltpu.VMEM((token_count, 128), F32),
        ],
        vmem=36 << 20,
    )
    parts, others[-2] = tie(wires.shares(teacher_share, teacher_own_share), others[-2])
    both, others[-2] = tie(both, others[-2])
    both, rows[-1] = tie(both, rows[-1])
    both = wires.major_swap(both)
    both_others = wires.minor_parts(both)
    final_out, rows[-1] = tie(final_out, rows[-1])
    student_rows = wires.major_gather(final_out)
    teacher_up_full = wires.minor_woven(rows[-2], others[-2])
    teacher_mid, normed_own = norm_forward(teacher_stream, *parts, tv[4], tv[5], tv[6])
    (hidden,) = kernel_call(
        up_body,
        [((token_count, teacher_up.shape[1]), BF)],
        [normed_own, wires.near(normed_own), teacher_up_full, teacher_up_bias[None]],
        vmem=32 << 20,
    )
    share, own_share = kernel_call(
        down_body,
        [((half, teacher_pad), BF), ((half, teacher_pad), F32)],
        [hidden, wires.minor_woven(rows[-1], others[-1])],
        vmem=32 << 20,
    )
    _, teacher_final = norm_forward(
        teacher_mid, *wires.shares(share, own_share), tv[7], tv[8], tv[9]
    )
    teacher_final, student_rows = tie(teacher_final, student_rows)
    teacher_rows, both_others = tie(wires.major_gather(teacher_final), both_others)
    teacher_head_part = wires.minor_woven(both, both_others, 0, cut)
    head_part = wires.minor_woven(both, both_others, cut, head.shape[0])

    teacher_sides = (teacher_rows, wires.near(teacher_rows))
    student_sides = (student_rows, wires.near(student_rows))
    row_ids = jnp.arange(MAJOR, dtype=jnp.int32) * wires.minors + wires.minor
    row_lengths = jnp.sum(
        jnp.where(
            row_ids[:, None] == jnp.arange(lengths.shape[0], dtype=jnp.int32)[None, :],
            lengths[None, :],
            0,
        ),
        axis=1,
    )
    places = [
        jnp.concatenate([start.reshape(1).astype(jnp.int32), row_lengths])
        for start in (own_at, half - own_at)
    ]
    row_weight = 1.0 / jnp.sum(lengths).astype(F32)
    sides = [
        logits_call(place, teacher, student, teacher_head_part, head_part)
        for place, teacher, student in zip(places, teacher_sides, student_sides)
    ]
    own_stats, other_stats = sides[0][2], sides[1][2]
    stats = merged(
        own_stats, wires.near(other_stats), wires.far(own_stats), wires.across(other_stats)
    )
    stats = merged(
        wires.major_swap(jnp.broadcast_to(stats[None], (MAJOR, *stats.shape)))
    )
    other_stats = wires.near(stats)
    divergence = (
        stats[2] / stats[1] - (stats[0] + jnp.log(stats[1])) + (stats[3] + jnp.log(stats[4]))
    ).reshape(MAJOR, half)
    counted = own_at + jnp.arange(half, dtype=jnp.int32)[None, :] < row_lengths[:, None]
    loss_part = jnp.sum(jnp.where(counted, divergence, 0.0)) * (
        row_weight * (2.0 / (MAJOR * wires.mp))
    )

    weight = row_weight.reshape(1)
    share = logits_back_call(places[1], weight, *sides[1][:2], other_stats, head_part)
    share = logits_back_call(
        places[0], weight, *sides[0][:2], stats, head_part, wires.near(share)
    )
    share = wires.major_swap(share.reshape(MAJOR, half, width))
    share = jnp.sum(share.astype(F32), axis=0).astype(BF)
    grad_stream, out_own, final_sums = norm_backward(
        stream, final_norm[0], share, wires.far(share)
    )
    small_sums = []
    products, started, ended = [], [], []

    def start(parts):
        mine, theirs = wires.grad_started(*products)
        parts, mine = tie(parts, mine)
        started.append((mine, theirs))
        products.clear()
        return parts

    def passed(parts, count):
        for mine, theirs in started[len(ended) : count]:
            if theirs is not None:
                parts, theirs = tie(parts, theirs)
            if ended:
                mine, ended[-1] = tie(mine, ended[-1])
            ended.append(wires.grad_ended(mine, theirs))
        return parts

    above = final_sums
    for layer in reversed(range(layers)):
        layer_in, one, qkv, totals, attended, middle, two, pre_act, hidden = saved[layer]
        vector = norm_vectors[layer]
        out = (out_own, wires.near(out_own))
        grad_pre, up_sums, share, own_share = kernel_call(
            mlp_backward_body,
            [
                ((token_count, units), BF),
                ((1, units), F32),
                ((half, width), BF),
                ((half, width), F32),
            ],
            [*out, columns(layer, 0), columns(layer, 1), pre_act],
        )
        share = passed(share, 2 * (layers - 1 - layer) - 1)
        parts = wires.shares(share, own_share)
        products.extend([(*two, grad_pre), (*out, hidden)])
        parts = start(parts)
        grad_middle, mid_own, middle_sums = norm_backward(
            middle, vector[3], *parts, grad_stream
        )
        mid = (mid_own, wires.near(mid_own))
        grad_qkv, qkv_sums, share, own_share = kernel_call(
            functools.partial(attention_backward_body, heads, HD),
            [
                ((token_count, 3 * part), BF),
                ((1, 3 * part), F32),
                ((half, width), BF),
                ((half, width), F32),
            ],
            [wires.near_ref, *mid, columns(layer, 2), qkv, totals],
            scratch=[
                pltpu.VMEM((token_count, part), BF),
                pltpu.VMEM((half, HD), F32),
                pltpu.VMEM((half, HD), F32),
            ],
        )
        share = passed(share, 2 * (layers - 1 - layer))
        parts = wires.shares(share, own_share)
        products.extend([(*one, grad_qkv), (*mid, attended)])
        parts = start(parts)
        grad_stream, out_own, in_sums = norm_backward(
            layer_in, vector[0], *parts, grad_middle
        )
        small_sums.insert(0, [middle_sums, in_sums, above, qkv_sums, up_sums])
        above = in_sums
    input_grad = wires.natural(grad_stream, wires.near(grad_stream))
    everyone = wires.dp * wires.mp
    mp_ref = wires.mp_at.reshape(1).astype(jnp.int32)
    packet = (everyone, 8, 128)
    (packets,) = kernel_call(
        functools.partial(pack_body, wires.mp),
        [(packet, F32)],
        [mp_ref, final_sums, *sum(small_sums, [])],
        scratch=[pltpu.VMEM((layers, (2 + up_blocks) * part), F32)],
        vmem=8 << 20,
    )
    packets = lax.all_to_all(packets, ("dp", "mp"), 0, 0)
    for at in range(len(ended), len(started)):
        mine, theirs = started[at]
        if at == 2 * layers - 2:
            mine, ended[-1] = tie(mine, ended[-1])
            mine, packets = tie(mine, packets)
        if at == 2 * layers - 1:
            mine, ended[-1] = tie(mine, ended[-1])
        ended.append(wires.grad_ended(mine, theirs, direct=at >= 2 * layers - 2))
    squared = ended
    cuts = [units, 2 * units, 2 * units + 3 * part]
    ended = [part_grad.astype(F32) for part_grad in ended]
    ended = [jnp.concatenate(pair, axis=1) for pair in zip(ended[0::2], ended[1::2])][::-1]
    up_shards, down_shards, attn_shards, proj_shards = zip(
        *[jnp.split(whole, cuts, axis=1) for whole in ended]
    )

    (packets,) = kernel_call(
        square_body, [(packet, F32)], [loss_part.reshape(1), packets, *squared], vmem=16 << 20
    )
    packets = lax.all_to_all(packets, ("dp", "mp"), 0, 0)
    states = (
        *(norm_vectors, vector_first, vector_second, vector_average),
        *(final_norm, final_first, final_second, final_average),
        *(column_biases, bias_first, bias_second, bias_average),
    )
    states = [jnp.swapaxes(state, 0, 1) if state.ndim == 3 else state for state in states]
    (scalars,) = kernel_call(scalar_body, [((8, 128), F32)], [packets], vmem=8 << 20)
    small_out = kernel_call(
        functools.partial(small_update_body, wires.mp),
        [(state.shape, F32) for state in states],
        [mp_ref, packets, scalars, *states],
        scratch=[
            pltpu.VMEM((layers, (2 + up_blocks) * part), F32),
            pltpu.VMEM((layers * 6 + 2, width), F32),
        ],
        vmem=16 << 20,
    )
    small_out = [jnp.swapaxes(state, 0, 1) if state.ndim == 3 else state for state in small_out]
    clip, grad_norm, loss_total = scalars[0, 0], scalars[1, 0], scalars[2, 0]

    col_shard = jnp.stack(
        [
            jnp.concatenate(
                [
                    attn_shards[layer].reshape(shard_rows, 3, part),
                    up_shards[layer].reshape(shard_rows, up_blocks, part),
                ],
                axis=1,
            )
            for layer in range(layers)
        ]
    )
    row_shard = jnp.stack(
        [
            jnp.concatenate(
                [
                    proj_shards[layer].T.reshape(1, part, shard_rows),
                    down_shards[layer].T.reshape(up_blocks, part, shard_rows),
                ],
                axis=0,
            )
            for layer in range(layers)
        ]
    )
    column_out = adam_update(
        column_weights, column_first, column_second, column_average, col_shard, clip, 0.1, 0.1
    )
    row_out = adam_update(
        row_weights, row_first, row_second, row_average, row_shard, clip, 0.2, 0.1
    )
    return (
        loss_total,
        grad_norm,
        input_grad,
        *column_out,
        *row_out,
        *small_out[8:],
        *small_out[:8],
    )


def solution(mesh):
    tokens, copied = P("dp", None), P()
    columns, rows, biases = P(None, "dp", None, "mp"), P(None, None, "mp", "dp"), P(None, None, "mp")
    placed = (
        tokens,
        copied,
        tokens,
        P("dp", None, None),
        P(None, "dp"),
        P("dp", "mp"),
        P("mp"),
        P("mp", "dp"),
        copied,
        P("dp", "mp"),
        P("dp", "mp"),
        *[columns] * 4,
        *[rows] * 4,
        *[biases] * 4,
        *[copied] * 8,
    )
    return jax.shard_map(
        local,
        mesh=mesh,
        in_specs=placed,
        out_specs=(
            copied,
            copied,
            tokens,
            *[columns] * 4,
            *[rows] * 4,
            *[biases] * 4,
            *[copied] * 8,
        ),
        check_vma=False,
    )
```

```python
import functools

import jax
import jax.numpy as jnp
from jax import lax
from jax.experimental import pallas as pl
from jax.experimental.pallas import tpu as pltpu
from jax.sharding import PartitionSpec as P

HD = 64
THEADS = 25
THD = 64
SEQ = 512
STEP = 4
MAJOR = 4

EPSILON = 1e-05
GELU_COEFF = 0.7978845608028654
BETA_ONE = 0.9
BETA_TWO = 0.999
ADAM_EPSILON = 1e-08
CLIP_LIMIT = 0.002

BF = jnp.bfloat16
F32 = jnp.float32


def dot(a, b):
    return jnp.dot(a, b, preferred_element_type=F32)


def dot_nt(a, b):
    return lax.dot_general(a, b, (((1,), (1,)), ((), ())), preferred_element_type=F32)


def dot_tn(a, b):
    return lax.dot_general(a, b, (((0,), (0,)), ((), ())), preferred_element_type=F32)


def layer_norm(values, gain, shift):
    centered = values - jnp.mean(values, axis=-1, keepdims=True)
    variance = jnp.mean(centered * centered, axis=-1, keepdims=True)
    return centered * lax.rsqrt(variance + EPSILON) * gain + shift


def gelu_tanh(values):
    return (
        0.5 * values * (1.0 + jnp.tanh(GELU_COEFF * (values + 0.044715 * values * values * values)))
    )


def kernel_call(body, outs, blocks, scratch=(), vmem=24 << 20, flops=10**6):
    specs, operands = [], []
    for entry in blocks:
        if isinstance(entry, tuple):
            array, shape, index = entry
            specs.append(pl.BlockSpec(shape, functools.partial(lambda at, _: at, index)))
            operands.append(array)
        elif entry.ndim == 1:
            specs.append(pl.BlockSpec(memory_space=pltpu.SMEM))
            operands.append(entry)
        else:
            whole = (0,) * entry.ndim
            specs.append(pl.BlockSpec(entry.shape, functools.partial(lambda at, _: at, whole)))
            operands.append(entry)
    return pl.pallas_call(
        body,
        grid=(1,),
        out_shape=[jax.ShapeDtypeStruct(shape, kind) for shape, kind in outs],
        in_specs=specs,
        out_specs=[
            pl.BlockSpec(shape, functools.partial(lambda at, _: at, (0,) * len(shape)))
            for shape, _ in outs
        ],
        scratch_shapes=list(scratch),
        compiler_params=pltpu.CompilerParams(vmem_limit_bytes=vmem),
        cost_estimate=pl.CostEstimate(flops=flops, transcendentals=0, bytes_accessed=10**5),
    )(*operands)


def masked_scores(queries, key_rows, start):
    scores = dot_nt(queries, key_rows) * (queries.shape[1] ** (-0.5))
    query_pos = start + lax.broadcasted_iota(jnp.int32, scores.shape, 0)
    key_pos = lax.broadcasted_iota(jnp.int32, scores.shape, 1)
    return jnp.where(key_pos <= query_pos, scores, -jnp.inf)


def attention_forward_body(
    heads, size, near_ref, kept_ref, own_ref, other_ref, weight_ref, bias_ref,
    share_ref, own_share_ref, out_ref, qkv_ref, total_ref,
):
    half, part = own_ref.shape[0], heads * size
    first = near_ref[0] == 0
    attn = weight_ref[:, : 3 * part]
    own = dot(own_ref[...], attn) + bias_ref[...]
    other = dot(other_ref[...], attn) + bias_ref[...]
    qkv_ref[:half, :] = jnp.where(first, own, other).astype(BF)
    qkv_ref[half:, :] = jnp.where(first, other, own).astype(BF)
    lane = lax.broadcasted_iota(jnp.int32, (half, total_ref.shape[1]), 1)
    for block in range(2):
        rows = slice(block * half, (block + 1) * half)
        seen = (block + 1) * half
        to = pl.multiple_of((near_ref[0] ^ block) * half, half)
        totals = jnp.zeros(lane.shape, F32)
        for head in range(heads):
            q = qkv_ref[rows, head * size : (head + 1) * size]
            k = qkv_ref[:seen, part + head * size : part + (head + 1) * size]
            v = qkv_ref[:seen, 2 * part + head * size : 2 * part + (head + 1) * size]
            scores = masked_scores(q, k, block * half)
            highest = jnp.max(scores, axis=-1, keepdims=True)
            mass = jnp.exp(scores - highest)
            whole = jnp.sum(mass, axis=-1, keepdims=True)
            weights = (mass * (1.0 / whole)).astype(BF)
            result = jnp.where(kept_ref[head] == 1, dot(weights, v), 0.0)
            out_ref[pl.ds(to, half), head * size : (head + 1) * size] = result.astype(BF)
            totals = jnp.where(lane == head, highest + jnp.log(whole), totals)
        total_ref[rows, :] = totals
    proj = weight_ref[:, 3 * part : 4 * part]
    put(share_ref, dot_nt(out_ref[half:, :], proj))
    put(own_share_ref, dot_nt(out_ref[:half, :], proj))


def mlp_forward_body(
    own_ref, other_ref, up_ref, down_ref, bias_ref, pre_ref, hidden_ref, share_ref, own_share_ref
):
    half = own_ref.shape[0]
    for rows, from_ref in ((slice(half, None), other_ref), (slice(0, half), own_ref)):
        pre = dot(from_ref[...], up_ref[...]) + bias_ref[...]
        pre_ref[rows, :] = pre
        hidden = gelu_tanh(pre).astype(BF)
        hidden_ref[rows, :] = hidden
        share = dot_nt(hidden, down_ref[...])
        if from_ref is other_ref:
            share_ref[...] = share.astype(BF)
        else:
            own_share_ref[...] = share


def gelu_slope(values):
    inner = jnp.tanh(GELU_COEFF * (values + 0.044715 * values * values * values))
    slope = GELU_COEFF * (1.0 + 3.0 * 0.044715 * values * values)
    return 0.5 * (1.0 + inner) + 0.5 * values * (1.0 - inner * inner) * slope


def mlp_backward_body(
    own_ref, other_ref, up_ref, down_ref, pre_ref, grad_ref, bias_ref, share_ref, own_share_ref
):
    half = own_ref.shape[0]
    total = jnp.zeros(bias_ref.shape, F32)
    for rows, from_ref in ((slice(half, None), other_ref), (slice(0, half), own_ref)):
        grad = (dot(from_ref[...], down_ref[...]) * gelu_slope(pre_ref[rows, :])).astype(BF)
        grad_ref[rows, :] = grad
        total = total + jnp.sum(grad.astype(F32), axis=0, keepdims=True)
        share = dot_nt(grad, up_ref[...])
        if from_ref is other_ref:
            share_ref[...] = share.astype(BF)
        else:
            own_share_ref[...] = share
    bias_ref[...] = total


def attention_backward_body(
    heads, size, near_ref, own_ref, other_ref, weight_ref, qkv_ref, total_ref,
    grad_ref, bias_ref, share_ref, own_share_ref, grad_out_ref, key_ref, value_ref,
):
    half, part = own_ref.shape[0], heads * size
    scale = size ** (-0.5)
    first = near_ref[0] == 0
    proj = weight_ref[:, 3 * part : 4 * part]
    own = dot(own_ref[...], proj)
    other = dot(other_ref[...], proj)
    grad_out_ref[:half, :] = jnp.where(first, own, other).astype(BF)
    grad_out_ref[half:, :] = jnp.where(first, other, own).astype(BF)
    spots = [pl.multiple_of((near_ref[0] ^ block) * half, half) for block in range(2)]
    for head in range(heads):
        at = [slice(i * part + head * size, i * part + (head + 1) * size) for i in range(3)]
        for block in range(2):
            rows = slice(block * half, (block + 1) * half)
            seen = (block + 1) * half
            q = qkv_ref[rows, at[0]]
            k = qkv_ref[:seen, at[1]]
            v = qkv_ref[:seen, at[2]]
            grad_out = grad_out_ref[rows, at[0]]
            probs = jnp.exp(masked_scores(q, k, block * half) - total_ref[rows, head : head + 1])
            grad_probs = dot_nt(grad_out, v)
            inner = jnp.sum(probs * grad_probs, axis=-1, keepdims=True)
            grad_scores = (probs * (grad_probs - inner) * scale).astype(BF)
            grad_ref[pl.ds(spots[block], half), at[0]] = dot(grad_scores, k).astype(BF)
            grad_k = dot_tn(grad_scores, q)
            grad_v = dot_tn(probs.astype(BF), grad_out)
            if block == 0:
                key_ref[...] = grad_k
                value_ref[...] = grad_v
            else:
                for side in range(2):
                    part_rows = slice(side * half, (side + 1) * half)
                    whole_k, whole_v = grad_k[part_rows], grad_v[part_rows]
                    if side == 0:
                        whole_k = whole_k + key_ref[...]
                        whole_v = whole_v + value_ref[...]
                    grad_ref[pl.ds(spots[side], half), at[1]] = whole_k.astype(BF)
                    grad_ref[pl.ds(spots[side], half), at[2]] = whole_v.astype(BF)
    bias_ref[...] = jnp.sum(grad_ref[...].astype(F32), axis=0, keepdims=True)
    attn = weight_ref[:, : 3 * part]
    share_ref[...] = dot_nt(grad_ref[half:, :], attn).astype(BF)
    own_share_ref[...] = dot_nt(grad_ref[:half, :], attn)


def padded_width(width):
    return -(-width // 128) * 128


def put(out_ref, value):
    width = value.shape[1]
    out_ref[:, :width] = value.astype(out_ref.dtype)
    if out_ref.shape[1] > width:
        out_ref[:, width:] = jnp.zeros((value.shape[0], out_ref.shape[1] - width), out_ref.dtype)


def weave_body(minor_ref, mine_ref, theirs_ref, out_ref):
    first = minor_ref[0] == 0
    out_ref[0, 0] = jnp.where(first, mine_ref[0], theirs_ref[0])
    out_ref[0, 1] = jnp.where(first, theirs_ref[0], mine_ref[0])


def weave_call(minor, mine, theirs, start, rows, moved):
    majors, _, cols = mine.shape
    block = pl.BlockSpec(
        (pl.Element(1), pl.Element(rows), pl.Element(cols)), lambda k: (k, start, 0)
    )
    return pl.pallas_call(
        weave_body,
        grid=(majors,),
        out_shape=jax.ShapeDtypeStruct((majors, 2, rows, cols), mine.dtype),
        in_specs=[pl.BlockSpec(memory_space=pltpu.SMEM), block, block],
        out_specs=pl.BlockSpec((1, 2, rows, cols), lambda k: (k, 0, 0, 0)),
        compiler_params=pltpu.CompilerParams(vmem_limit_bytes=16 << 20),
        cost_estimate=pl.CostEstimate(flops=10**5, transcendentals=0, bytes_accessed=moved),
    )(minor, mine, theirs).reshape(majors * 2 * rows, cols)


def up_body(own_ref, other_ref, weight_ref, bias_ref, out_ref):
    half = own_ref.shape[0]
    depth = weight_ref.shape[0]
    for rows, from_ref in ((slice(half, None), other_ref), (slice(0, half), own_ref)):
        pre = dot(from_ref[:, :depth], weight_ref[...]) + bias_ref[...]
        out_ref[rows, :] = gelu_tanh(pre).astype(BF)


def down_body(hidden_ref, weight_ref, share_ref, own_share_ref):
    half = share_ref.shape[0]
    put(share_ref, dot_nt(hidden_ref[half:, :], weight_ref[...]))
    put(own_share_ref, dot_nt(hidden_ref[:half, :], weight_ref[...]))


def norm_forward_body(stream_ref, pair_ref, far_ref, bias_ref, gain_ref, shift_ref, new_ref, out_ref):
    width = stream_ref.shape[1]
    new = (
        stream_ref[...]
        + (pair_ref[:, :width].astype(F32) + far_ref[:, :width].astype(F32))
        + bias_ref[...]
    )
    new_ref[...] = new
    put(out_ref, layer_norm(new, gain_ref[...], shift_ref[...]))


def norm_backward_body(values_ref, gain_ref, pair_ref, far_ref, *refs):
    *top_ref, new_ref, low_ref, sums_ref = refs
    grad = pair_ref[...].astype(F32) + far_ref[...].astype(F32)
    values = values_ref[...]
    centered = values - jnp.mean(values, axis=-1, keepdims=True)
    variance = jnp.mean(centered * centered, axis=-1, keepdims=True)
    scale = lax.rsqrt(variance + EPSILON)
    unit = centered * scale
    inner = grad * gain_ref[...]
    new = scale * (
        inner
        - jnp.mean(inner, axis=-1, keepdims=True)
        - unit * jnp.mean(inner * unit, axis=-1, keepdims=True)
    )
    if top_ref:
        new = top_ref[0][...] + new
    new_ref[...] = new
    low_ref[...] = new.astype(BF)
    sums_ref[0:1, :] = jnp.sum(grad * unit, axis=0, keepdims=True)
    sums_ref[1:2, :] = jnp.sum(grad, axis=0, keepdims=True)
    sums_ref[2:3, :] = jnp.sum(new, axis=0, keepdims=True)
    sums_ref[3:, :] = jnp.zeros_like(sums_ref[3:, :])


def norm_forward(stream, pair, far, bias, gain, shift):
    return kernel_call(
        norm_forward_body,
        [(stream.shape, F32), (pair.shape, BF)],
        [stream, pair, far, bias[None], gain[None], shift[None]],
        vmem=16 << 20,
    )


def norm_backward(values, gain, pair, far, *top):
    return kernel_call(
        norm_backward_body,
        [(values.shape, F32), (values.shape, BF), ((8, values.shape[1]), F32)],
        [values, gain[None], pair, far, *top],
        vmem=16 << 20,
    )


def weight_grad_body(shape, count, minor_ref, *refs):
    majors, minors, rows = shape
    operands, (mine_ref, theirs_ref, sum_ref) = refs[: 3 * count], refs[3 * count :]
    start = 0
    for at in range(count):
        own, other, grad = operands[3 * at : 3 * at + 3]
        half, cols = own.shape[0], grad.shape[1]
        sum_ref[:, start : start + cols] = dot_tn(own[...], grad[:half, :]) + dot_tn(
            other[...], grad[half:, :]
        )
        start += cols
    for k in range(majors):
        to = slice(k * rows, (k + 1) * rows)
        here = pl.multiple_of((k * minors + minor_ref[0]) * rows, 8)
        there = pl.multiple_of((k * minors + 1 - minor_ref[0]) * rows, 8)
        mine_ref[to, :] = sum_ref[pl.ds(here, rows), :]
        theirs_ref[to, :] = sum_ref[pl.ds(there, rows), :].astype(BF)


STATS = 8


def logits_body(
    place_ref, teacher_ref, student_ref, teacher_head_ref, head_ref, t_ref, z_ref, stats_ref
):
    counted = place_ref[1 + pl.program_id(0)] > place_ref[0]

    @pl.when(counted)
    def _():
        t = dot(teacher_ref[:, : teacher_head_ref.shape[0]], teacher_head_ref[...])
        t_ref[...] = t
        z = dot(student_ref[...], head_ref[...])
        z_ref[...] = z
        t_peak = jnp.max(t, axis=-1, keepdims=True)
        t_exp = jnp.exp(t - t_peak)
        z_peak = jnp.max(z, axis=-1, keepdims=True)
        columns = (
            t_peak,
            jnp.sum(t_exp, axis=-1, keepdims=True),
            jnp.sum(t_exp * (t - z), axis=-1, keepdims=True),
            z_peak,
            jnp.sum(jnp.exp(z - z_peak), axis=-1, keepdims=True),
        )
        lane = lax.broadcasted_iota(jnp.int32, (t.shape[0], 128), 1)
        packed = jnp.zeros(lane.shape, F32)
        for at, column in enumerate(columns):
            packed = jnp.where(lane == at, column, packed)
        stats_ref[...] = packed.T[:STATS, :]

    @pl.when(jnp.logical_not(counted))
    def _():
        row = lax.broadcasted_iota(jnp.int32, stats_ref.shape, 0)
        stats_ref[...] = jnp.where((row == 1) | (row == 4), 1.0, 0.0)


def merge_body(*refs):
    *in_refs, out_ref = refs
    many = [ref[...] for ref in in_refs]
    if many[0].ndim == 3:
        many = [many[0][k] for k in range(many[0].shape[0])]
    t_high = functools.reduce(jnp.maximum, [one[0:1] for one in many])
    z_high = functools.reduce(jnp.maximum, [one[3:4] for one in many])
    t_scale = [jnp.exp(one[0:1] - t_high) for one in many]
    z_scale = [jnp.exp(one[3:4] - z_high) for one in many]
    out_ref[0:1, :] = t_high
    out_ref[1:2, :] = sum(one[1:2] * scale for one, scale in zip(many, t_scale))
    out_ref[2:3, :] = sum(one[2:3] * scale for one, scale in zip(many, t_scale))
    out_ref[3:4, :] = z_high
    out_ref[4:5, :] = sum(one[4:5] * scale for one, scale in zip(many, z_scale))
    out_ref[5:, :] = jnp.zeros_like(out_ref[5:, :])


def logits_back_body(place_ref, weight_ref, t_ref, z_ref, stats_ref, head_ref, *refs):
    out_ref = refs[-1]
    length = place_ref[1 + pl.program_id(0)]

    @pl.when(length > place_ref[0])
    def _():
        stats = stats_ref[...]
        row = lax.broadcasted_iota(jnp.int32, stats.shape, 0)
        logs = jnp.log(jnp.where((row == 1) | (row == 4), stats, 1.0))
        totals = stats + pltpu.roll(logs, STATS - 1, 0)
        totals = jnp.concatenate([totals] * (128 // STATS), axis=0).T
        rows = t_ref.shape[0]
        position = place_ref[0] + lax.broadcasted_iota(jnp.int32, (rows, 1), 0)
        weight = jnp.where(position < length, weight_ref[0], 0.0)
        grad = (jnp.exp(z_ref[...] - totals[:, 3:4]) - jnp.exp(t_ref[...] - totals[:, 0:1])) * weight
        share = dot_nt(grad.astype(BF), head_ref[...])
        if len(refs) == 2:
            share = share + refs[0][...].astype(F32)
        out_ref[...] = share.astype(BF)

    @pl.when(length <= place_ref[0])
    def _():
        out_ref[...] = jnp.zeros_like(out_ref) if len(refs) == 1 else refs[0][...]


def row_blocks(rows, cols):
    return pl.BlockSpec((rows, cols), lambda i: (i, 0))


def held_block(array):
    return pl.BlockSpec(array.shape, lambda i: (0, 0), pipeline_mode=pl.Buffered(1))


def stat_blocks(rows):
    return pl.BlockSpec((STATS, rows), lambda i: (0, i))


SCALAR = pl.BlockSpec(memory_space=pltpu.SMEM)


def logits_call(place, teacher, student, teacher_head, head):
    tokens = teacher.shape[0]
    rows, vocab = tokens // MAJOR, head.shape[1]
    return pl.pallas_call(
        logits_body,
        grid=(MAJOR,),
        out_shape=[
            jax.ShapeDtypeStruct((tokens, vocab), F32),
            jax.ShapeDtypeStruct((tokens, vocab), F32),
            jax.ShapeDtypeStruct((STATS, tokens), F32),
        ],
        in_specs=[
            SCALAR,
            row_blocks(rows, teacher.shape[1]),
            row_blocks(rows, student.shape[1]),
            held_block(teacher_head),
            held_block(head),
        ],
        out_specs=[row_blocks(rows, vocab), row_blocks(rows, vocab), stat_blocks(rows)],
        compiler_params=pltpu.CompilerParams(vmem_limit_bytes=44 << 20),
        cost_estimate=pl.CostEstimate(
            flops=10**6,
            transcendentals=0,
            bytes_accessed=10**5,
        ),
    )(place, teacher, student, teacher_head, head)


def logits_back_call(place, weight, t, z, stats, head, *more):
    tokens, vocab = t.shape
    rows, width = tokens // MAJOR, head.shape[0]
    return pl.pallas_call(
        logits_back_body,
        grid=(MAJOR,),
        out_shape=jax.ShapeDtypeStruct((tokens, width), BF),
        in_specs=[
            SCALAR,
            SCALAR,
            row_blocks(rows, vocab),
            row_blocks(rows, vocab),
            stat_blocks(rows),
            held_block(head),
            *[row_blocks(rows, width) for _ in more],
        ],
        out_specs=row_blocks(rows, width),
        compiler_params=pltpu.CompilerParams(vmem_limit_bytes=40 << 20),
        cost_estimate=pl.CostEstimate(
            flops=10**6,
            transcendentals=0,
            bytes_accessed=10**5,
        ),
    )(place, weight, t, z, stats, head, *more)


def merged(*many):
    return pl.pallas_call(
        merge_body, out_shape=jax.ShapeDtypeStruct(many[0].shape[-2:], F32)
    )(*many)


def adam_update(weight, first, second, average, grad, clip, rate, decay):
    keep = min(0.995, (1.0 + STEP) / (10.0 + STEP))
    grad = grad * clip
    first_new = BETA_ONE * first + (1.0 - BETA_ONE) * grad
    second_new = BETA_TWO * second + (1.0 - BETA_TWO) * grad * grad
    first_hat = first_new / (1.0 - BETA_ONE**STEP)
    second_hat = second_new / (1.0 - BETA_TWO**STEP)
    weight_new = weight - rate * (
        first_hat / (jnp.sqrt(second_hat) + ADAM_EPSILON) + decay * weight
    )
    average_new = keep * average + (1.0 - keep) * weight_new
    return (weight_new, first_new, second_new, average_new)


def tie(first, second):
    return lax.optimization_barrier((first, second))


SCALARS = 6


def pack_body(mp, mp_ref, final_ref, *refs):
    *layer_refs, out_ref, line_ref = refs
    devices, groups = out_ref.shape[0], out_ref.shape[0] // mp
    rows, lines = [], len(layer_refs) // 5
    for at in range(lines):
        middle, inner, above, qkv, up = layer_refs[5 * at : 5 * at + 5]
        rows += [(inner, 0), (inner, 1), (middle, 2), (middle, 0), (middle, 1), (above, 2)]
        part = qkv.shape[1] // 3
        line_ref[at : at + 1, :part] = qkv[:, :part]
        line_ref[at : at + 1, part : 2 * part] = qkv[:, 2 * part :]
        line_ref[at : at + 1, 2 * part :] = up[...]
    rows += [(final_ref, 0), (final_ref, 1)]
    out_ref[...] = jnp.zeros_like(out_ref)
    blocks = final_ref.shape[1] // 128
    each = -(-len(rows) * blocks // devices)
    for at, (ref, row) in enumerate(rows):
        for block in range(blocks):
            to = at * blocks + block
            out_ref[to // each, to % each : to % each + 1, :] = (
                0.5 * ref[row : row + 1, 128 * block : 128 * (block + 1)]
            )
    blocks = line_ref.shape[1] // 128
    own_each = -(-lines * blocks // groups)
    for at in range(lines * blocks):
        line, block = divmod(at, blocks)
        value = line_ref[line : line + 1, 128 * block : 128 * (block + 1)]
        row = each + at % own_each
        for m in range(mp):
            out_ref[at // own_each * mp + m, row : row + 1, :] = jnp.where(
                mp_ref[0] == m, value, 0.0
            )


def square_body(loss_ref, packets_ref, *refs):
    *grad_refs, out_ref = refs
    devices = packets_ref.shape[0]
    total = packets_ref[0]
    for at in range(1, devices):
        total = total + packets_ref[at]
    squares = jnp.sum(total * total)
    for ref in grad_refs:
        grad = ref[...].astype(F32)
        squares = squares + jnp.sum(grad * grad)
    row = lax.broadcasted_iota(jnp.int32, total.shape, 0)
    lane = lax.broadcasted_iota(jnp.int32, total.shape, 1)
    total = jnp.where((row == SCALARS) & (lane == 0), squares, total)
    total = jnp.where((row == SCALARS) & (lane == 1), loss_ref[0], total)
    for at in range(devices):
        out_ref[at] = total


def scalar_body(packets_ref, scalar_ref):
    devices = packets_ref.shape[0]
    sums = packets_ref[0, SCALARS : SCALARS + 1, :]
    for at in range(1, devices):
        sums = sums + packets_ref[at, SCALARS : SCALARS + 1, :]
    norm = jnp.sqrt(sums[:, 0:1])
    clip = CLIP_LIMIT / jnp.maximum(norm, CLIP_LIMIT)
    row = lax.broadcasted_iota(jnp.int32, scalar_ref.shape, 0)
    scalar_ref[...] = jnp.where(row == 0, clip, jnp.where(row == 1, norm, sums[:, 1:2]))


def small_update_body(mp, mp_ref, packets_ref, scalar_ref, *refs):
    states, outs = refs[:12], refs[12:24]
    line_ref, grad_ref = refs[24:]
    devices, groups = packets_ref.shape[0], packets_ref.shape[0] // mp
    clip = scalar_ref[0:1, 0:1]
    kinds, layers, width = states[0].shape
    blocks = width // 128
    each = -(-(layers * kinds + 2) * blocks // devices)
    for at in range(layers * kinds + 2):
        for block in range(blocks):
            source = at * blocks + block
            grad_ref[at : at + 1, 128 * block : 128 * (block + 1)] = packets_ref[
                source // each, source % each : source % each + 1, :
            ]

    def update(kind, pick, grad, rate):
        values = [ref[pick] for ref in states[4 * kind : 4 * kind + 4]]
        for ref, value in zip(
            outs[4 * kind : 4 * kind + 4], adam_update(*values, grad, clip, rate, 0.0)
        ):
            ref[pick] = value

    for layer in range(layers):
        update(0, (slice(None), layer), grad_ref[layer * kinds : (layer + 1) * kinds, :], 0.5)
    update(1, slice(None), grad_ref[layers * kinds : layers * kinds + 2, :], 0.5)
    part = states[8].shape[2]
    blocks = line_ref.shape[1] // 128
    own_each = -(-layers * blocks // groups)
    for at in range(layers * blocks):
        line, block = divmod(at, blocks)
        source = at // own_each * mp + mp_ref[0]
        from_row = each + at % own_each
        line_ref[line : line + 1, 128 * block : 128 * (block + 1)] = packets_ref[
            pl.ds(source, 1), from_row : from_row + 1, :
        ].reshape(1, 128)
    for layer in range(layers):
        grad = jnp.concatenate(
            [
                line_ref[layer : layer + 1, part * at : part * (at + 1)]
                for at in range(states[8].shape[0])
            ],
            axis=0,
        )
        update(2, (slice(None), layer), grad, 0.1)


class Wires:
    def __init__(self):
        self.dp = lax.axis_size("dp")
        self.mp = lax.axis_size("mp")
        self.minors = self.dp // MAJOR
        self.dp_at = lax.axis_index("dp")
        self.mp_at = lax.axis_index("mp")
        self.major = self.dp_at // self.minors
        self.minor = self.dp_at % self.minors
        self.near_at = self.mp_at % 2
        self.near_ref = self.near_at.reshape(1).astype(jnp.int32)
        self.minor_ref = self.minor.reshape(1).astype(jnp.int32)
        self.near_pairs = [(i, i ^ 1) for i in range(self.mp)]
        self.far_pairs = [(i, i ^ 2) for i in range(self.mp)]
        self.over_major = [
            [k * self.minors + j for k in range(MAJOR)] for j in range(self.minors)
        ]
        self.over_minor = [
            [k * self.minors + j for j in range(self.minors)] for k in range(MAJOR)
        ]

    def near(self, part):
        return lax.ppermute(part, "mp", self.near_pairs)

    def far(self, part):
        return lax.ppermute(part, "mp", self.far_pairs)

    def natural(self, own, other):
        first = self.near_at == 0
        return jnp.concatenate([jnp.where(first, own, other), jnp.where(first, other, own)], axis=0)

    def own_first(self, whole):
        half = whole.shape[0] // 2
        own = lax.dynamic_slice_in_dim(whole, self.near_at * half, half, 0)
        other = lax.dynamic_slice_in_dim(whole, (1 - self.near_at) * half, half, 0)
        return own, other

    def across(self, part):
        return lax.ppermute(part, "mp", [(i, i ^ 3) for i in range(self.mp)])

    def shares(self, other, own):
        pair = (own + self.near(other.astype(BF)).astype(F32)).astype(BF)
        return pair, self.far(pair)

    def minor_parts(self, part):
        if self.minors == 2:
            return lax.ppermute(part, "dp", [(i, i ^ 1) for i in range(self.dp)])
        return lax.all_gather(part, "dp", axis=0, axis_index_groups=self.over_minor)

    def minor_stack(self, part, others, axis):
        if self.minors == 2:
            first = self.minor == 0
            return jnp.stack(
                [jnp.where(first, part, others), jnp.where(first, others, part)], axis=axis
            )
        return jnp.moveaxis(others, 0, axis)

    def major_gather(self, part):
        return lax.all_gather(
            part, "dp", axis=0, tiled=True, axis_index_groups=self.over_major
        )

    def minor_joined(self, part):
        return self.minor_stack(part, self.minor_parts(part), 0).reshape(-1, part.shape[-1])

    def minor_woven(self, part, others, start=0, rows=None, moved=10**5):
        rows = part.shape[1] if rows is None else rows
        if self.minors == 2:
            return weave_call(self.minor_ref, part, others, start, rows, moved)
        stacked = self.minor_stack(part, others, 1)[:, :, start : start + rows]
        return stacked.reshape(-1, part.shape[-1])

    def major_swap(self, part):
        return lax.all_to_all(part, "dp", 0, 0, axis_index_groups=self.over_major)

    def grad_started(self, *products):
        width, cols = products[0][0].shape[1], sum(grad.shape[1] for _, _, grad in products)
        rows = width // self.dp
        if self.minors == 2 and rows % 8 == 0:
            mine, theirs = kernel_call(
                functools.partial(
                    weight_grad_body, (MAJOR, self.minors, rows), len(products)
                ),
                [((MAJOR * rows, cols), F32), ((MAJOR * rows, cols), BF)],
                [self.minor_ref, *sum(([*product] for product in products), [])],
                scratch=[pltpu.VMEM((width, cols), F32)],
                vmem=40 << 20,
                flops=2 * 2 * products[0][0].shape[0] * width * cols,
            )
            return mine, self.minor_parts(theirs)
        total = jnp.concatenate(
            [dot_tn(jnp.concatenate(product[:2]), product[2]) for product in products], axis=1
        )
        held = lax.psum_scatter(
            total.reshape(MAJOR, self.minors, rows, cols).astype(BF),
            "dp",
            scatter_dimension=1,
            axis_index_groups=self.over_minor,
        )
        return held.reshape(-1, cols).astype(F32), None

    def grad_ended(self, mine, theirs, direct=False):
        held = (mine if theirs is None else mine + theirs.astype(F32)).astype(BF)
        if direct:
            held = self.major_swap(held.reshape(MAJOR, -1, held.shape[-1]))
            return jnp.sum(held.astype(F32), axis=0)
        return lax.psum_scatter(
            held, "dp", scatter_dimension=0, tiled=True, axis_index_groups=self.over_major
        )


def local(
    inputs,
    lengths,
    teacher_inputs,
    teacher_qkv,
    teacher_proj,
    teacher_up,
    teacher_up_bias,
    teacher_down,
    teacher_vectors,
    teacher_head,
    head,
    column_weights,
    column_first,
    column_second,
    column_average,
    row_weights,
    row_first,
    row_second,
    row_average,
    column_biases,
    bias_first,
    bias_second,
    bias_average,
    norm_vectors,
    vector_first,
    vector_second,
    vector_average,
    final_norm,
    final_first,
    final_second,
    final_average,
):
    wires = Wires()
    token_count, width = inputs.shape
    half = token_count // 2
    teacher_width = teacher_inputs.shape[1]
    layers, shard_rows, col_blocks, part = column_weights.shape
    up_blocks = col_blocks - 3
    units = up_blocks * part

    slots = -(-THEADS // wires.mp)
    base_heads = THEADS // wires.mp
    extra_heads = THEADS % wires.mp
    own_start = wires.mp_at * base_heads + jnp.minimum(wires.mp_at, extra_heads)
    own_stop = own_start + base_heads + jnp.where(wires.mp_at < extra_heads, 1, 0)
    slot_start = jnp.minimum(own_start, THEADS - slots)
    head_ids = slot_start + jnp.arange(slots, dtype=jnp.int32)
    owned = ((head_ids >= own_start) & (head_ids < own_stop)).astype(jnp.int32)
    slot_width = slots * THD
    first_col = slot_start * THD

    qkv_shard = lax.dynamic_slice_in_dim(teacher_qkv, first_col, slot_width, 2)
    proj_shard = lax.dynamic_slice_in_dim(teacher_proj, first_col, slot_width, 0).T
    shards = []
    for layer in range(layers):
        cols = column_weights[layer].astype(BF)
        rows = row_weights[layer].astype(BF)
        shards.append(
            jnp.concatenate(
                [
                    cols[:, 3:].reshape(shard_rows, units),
                    rows[1:].reshape(units, shard_rows).T,
                    cols[:, :3].reshape(shard_rows, 3 * part),
                    rows[0].T,
                ],
                axis=1,
            )
        )
    shards.extend(
        [
            jnp.concatenate([qkv_shard.reshape(-1, 3 * slot_width), proj_shard], axis=1),
            teacher_up,
            teacher_down.T,
        ]
    )
    own_at = wires.near_at * half
    tv = teacher_vectors
    teacher_pad = padded_width(teacher_width)
    teacher_stream, teacher_other = (
        lax.dynamic_slice_in_dim(teacher_inputs, at, half, 0).astype(F32)
        for at in (own_at, half - own_at)
    )
    query_bias, value_bias = (
        lax.dynamic_slice_in_dim(tv[at], first_col, slot_width) for at in (2, 3)
    )
    teacher_start = (
        layer_norm(teacher_stream, tv[0], tv[1]).astype(BF),
        layer_norm(teacher_other, tv[0], tv[1]).astype(BF),
        jnp.concatenate([query_bias, jnp.zeros_like(query_bias), value_bias])[None],
    )

    held, rows, others = [], [], []

    def launch(mark):
        shard = shards[len(held)]
        if mark is not None:
            shard, mark = tie(shard, mark)
        if held:
            shard, rows[-1] = tie(shard, held[-1])
        held.append(wires.major_gather(shard).reshape(MAJOR, *shard.shape))
        rows.append(held[-1])
        others.append(wires.minor_parts(held[-1]))
        return mark

    for _ in range(layers):
        launch(None)
    vocab_part = head.shape[1] // MAJOR
    cut = teacher_head.shape[0]
    both = jnp.stack(
        [
            jnp.concatenate(
                [rows_[:, k * vocab_part : (k + 1) * vocab_part] for rows_ in (teacher_head, head)],
                axis=0,
            )
            for k in range(MAJOR)
        ]
    )

    stream = lax.dynamic_slice_in_dim(inputs, own_at, half, 0).astype(F32)
    heads = part // HD
    all_heads = jnp.ones((heads,), jnp.int32)

    layer_full = []

    def columns(layer, at):
        return (layer_full[layer], (width, units), (0, at))

    saved = []
    one_own = layer_norm(stream, norm_vectors[0, 0], norm_vectors[0, 1]).astype(BF)
    one_own, (teacher_stream, teacher_start, both, *shards[layers:]) = tie(
        one_own, (teacher_stream, teacher_start, both, *shards[layers:])
    )
    for layer in range(layers):
        vector = norm_vectors[layer]
        layer_full.append(wires.minor_woven(rows[layer], others[layer]))
        if layer == 0:
            layer_full[0] = launch(layer_full[0])
        one = (one_own, wires.near(one_own))
        bias = column_biases[layer]
        share, own_share, attended, qkv, totals = kernel_call(
            functools.partial(attention_forward_body, heads, HD),
            [
                ((half, width), BF),
                ((half, width), F32),
                ((token_count, part), BF),
                ((token_count, 3 * part), BF),
                ((token_count, 128), F32),
            ],
            [
                wires.near_ref,
                all_heads,
                *one,
                columns(layer, 2),
                jnp.concatenate([bias[0], jnp.zeros_like(bias[0]), bias[1]])[None],
            ],
        )
        middle, two_own = norm_forward(
            stream, *wires.shares(share, own_share), vector[2], vector[3], vector[4]
        )
        two = (two_own, wires.near(two_own))
        pre_act, hidden, share, own_share = kernel_call(
            mlp_forward_body,
            [
                ((token_count, units), F32),
                ((token_count, units), BF),
                ((half, width), BF),
                ((half, width), F32),
            ],
            [*two, columns(layer, 0), columns(layer, 1), bias[2:].reshape(1, units)],
        )
        saved.append((stream, one, qkv, totals, attended, middle, two, pre_act, hidden))
        later = norm_vectors[layer + 1] if layer + 1 < layers else final_norm
        parts, others[layer + 1] = tie(wires.shares(share, own_share), others[layer + 1])
        stream, one_own = norm_forward(middle, *parts, vector[5], later[0], later[1])
        if len(held) < len(shards):
            one_own = launch(one_own)
    final_out = one_own
    while len(held) < len(shards):
        launch(None)
    (mine, theirs), rows[-2] = tie((rows[-3], others[-3]), rows[-2])
    teacher_attn = wires.minor_woven(mine, theirs)
    teacher_share, teacher_own_share = kernel_call(
        functools.partial(attention_forward_body, slots, THD),
        [((half, teacher_pad), BF), ((half, teacher_pad), F32)],
        [
            wires.near_ref,
            owned,
            *teacher_start[:2],
            teacher_attn,
            teacher_start[2],
        ],
        scratch=[
            pltpu.VMEM((token_count, slot_width), BF),
            pltpu.VMEM((token_count, 3 * slot_width), BF),
            pltpu.VMEM((token_count, 128), F32),
        ],
        vmem=36 << 20,
    )
    both, early = tie(both, others[-2])
    parts, others[-2] = tie(wires.shares(teacher_share, teacher_own_share), early)
    both, rows[-1] = tie(both, rows[-1])
    both = wires.major_swap(both)
    both_others = wires.minor_parts(both)
    final_out, rows[-1] = tie(final_out, rows[-1])
    student_rows = wires.major_gather(final_out)
    teacher_up_full = wires.minor_woven(rows[-2], others[-2])
    teacher_mid, normed_own = norm_forward(teacher_stream, *parts, tv[4], tv[5], tv[6])
    (hidden,) = kernel_call(
        up_body,
        [((token_count, teacher_up.shape[1]), BF)],
        [normed_own, wires.near(normed_own), teacher_up_full, teacher_up_bias[None]],
        vmem=32 << 20,
    )
    share, own_share = kernel_call(
        down_body,
        [((half, teacher_pad), BF), ((half, teacher_pad), F32)],
        [hidden, wires.minor_woven(rows[-1], others[-1])],
        vmem=32 << 20,
    )
    _, teacher_final = norm_forward(
        teacher_mid, *wires.shares(share, own_share), tv[7], tv[8], tv[9]
    )
    teacher_final, student_rows = tie(teacher_final, student_rows)
    teacher_rows, both_others = tie(wires.major_gather(teacher_final), both_others)
    teacher_head_part = wires.minor_woven(both, both_others, 0, cut)
    head_part = wires.minor_woven(both, both_others, cut, head.shape[0])

    teacher_sides = (teacher_rows, wires.near(teacher_rows))
    student_sides = (student_rows, wires.near(student_rows))
    row_ids = jnp.arange(MAJOR, dtype=jnp.int32) * wires.minors + wires.minor
    row_lengths = jnp.sum(
        jnp.where(
            row_ids[:, None] == jnp.arange(lengths.shape[0], dtype=jnp.int32)[None, :],
            lengths[None, :],
            0,
        ),
        axis=1,
    )
    places = [
        jnp.concatenate([start.reshape(1).astype(jnp.int32), row_lengths])
        for start in (own_at, half - own_at)
    ]
    row_weight = 1.0 / jnp.sum(lengths).astype(F32)
    sides = [
        logits_call(place, teacher, student, teacher_head_part, head_part)
        for place, teacher, student in zip(places, teacher_sides, student_sides)
    ]
    own_stats, other_stats = sides[0][2], sides[1][2]
    stats = merged(
        own_stats, wires.near(other_stats), wires.far(own_stats), wires.across(other_stats)
    )
    stats = merged(
        wires.major_swap(jnp.broadcast_to(stats[None], (MAJOR, *stats.shape)))
    )
    other_stats = wires.near(stats)
    divergence = (
        stats[2] / stats[1] - (stats[0] + jnp.log(stats[1])) + (stats[3] + jnp.log(stats[4]))
    ).reshape(MAJOR, half)
    counted = own_at + jnp.arange(half, dtype=jnp.int32)[None, :] < row_lengths[:, None]
    loss_part = jnp.sum(jnp.where(counted, divergence, 0.0)) * (
        row_weight * (2.0 / (MAJOR * wires.mp))
    )

    weight = row_weight.reshape(1)
    share = logits_back_call(places[1], weight, *sides[1][:2], other_stats, head_part)
    share = logits_back_call(
        places[0], weight, *sides[0][:2], stats, head_part, wires.near(share)
    )
    share = wires.major_swap(share.reshape(MAJOR, half, width))
    share = jnp.sum(share.astype(F32), axis=0).astype(BF)
    grad_stream, out_own, final_sums = norm_backward(
        stream, final_norm[0], share, wires.far(share)
    )
    small_sums = []
    products, started, ended = [], [], []

    def start(parts):
        mine, theirs = wires.grad_started(*products)
        parts, mine = tie(parts, mine)
        started.append((mine, theirs))
        products.clear()
        return parts

    def passed(parts, count):
        for mine, theirs in started[len(ended) : count]:
            if theirs is not None:
                parts, theirs = tie(parts, theirs)
            if ended:
                mine, ended[-1] = tie(mine, ended[-1])
            ended.append(wires.grad_ended(mine, theirs))
        return parts

    above = final_sums
    for layer in reversed(range(layers)):
        layer_in, one, qkv, totals, attended, middle, two, pre_act, hidden = saved[layer]
        vector = norm_vectors[layer]
        out = (out_own, wires.near(out_own))
        grad_pre, up_sums, share, own_share = kernel_call(
            mlp_backward_body,
            [
                ((token_count, units), BF),
                ((1, units), F32),
                ((half, width), BF),
                ((half, width), F32),
            ],
            [*out, columns(layer, 0), columns(layer, 1), pre_act],
        )
        share = passed(share, 2 * (layers - 1 - layer) - 1)
        parts = wires.shares(share, own_share)
        products.extend([(*two, grad_pre), (*out, hidden)])
        parts = start(parts)
        grad_middle, mid_own, middle_sums = norm_backward(
            middle, vector[3], *parts, grad_stream
        )
        mid = (mid_own, wires.near(mid_own))
        grad_qkv, qkv_sums, share, own_share = kernel_call(
            functools.partial(attention_backward_body, heads, HD),
            [
                ((token_count, 3 * part), BF),
                ((1, 3 * part), F32),
                ((half, width), BF),
                ((half, width), F32),
            ],
            [wires.near_ref, *mid, columns(layer, 2), qkv, totals],
            scratch=[
                pltpu.VMEM((token_count, part), BF),
                pltpu.VMEM((half, HD), F32),
                pltpu.VMEM((half, HD), F32),
            ],
        )
        share = passed(share, 2 * (layers - 1 - layer))
        parts = wires.shares(share, own_share)
        products.extend([(*one, grad_qkv), (*mid, attended)])
        parts = start(parts)
        grad_stream, out_own, in_sums = norm_backward(
            layer_in, vector[0], *parts, grad_middle
        )
        small_sums.insert(0, [middle_sums, in_sums, above, qkv_sums, up_sums])
        above = in_sums
    input_grad = wires.natural(grad_stream, wires.near(grad_stream))
    everyone = wires.dp * wires.mp
    mp_ref = wires.mp_at.reshape(1).astype(jnp.int32)
    packet = (everyone, 8, 128)
    (packets,) = kernel_call(
        functools.partial(pack_body, wires.mp),
        [(packet, F32)],
        [mp_ref, final_sums, *sum(small_sums, [])],
        scratch=[pltpu.VMEM((layers, (2 + up_blocks) * part), F32)],
        vmem=8 << 20,
    )
    packets = lax.all_to_all(packets, ("dp", "mp"), 0, 0)
    for at in range(len(ended), len(started)):
        mine, theirs = started[at]
        if at == 2 * layers - 2:
            mine, ended[-1] = tie(mine, ended[-1])
            mine, packets = tie(mine, packets)
        if at == 2 * layers - 1:
            mine, ended[-1] = tie(mine, ended[-1])
        ended.append(wires.grad_ended(mine, theirs, direct=at >= 2 * layers - 2))
    squared = ended
    cuts = [units, 2 * units, 2 * units + 3 * part]
    ended = [part_grad.astype(F32) for part_grad in ended]
    ended = [jnp.concatenate(pair, axis=1) for pair in zip(ended[0::2], ended[1::2])][::-1]
    up_shards, down_shards, attn_shards, proj_shards = zip(
        *[jnp.split(whole, cuts, axis=1) for whole in ended]
    )

    (packets,) = kernel_call(
        square_body, [(packet, F32)], [loss_part.reshape(1), packets, *squared], vmem=16 << 20
    )
    packets = lax.all_to_all(packets, ("dp", "mp"), 0, 0)
    states = (
        *(norm_vectors, vector_first, vector_second, vector_average),
        *(final_norm, final_first, final_second, final_average),
        *(column_biases, bias_first, bias_second, bias_average),
    )
    states = [jnp.swapaxes(state, 0, 1) if state.ndim == 3 else state for state in states]
    (scalars,) = kernel_call(scalar_body, [((8, 128), F32)], [packets], vmem=8 << 20)
    small_out = kernel_call(
        functools.partial(small_update_body, wires.mp),
        [(state.shape, F32) for state in states],
        [mp_ref, packets, scalars, *states],
        scratch=[
            pltpu.VMEM((layers, (2 + up_blocks) * part), F32),
            pltpu.VMEM((layers * 6 + 2, width), F32),
        ],
        vmem=16 << 20,
    )
    small_out = [jnp.swapaxes(state, 0, 1) if state.ndim == 3 else state for state in small_out]
    clip, grad_norm, loss_total = scalars[0, 0], scalars[1, 0], scalars[2, 0]

    col_shard = jnp.stack(
        [
            jnp.concatenate(
                [
                    attn_shards[layer].reshape(shard_rows, 3, part),
                    up_shards[layer].reshape(shard_rows, up_blocks, part),
                ],
                axis=1,
            )
            for layer in range(layers)
        ]
    )
    row_shard = jnp.stack(
        [
            jnp.concatenate(
                [
                    proj_shards[layer].T.reshape(1, part, shard_rows),
                    down_shards[layer].T.reshape(up_blocks, part, shard_rows),
                ],
                axis=0,
            )
            for layer in range(layers)
        ]
    )
    column_out = adam_update(
        column_weights, column_first, column_second, column_average, col_shard, clip, 0.1, 0.1
    )
    row_out = adam_update(
        row_weights, row_first, row_second, row_average, row_shard, clip, 0.2, 0.1
    )
    return (
        loss_total,
        grad_norm,
        input_grad,
        *column_out,
        *row_out,
        *small_out[8:],
        *small_out[:8],
    )


def solution(mesh):
    tokens, copied = P("dp", None), P()
    columns, rows, biases = P(None, "dp", None, "mp"), P(None, None, "mp", "dp"), P(None, None, "mp")
    placed = (
        tokens,
        copied,
        tokens,
        P("dp", None, None),
        P(None, "dp"),
        P("dp", "mp"),
        P("mp"),
        P("mp", "dp"),
        copied,
        P("dp", "mp"),
        P("dp", "mp"),
        *[columns] * 4,
        *[rows] * 4,
        *[biases] * 4,
        *[copied] * 8,
    )
    return jax.shard_map(
        local,
        mesh=mesh,
        in_specs=placed,
        out_specs=(
            copied,
            copied,
            tokens,
            *[columns] * 4,
            *[rows] * 4,
            *[biases] * 4,
            *[copied] * 8,
        ),
        check_vma=False,
    )
```
